128 devices in a mesh: dp: 8 (over z_lo, x), seq: 16 (over z_hi, y, core).
Axes of the slice: x: 4, y: 4, z: 4 (z_hi: 2, z_lo: 2; z = z_hi * 2 + z_lo), core: 2. Of those that a mesh axis runs over, the one named last changes fastest.
Arguments:
- series: bfloat16 [8, 8192, 128], P('dp', 'seq'), may hold values from -6 to 6
- cotangent: bfloat16 [8, 8192, 128], P('dp', 'seq'), may hold values from -6 to 6
- w_in: bfloat16 [128, 384], replicated, may hold values from -0.5 to 0.5
- w_out: bfloat16 [128, 128], replicated, may hold values from -0.5 to 0.5
- taps: float32 [3, 384], replicated, may hold values from -3 to 3
- skip_one: float32 [128], replicated, may hold values from 0.5 to 1.5
- skip_two: float32 [128], replicated, may hold values from 0.5 to 1.5
- filter_one: float32 [8, 8192], P(None, 'seq'), may hold values from -0.0625 to 0.0625
- filter_two: float32 [8, 8192], P(None, 'seq'), may hold values from -0.0625 to 0.0625
Outputs:
- output: bfloat16 [8, 8192, 128], P('dp', 'seq')
- d_series: bfloat16 [8, 8192, 128], P('dp', 'seq')
- grad_w_in: float32 [128, 384], replicated
- grad_w_out: float32 [128, 128], replicated
- grad_taps: float32 [3, 384], replicated
- grad_skip_one: float32 [128], replicated
- grad_skip_two: float32 [128], replicated
- grad_filter_one: float32 [8, 8192], P(None, 'seq')
- grad_filter_two: float32 [8, 8192], P(None, 'seq')
The draws below stay inside these ranges and needn't reach their ends.
All inputs are finite; a program needn't handle non-finite values.
Results may differ from the reference program's by a relative error of at most 0.015.
Values may be sent and summed in bfloat16 or wider, within the bound.
A program may use at most 128 MiB of HBM per device.

```python
import jax
import jax.numpy as jnp
from jax import lax

D = 128
FILTERS = 8
L = 8192
SERIES = 8


def level_of(stream_key, extent, pieces, smallest, largest):
    def one(dim, shards_of):
        draws = jax.random.uniform(jax.random.fold_in(jax.random.fold_in(stream_key, 6), dim), (shards_of,), jnp.float32, smallest / len(pieces), largest / len(pieces))
        return jnp.repeat(jnp.exp(draws), extent[dim] // shards_of).reshape((-1,) + (1,) * (len(extent) - dim - 1))

    gain = one(*pieces[0])
    for cut in pieces[1:]:
        gain = gain * one(*cut)
    return gain


def bell_draw(rng, shape, spread, bound, cuts=(), held_as=jnp.bfloat16):
    values = spread * jax.random.normal(rng, shape, jnp.float32)
    if cuts:
        values = values * level_of(rng, shape, cuts, -0.22, 0.18)
    return jnp.clip(values, -bound, bound).astype(held_as)


def setup_inputs(seed: int = 0) -> dict:
    seeds = jax.random.split(jax.random.key(seed), 10)
    return {
        "series": bell_draw(seeds[0], (SERIES, L, D), 1.0, 6.0, ((0, 8), (1, 16))),
        "cotangent": bell_draw(seeds[1], (SERIES, L, D), 1.0, 6.0, ((0, 8), (1, 16))),
        "w_in": bell_draw(seeds[2], (D, 3 * D), D ** -0.5, 0.5),
        "w_out": bell_draw(seeds[3], (D, D), D ** -0.5, 0.5),
        "taps": bell_draw(seeds[4], (3, 3 * D), 0.6, 3.0, (), jnp.float32),
        "skip_one": jnp.clip(jax.random.uniform(seeds[5], (D,), jnp.float32, 0.5, 1.5), 0.5, 1.5),
        "skip_two": jnp.clip(jax.random.uniform(seeds[6], (D,), jnp.float32, 0.5, 1.5), 0.5, 1.5),
        "filter_one": bell_draw(seeds[7], (FILTERS, L), L ** -0.5, 0.0625, ((1, 16),), jnp.float32),
        "filter_two": bell_draw(seeds[8], (FILTERS, L), L ** -0.5, 0.0625, ((1, 16),), jnp.float32),
    }


def filter_spectrum(filter_rows, channels, length):
    spectral = jnp.fft.rfft(filter_rows, n=2 * length, axis=1)
    return jnp.repeat(spectral.T, channels // filter_rows.shape[0], axis=1)[None]

def causal_conv(filter_rows, field, length):
    spectral = jnp.fft.rfft(field, n=2 * length, axis=1) * filter_spectrum(filter_rows, field.shape[2], length)
    return jnp.fft.irfft(spectral, n=2 * length, axis=1)[:, :length]

def anticausal_conv(filter_rows, field, length):
    spectral = jnp.fft.rfft(field, n=2 * length, axis=1) * jnp.conj(filter_spectrum(filter_rows, field.shape[2], length))
    return jnp.fft.irfft(spectral, n=2 * length, axis=1)[:, :length]

def filter_gradient(grad_field, field, filters, length):
    spectral = jnp.fft.rfft(grad_field, n=2 * length, axis=1) * jnp.conj(jnp.fft.rfft(field, n=2 * length, axis=1))
    series_count, bins, channels = spectral.shape
    spectral = lax.optimization_barrier(jnp.sum(spectral.reshape(series_count, bins, filters, channels // filters), axis=(0, 3)))
    return jnp.fft.irfft(spectral, n=2 * length, axis=0)[:length].T

def reference(series, cotangent, w_in, w_out, taps, skip_one, skip_two, filter_one, filter_two):
    highest = lax.Precision.HIGHEST
    width_d = series.shape[2]
    filters = filter_one.shape[0]
    series_wide = series.astype(jnp.float32)
    cot_wide = cotangent.astype(jnp.float32)
    projected = jnp.einsum('etd,dc->etc', series_wide, w_in.astype(jnp.float32), precision=highest)
    padded = jnp.pad(projected, ((0, 0), (2, 0), (0, 0)))
    convolved = taps[0] * padded[:, 2:] + taps[1] * padded[:, 1:-1] + taps[2] * padded[:, :-2]
    value_part = convolved[..., :width_d]
    gate_one = convolved[..., width_d:2 * width_d]
    gate_two = convolved[..., 2 * width_d:]
    y_one = causal_conv(filter_one, value_part, L) + skip_one * value_part
    gated_mid = gate_one * y_one
    y_two = causal_conv(filter_two, gated_mid, L) + skip_two * gated_mid
    product = (gate_two * y_two).astype(jnp.bfloat16)
    output = jnp.einsum('etc,cd->etd', product.astype(jnp.float32), w_out.astype(jnp.float32), precision=highest).astype(jnp.bfloat16)
    d_product = jnp.einsum('etd,cd->etc', cot_wide, w_out.astype(jnp.float32), precision=highest)
    grad_two = d_product * gate_two
    d_gate_two = d_product * y_two
    d_mid = anticausal_conv(filter_two, grad_two, L) + skip_two * grad_two
    grad_one = d_mid * gate_one
    d_gate_one = d_mid * y_one
    d_value = anticausal_conv(filter_one, grad_one, L) + skip_one * grad_one
    d_convolved = jnp.concatenate([d_value, d_gate_one, d_gate_two], axis=2)
    padded_back = jnp.pad(d_convolved, ((0, 0), (0, 2), (0, 0)))
    d_projected = (taps[0] * padded_back[:, :-2] + taps[1] * padded_back[:, 1:-1] + taps[2] * padded_back[:, 2:]).astype(jnp.bfloat16)
    d_series = jnp.einsum('etc,dc->etd', d_projected.astype(jnp.float32), w_in.astype(jnp.float32), precision=highest).astype(jnp.bfloat16)
    grad_scale = 1.0 / jnp.sqrt(jnp.float32(SERIES * L))
    grad_w_in = grad_scale * jnp.einsum('etd,etc->dc', series_wide, d_projected.astype(jnp.float32), precision=highest)
    grad_w_out = grad_scale * jnp.einsum('etc,etd->cd', product.astype(jnp.float32), cot_wide, precision=highest)
    grad_taps = grad_scale * jnp.stack([lax.optimization_barrier(jnp.sum(d_convolved * padded[:, 2 - offset:2 - offset + L], axis=(0, 1))) for offset in range(3)])
    grad_skip_one = grad_scale * lax.optimization_barrier(jnp.sum(grad_one * value_part, axis=(0, 1)))
    grad_skip_two = grad_scale * lax.optimization_barrier(jnp.sum(grad_two * gated_mid, axis=(0, 1)))
    grad_filter_one = grad_scale * filter_gradient(grad_one, value_part, filters, L)
    grad_filter_two = grad_scale * filter_gradient(grad_two, gated_mid, filters, L)
    return (output, d_series, grad_w_in, grad_w_out, grad_taps, grad_skip_one, grad_skip_two, grad_filter_one, grad_filter_two)
```

```python
import math

import numpy as np

import jax
import jax.numpy as jnp
from jax import lax
from jax.sharding import PartitionSpec as P

HIGHEST = lax.Precision.HIGHEST
LANES = 128


def dft_tables(length):
    size = 2 * length
    rows = size // LANES
    half = length // LANES
    k1 = np.arange(rows)
    f1 = np.exp(-2j * np.pi * (np.outer(k1, np.arange(half)) % rows) / rows)
    turn = np.exp(-2j * np.pi * np.outer(k1, np.arange(LANES)) / size)
    f2 = np.exp(-2j * np.pi * (np.outer(np.arange(LANES), np.arange(LANES)) % LANES) / LANES)
    fwd1 = np.concatenate([f1.real, f1.imag], axis=0)
    fwd2 = np.block([[f2.real, f2.imag], [-f2.imag, f2.real]])
    inv2 = np.block([[f2.real, -f2.imag], [f2.imag, f2.real]])
    inv1 = np.concatenate([f1.real.T, f1.imag.T], axis=1) / size
    as32 = lambda a: jnp.asarray(np.asarray(a, np.float32))
    return {
        "rows": rows,
        "fwd1": as32(fwd1),
        "fwd2": as32(fwd2),
        "inv1": as32(inv1),
        "inv2": as32(inv2),
        "turn_r": as32(turn.real)[:, None, :],
        "turn_i": as32(turn.imag)[:, None, :],
    }


def spectrum(x, tab):
    rows = tab["rows"]
    a = jnp.einsum("kn,ncm->kcm", tab["fwd1"], x, precision=HIGHEST)
    ar, ai = a[:rows], a[rows:]
    tr, ti = tab["turn_r"], tab["turn_i"]
    cat = jnp.concatenate([ar * tr - ai * ti, ar * ti + ai * tr], axis=-1)
    return jnp.einsum("kcm,mj->kcj", cat, tab["fwd2"], precision=HIGHEST)


def signal(s, tab):
    b = jnp.einsum("kcj,jm->kcm", s, tab["inv2"], precision=HIGHEST)
    br, bi = b[..., :LANES], b[..., LANES:]
    tr, ti = tab["turn_r"], tab["turn_i"]
    stacked = jnp.concatenate([br * tr + bi * ti, bi * tr - br * ti], axis=0)
    return jnp.einsum("nk,kcm->ncm", tab["inv1"], stacked, precision=HIGHEST)


def cmul(a, b, conj=False):
    ar, ai = a[..., :LANES], a[..., LANES:]
    br, bi = b[..., :LANES], b[..., LANES:]
    if conj:
        bi = -bi
    return jnp.concatenate([ar * br - ai * bi, ar * bi + ai * br], axis=-1)


def fold(x):
    c, length = x.shape
    return jnp.swapaxes(x.reshape(c, length // LANES, LANES), 0, 1)


def unfold(x):
    half, c, lanes = x.shape
    return jnp.swapaxes(x, 0, 1).reshape(c, half * lanes)


def shards(series, cotangent, w_in, w_out, taps, skip_one, skip_two, filter_one, filter_two):
    _, block, width = series.shape
    seq_n = lax.axis_size("seq")
    dp_n = lax.axis_size("dp")
    length = block * seq_n
    half = length // LANES
    me = lax.axis_index("seq")
    per = width // seq_n
    filters = filter_one.shape[0]
    group_width = width // filters
    per_group = group_width // per
    group = me // per_group
    grad_scale = 1.0 / math.sqrt(dp_n * series.shape[0] * length)
    tab = dft_tables(length)

    series_full = lax.all_gather(series[0], "seq", axis=0, tiled=True)
    cot_full = lax.all_gather(cotangent[0], "seq", axis=0, tiled=True)
    filt = lax.all_gather(jnp.stack([filter_one, filter_two]), "seq", axis=2, tiled=True)
    h_rows = lax.dynamic_index_in_dim(filt, group, axis=1, keepdims=False)

    w_sel = lax.dynamic_index_in_dim(
        w_in.reshape(width, 3, seq_n, per), me, axis=2, keepdims=False
    ).reshape(width, 3 * per)
    taps_sel = lax.dynamic_index_in_dim(
        taps.reshape(3, 3, seq_n, per), me, axis=2, keepdims=False
    ).reshape(3, 3 * per)
    wout_sel = lax.dynamic_index_in_dim(
        w_out.reshape(seq_n, per, width), me, axis=0, keepdims=False
    )
    skip1 = lax.dynamic_index_in_dim(skip_one.reshape(seq_n, per), me, axis=0, keepdims=False)
    skip2 = lax.dynamic_index_in_dim(skip_two.reshape(seq_n, per), me, axis=0, keepdims=False)
    skip1 = skip1[None, :, None]
    skip2 = skip2[None, :, None]

    proj = jnp.einsum("td,dc->ct", series_full, w_sel, preferred_element_type=jnp.float32)
    prev1 = jnp.pad(proj, ((0, 0), (1, 0)))[:, :length]
    prev2 = jnp.pad(proj, ((0, 0), (2, 0)))[:, :length]
    conv = taps_sel[0][:, None] * proj + taps_sel[1][:, None] * prev1 + taps_sel[2][:, None] * prev2
    conv_f = fold(conv)
    value = conv_f[:, :per]
    gate_one = conv_f[:, per : 2 * per]
    gate_two = conv_f[:, 2 * per :]

    h_spec = spectrum(fold(h_rows), tab)
    h_one = h_spec[:, 0:1]
    h_two = h_spec[:, 1:2]

    v_spec = spectrum(value, tab)
    y_one = signal(cmul(v_spec, h_one), tab) + skip1 * value
    gated_mid = gate_one * y_one
    m_spec = spectrum(gated_mid, tab)
    y_two = signal(cmul(m_spec, h_two), tab) + skip2 * gated_mid
    product = (gate_two * y_two).astype(jnp.bfloat16)

    cot_folded = cot_full.reshape(half, LANES, width)
    d_product = jnp.einsum(
        "nmd,cd->ncm", cot_folded, wout_sel, preferred_element_type=jnp.float32
    )
    grad_two = d_product * gate_two
    d_gate_two = d_product * y_two
    g2_spec = spectrum(grad_two, tab)
    d_mid = signal(cmul(g2_spec, h_two, conj=True), tab) + skip2 * grad_two
    grad_one = d_mid * gate_one
    d_gate_one = d_mid * y_one
    g1_spec = spectrum(grad_one, tab)
    d_value = signal(cmul(g1_spec, h_one, conj=True), tab) + skip1 * grad_one

    corr = jnp.concatenate(
        [
            jnp.sum(cmul(g1_spec, v_spec, conj=True), axis=1, keepdims=True),
            jnp.sum(cmul(g2_spec, m_spec, conj=True), axis=1, keepdims=True),
        ],
        axis=1,
    )
    filt_grad = unfold(signal(corr, tab))

    d_conv = unfold(jnp.concatenate([d_value, d_gate_one, d_gate_two], axis=1))
    next1 = jnp.pad(d_conv, ((0, 0), (0, 1)))[:, 1:]
    next2 = jnp.pad(d_conv, ((0, 0), (0, 2)))[:, 2:]
    d_proj = (
        taps_sel[0][:, None] * d_conv + taps_sel[1][:, None] * next1 + taps_sel[2][:, None] * next2
    ).astype(jnp.bfloat16)

    local_taps = jnp.stack(
        [jnp.sum(d_conv * proj, axis=1), jnp.sum(d_conv * prev1, axis=1), jnp.sum(d_conv * prev2, axis=1)]
    )
    local_skip1 = jnp.sum(grad_one * value, axis=(0, 2))
    local_skip2 = jnp.sum(grad_two * gated_mid, axis=(0, 2))
    local_w_in = jnp.einsum("td,ct->dc", series_full, d_proj, preferred_element_type=jnp.float32)
    local_w_out = jnp.einsum(
        "ncm,nmd->cd", product, cot_folded, preferred_element_type=jnp.float32
    )

    prod_blocks = product.reshape(seq_n, half // seq_n, per, LANES)
    prod_blocks = lax.all_to_all(prod_blocks, "seq", 0, 0, tiled=True)
    output = jnp.einsum(
        "jnim,jid->nmd",
        prod_blocks,
        w_out.reshape(seq_n, per, width),
        preferred_element_type=jnp.float32,
    ).astype(jnp.bfloat16)
    output = output.reshape(1, block, width)

    dp_blocks = d_proj.reshape(3, per, seq_n, block)
    dp_blocks = lax.all_to_all(dp_blocks, "seq", 2, 2, tiled=True)
    d_series = jnp.einsum(
        "pijt,dpji->td",
        dp_blocks,
        w_in.reshape(width, 3, seq_n, per),
        preferred_element_type=jnp.float32,
    ).astype(jnp.bfloat16)
    d_series = d_series.reshape(1, block, width)

    fg_blocks = lax.all_to_all(filt_grad.reshape(2, seq_n, block), "seq", 1, 1, tiled=True)
    fg_blocks = jnp.sum(fg_blocks.reshape(2, filters, per_group, block), axis=2)

    flat = jnp.concatenate(
        [
            local_w_in.reshape(-1),
            local_w_out.reshape(-1),
            local_taps.reshape(-1),
            local_skip1,
            local_skip2,
        ]
    )
    flat, fg_blocks = lax.psum((flat, fg_blocks), "dp")
    gathered = lax.all_gather(flat, "seq", axis=0, tiled=False)
    sizes = [width * 3 * per, per * width, 3 * 3 * per, per, per]
    offsets = np.cumsum([0] + sizes)
    part = lambda i: gathered[:, offsets[i] : offsets[i + 1]]
    grad_w_in = jnp.transpose(part(0).reshape(seq_n, width, 3, per), (1, 2, 0, 3)).reshape(
        width, 3 * width
    )
    grad_w_out = part(1).reshape(width, width)
    grad_taps = jnp.transpose(part(2).reshape(seq_n, 3, 3, per), (1, 2, 0, 3)).reshape(3, 3 * width)
    grad_skip_one = part(3).reshape(width)
    grad_skip_two = part(4).reshape(width)

    return (
        output,
        d_series,
        grad_scale * grad_w_in,
        grad_scale * grad_w_out,
        grad_scale * grad_taps,
        grad_scale * grad_skip_one,
        grad_scale * grad_skip_two,
        grad_scale * fg_blocks[0],
        grad_scale * fg_blocks[1],
    )


def solution(mesh):
    in_specs = (
        P("dp", "seq", None),
        P("dp", "seq", None),
        P(),
        P(),
        P(),
        P(),
        P(),
        P(None, "seq"),
        P(None, "seq"),
    )
    out_specs = (
        P("dp", "seq", None),
        P("dp", "seq", None),
        P(),
        P(),
        P(),
        P(),
        P(),
        P(None, "seq"),
        P(None, "seq"),
    )
    return jax.shard_map(shards, mesh=mesh, in_specs=in_specs, out_specs=out_specs, check_vma=False)
```

```python
import math

import numpy as np

import jax
import jax.numpy as jnp
from jax import lax
from jax.sharding import PartitionSpec as P

HIGHEST = lax.Precision.HIGHEST
LANES = 128


def dft_tables(length):
    size = 2 * length
    rows = size // LANES
    half = length // LANES
    k1 = np.arange(rows)
    f1 = np.exp(-2j * np.pi * (np.outer(k1, np.arange(half)) % rows) / rows)
    turn = np.exp(-2j * np.pi * np.outer(k1, np.arange(LANES)) / size)
    f2 = np.exp(-2j * np.pi * (np.outer(np.arange(LANES), np.arange(LANES)) % LANES) / LANES)
    fwd1 = np.concatenate([f1.real, f1.imag], axis=0)
    fwd2 = np.block([[f2.real, f2.imag], [-f2.imag, f2.real]])
    inv2 = np.block([[f2.real, -f2.imag], [f2.imag, f2.real]])
    inv1 = np.concatenate([f1.real.T, f1.imag.T], axis=1) / size
    as32 = lambda a: jnp.asarray(np.asarray(a, np.float32))
    return {
        "rows": rows,
        "fwd1": as32(fwd1),
        "fwd2": as32(fwd2),
        "inv1": as32(inv1),
        "inv2": as32(inv2),
        "turn_r": as32(turn.real)[:, None, :],
        "turn_i": as32(turn.imag)[:, None, :],
    }


def spectrum(x, tab):
    rows = tab["rows"]
    a = jnp.einsum("kn,ncm->kcm", tab["fwd1"], x, precision=HIGHEST)
    ar, ai = a[:rows], a[rows:]
    tr, ti = tab["turn_r"], tab["turn_i"]
    cat = jnp.concatenate([ar * tr - ai * ti, ar * ti + ai * tr], axis=-1)
    return jnp.einsum("kcm,mj->kcj", cat, tab["fwd2"], precision=HIGHEST)


def signal(s, tab):
    b = jnp.einsum("kcj,jm->kcm", s, tab["inv2"], precision=HIGHEST)
    br, bi = b[..., :LANES], b[..., LANES:]
    tr, ti = tab["turn_r"], tab["turn_i"]
    stacked = jnp.concatenate([br * tr + bi * ti, bi * tr - br * ti], axis=0)
    return jnp.einsum("nk,kcm->ncm", tab["inv1"], stacked, precision=HIGHEST)


def cmul(a, b, conj=False):
    ar, ai = a[..., :LANES], a[..., LANES:]
    br, bi = b[..., :LANES], b[..., LANES:]
    if conj:
        bi = -bi
    return jnp.concatenate([ar * br - ai * bi, ar * bi + ai * br], axis=-1)


def fold(x):
    c, length = x.shape
    return jnp.swapaxes(x.reshape(c, length // LANES, LANES), 0, 1)


def unfold(x):
    half, c, lanes = x.shape
    return jnp.swapaxes(x, 0, 1).reshape(c, half * lanes)


def shards(series, cotangent, w_in, w_out, taps, skip_one, skip_two, filter_one, filter_two):
    _, block, width = series.shape
    seq_n = lax.axis_size("seq")
    dp_n = lax.axis_size("dp")
    length = block * seq_n
    half = length // LANES
    me = lax.axis_index("seq")
    per = width // seq_n
    filters = filter_one.shape[0]
    group_width = width // filters
    per_group = group_width // per
    group = me // per_group
    grad_scale = 1.0 / math.sqrt(dp_n * series.shape[0] * length)
    tab = dft_tables(length)

    rows_sent = jnp.repeat(jnp.swapaxes(jnp.stack([filter_one, filter_two]), 0, 1), per_group, axis=0)
    rows_got = lax.all_to_all(rows_sent, "seq", 0, 0, tiled=True)
    h_rows = jnp.swapaxes(rows_got, 0, 1).reshape(2, length)

    taps_sel = lax.dynamic_index_in_dim(
        taps.reshape(3, 3, seq_n, per), me, axis=2, keepdims=False
    ).reshape(3, 3 * per)
    skip1 = lax.dynamic_index_in_dim(skip_one.reshape(seq_n, per), me, axis=0, keepdims=False)
    skip2 = lax.dynamic_index_in_dim(skip_two.reshape(seq_n, per), me, axis=0, keepdims=False)
    skip1 = skip1[None, :, None]
    skip2 = skip2[None, :, None]

    proj_blk = jnp.einsum("td,dc->ct", series[0], w_in, preferred_element_type=jnp.float32)
    proj_blk = lax.all_to_all(proj_blk.reshape(3, seq_n, per, block), "seq", 1, 1, tiled=True)
    proj = jnp.swapaxes(proj_blk, 1, 2).reshape(3 * per, length)
    prev1 = jnp.pad(proj, ((0, 0), (1, 0)))[:, :length]
    prev2 = jnp.pad(proj, ((0, 0), (2, 0)))[:, :length]
    conv = taps_sel[0][:, None] * proj + taps_sel[1][:, None] * prev1 + taps_sel[2][:, None] * prev2
    conv_f = fold(conv)
    value = conv_f[:, :per]
    gate_one = conv_f[:, per : 2 * per]
    gate_two = conv_f[:, 2 * per :]

    h_spec = spectrum(fold(h_rows), tab)
    h_one = h_spec[:, 0:1]
    h_two = h_spec[:, 1:2]

    v_spec = spectrum(value, tab)
    y_one = signal(cmul(v_spec, h_one), tab) + skip1 * value
    gated_mid = gate_one * y_one
    m_spec = spectrum(gated_mid, tab)
    y_two = signal(cmul(m_spec, h_two), tab) + skip2 * gated_mid
    product = (gate_two * y_two).astype(jnp.bfloat16)

    dprod_blk = jnp.einsum("td,cd->ct", cotangent[0], w_out, preferred_element_type=jnp.float32)
    dprod_blk = lax.all_to_all(dprod_blk.reshape(seq_n, per, block), "seq", 0, 0, tiled=True)
    d_product = jnp.swapaxes(
        dprod_blk.reshape(seq_n, per, block // LANES, LANES), 1, 2
    ).reshape(half, per, LANES)
    grad_two = d_product * gate_two
    d_gate_two = d_product * y_two
    g2_spec = spectrum(grad_two, tab)
    d_mid = signal(cmul(g2_spec, h_two, conj=True), tab) + skip2 * grad_two
    grad_one = d_mid * gate_one
    d_gate_one = d_mid * y_one
    g1_spec = spectrum(grad_one, tab)
    d_value = signal(cmul(g1_spec, h_one, conj=True), tab) + skip1 * grad_one

    corr = jnp.concatenate(
        [
            jnp.sum(cmul(g1_spec, v_spec, conj=True), axis=1, keepdims=True),
            jnp.sum(cmul(g2_spec, m_spec, conj=True), axis=1, keepdims=True),
        ],
        axis=1,
    )
    filt_grad = unfold(signal(corr, tab))

    d_conv = unfold(jnp.concatenate([d_value, d_gate_one, d_gate_two], axis=1))
    next1 = jnp.pad(d_conv, ((0, 0), (0, 1)))[:, 1:]
    next2 = jnp.pad(d_conv, ((0, 0), (0, 2)))[:, 2:]
    d_proj = (
        taps_sel[0][:, None] * d_conv + taps_sel[1][:, None] * next1 + taps_sel[2][:, None] * next2
    ).astype(jnp.bfloat16)

    local_taps = jnp.stack(
        [jnp.sum(d_conv * proj, axis=1), jnp.sum(d_conv * prev1, axis=1), jnp.sum(d_conv * prev2, axis=1)]
    )
    local_skip1 = jnp.sum(grad_one * value, axis=(0, 2))
    local_skip2 = jnp.sum(grad_two * gated_mid, axis=(0, 2))
    prod_blocks = product.reshape(seq_n, half // seq_n, per, LANES)
    prod_blocks = lax.all_to_all(prod_blocks, "seq", 0, 0, tiled=True)
    output = jnp.einsum(
        "jnim,jid->nmd",
        prod_blocks,
        w_out.reshape(seq_n, per, width),
        preferred_element_type=jnp.float32,
    ).astype(jnp.bfloat16)
    output = output.reshape(1, block, width)

    dp_blocks = d_proj.reshape(3, per, seq_n, block)
    dp_blocks = lax.all_to_all(dp_blocks, "seq", 2, 2, tiled=True)
    d_series = jnp.einsum(
        "pijt,dpji->td",
        dp_blocks,
        w_in.reshape(width, 3, seq_n, per),
        preferred_element_type=jnp.float32,
    ).astype(jnp.bfloat16)
    d_series = d_series.reshape(1, block, width)

    fg_blocks = lax.all_to_all(filt_grad.reshape(2, seq_n, block), "seq", 1, 1, tiled=True)
    fg_blocks = jnp.sum(fg_blocks.reshape(2, filters, per_group, block), axis=2)

    prod_rows = jnp.transpose(prod_blocks, (1, 3, 0, 2)).reshape(block, width)
    dp_rows = jnp.transpose(dp_blocks, (3, 0, 2, 1)).reshape(block, 3 * width)
    local_w_in = jnp.einsum("td,tc->dc", series[0], dp_rows, preferred_element_type=jnp.float32)
    local_w_out = jnp.einsum("tc,td->cd", prod_rows, cotangent[0], preferred_element_type=jnp.float32)
    small = jnp.concatenate([local_taps.reshape(3, 3, 1, per), jnp.stack([local_skip1, local_skip2, jnp.zeros_like(local_skip1)]).reshape(3, 1, 1, per)], axis=1)
    small_full = jnp.zeros((3, 4, seq_n, per), jnp.float32)
    small_full = lax.dynamic_update_slice(small_full, small, (0, 0, me, 0))
    grad_w_in, grad_w_out, small_full = lax.psum((local_w_in, local_w_out, small_full), ("dp", "seq"))
    fg_blocks = lax.psum(fg_blocks, "dp")
    small_full = small_full.reshape(3, 4, width)
    grad_taps = small_full[:, :3].reshape(3, 3 * width)
    grad_skip_one = small_full[0, 3]
    grad_skip_two = small_full[1, 3]

    return (
        output,
        d_series,
        grad_scale * grad_w_in,
        grad_scale * grad_w_out,
        grad_scale * grad_taps,
        grad_scale * grad_skip_one,
        grad_scale * grad_skip_two,
        grad_scale * fg_blocks[0],
        grad_scale * fg_blocks[1],
    )


def solution(mesh):
    in_specs = (
        P("dp", "seq", None),
        P("dp", "seq", None),
        P(),
        P(),
        P(),
        P(),
        P(),
        P(None, "seq"),
        P(None, "seq"),
    )
    out_specs = (
        P("dp", "seq", None),
        P("dp", "seq", None),
        P(),
        P(),
        P(),
        P(),
        P(),
        P(None, "seq"),
        P(None, "seq"),
    )
    return jax.shard_map(shards, mesh=mesh, in_specs=in_specs, out_specs=out_specs, check_vma=False)
```

```python
import math

import numpy as np

import jax
import jax.numpy as jnp
from jax import lax
from jax.sharding import PartitionSpec as P

HIGHEST = lax.Precision.HIGHEST
LANES = 128


def dft_tables(length):
    size = 2 * length
    rows = size // LANES
    half = length // LANES
    k1 = np.arange(rows)
    f1 = np.exp(-2j * np.pi * (np.outer(k1, np.arange(half)) % rows) / rows)
    turn = np.exp(-2j * np.pi * np.outer(k1, np.arange(LANES)) / size)
    f2 = np.exp(-2j * np.pi * (np.outer(np.arange(LANES), np.arange(LANES)) % LANES) / LANES)
    fwd1 = np.concatenate([f1.real, f1.imag], axis=0)
    fwd2 = np.block([[f2.real, f2.imag], [-f2.imag, f2.real]])
    inv2 = np.block([[f2.real, -f2.imag], [f2.imag, f2.real]])
    inv1 = np.concatenate([f1.real.T, f1.imag.T], axis=1) / size
    as32 = lambda a: jnp.asarray(np.asarray(a, np.float32))
    return {
        "rows": rows,
        "fwd1": as32(fwd1),
        "fwd2": as32(fwd2),
        "inv1": as32(inv1),
        "inv2": as32(inv2),
        "turn_r": as32(turn.real)[:, None, :],
        "turn_i": as32(turn.imag)[:, None, :],
    }


def spectrum(x, tab):
    rows = tab["rows"]
    a = jnp.einsum("kn,ncm->kcm", tab["fwd1"], x, precision=HIGHEST)
    ar, ai = a[:rows], a[rows:]
    tr, ti = tab["turn_r"], tab["turn_i"]
    cat = jnp.concatenate([ar * tr - ai * ti, ar * ti + ai * tr], axis=-1)
    return jnp.einsum("kcm,mj->kcj", cat, tab["fwd2"], precision=HIGHEST)


def signal(s, tab):
    b = jnp.einsum("kcj,jm->kcm", s, tab["inv2"], precision=HIGHEST)
    br, bi = b[..., :LANES], b[..., LANES:]
    tr, ti = tab["turn_r"], tab["turn_i"]
    stacked = jnp.concatenate([br * tr + bi * ti, bi * tr - br * ti], axis=0)
    return jnp.einsum("nk,kcm->ncm", tab["inv1"], stacked, precision=HIGHEST)


def cmul(a, b, conj=False):
    ar, ai = a[..., :LANES], a[..., LANES:]
    br, bi = b[..., :LANES], b[..., LANES:]
    if conj:
        bi = -bi
    return jnp.concatenate([ar * br - ai * bi, ar * bi + ai * br], axis=-1)


def fold(x):
    c, length = x.shape
    return jnp.swapaxes(x.reshape(c, length // LANES, LANES), 0, 1)


def unfold(x):
    half, c, lanes = x.shape
    return jnp.swapaxes(x, 0, 1).reshape(c, half * lanes)


def shards(series, cotangent, w_in, w_out, taps, skip_one, skip_two, filter_one, filter_two):
    _, block, width = series.shape
    seq_n = lax.axis_size("seq")
    dp_n = lax.axis_size("dp")
    length = block * seq_n
    half = length // LANES
    me = lax.axis_index("seq")
    per = width // seq_n
    filters = filter_one.shape[0]
    group_width = width // filters
    per_group = group_width // per
    group = me // per_group
    grad_scale = 1.0 / math.sqrt(dp_n * series.shape[0] * length)
    tab = dft_tables(length)

    taps_sel = lax.dynamic_index_in_dim(
        taps.reshape(3, 3, seq_n, per), me, axis=2, keepdims=False
    ).reshape(3, 3 * per)
    skip1 = lax.dynamic_index_in_dim(skip_one.reshape(seq_n, per), me, axis=0, keepdims=False)
    skip2 = lax.dynamic_index_in_dim(skip_two.reshape(seq_n, per), me, axis=0, keepdims=False)
    skip1 = skip1[None, :, None]
    skip2 = skip2[None, :, None]

    proj_blk = jnp.einsum("td,dc->ct", series[0], w_in, preferred_element_type=jnp.float32)
    proj_blk = jnp.swapaxes(proj_blk.reshape(3, seq_n, per, block), 0, 1).reshape(seq_n, 3 * per, block)
    dprod_blk = jnp.einsum("td,cd->ct", cotangent[0], w_out, preferred_element_type=jnp.float32)
    dprod_blk = dprod_blk.reshape(seq_n, per, block)
    rows_sent = jnp.repeat(jnp.swapaxes(jnp.stack([filter_one, filter_two]), 0, 1), per_group, axis=0)
    got = lax.all_to_all(
        jnp.concatenate([proj_blk, dprod_blk, rows_sent], axis=1), "seq", 0, 0, tiled=True
    )
    proj = jnp.swapaxes(got[:, : 3 * per], 0, 1).reshape(3 * per, length)
    d_product = jnp.swapaxes(
        got[:, 3 * per : 4 * per].reshape(seq_n, per, block // LANES, LANES), 1, 2
    ).reshape(half, per, LANES)
    h_rows = jnp.swapaxes(got[:, 4 * per :], 0, 1).reshape(2, length)
    prev1 = jnp.pad(proj, ((0, 0), (1, 0)))[:, :length]
    prev2 = jnp.pad(proj, ((0, 0), (2, 0)))[:, :length]
    conv = taps_sel[0][:, None] * proj + taps_sel[1][:, None] * prev1 + taps_sel[2][:, None] * prev2
    conv_f = fold(conv)
    value = conv_f[:, :per]
    gate_one = conv_f[:, per : 2 * per]
    gate_two = conv_f[:, 2 * per :]

    h_spec = spectrum(fold(h_rows), tab)
    h_one = h_spec[:, 0:1]
    h_two = h_spec[:, 1:2]

    v_spec = spectrum(value, tab)
    y_one = signal(cmul(v_spec, h_one), tab) + skip1 * value
    gated_mid = gate_one * y_one
    m_spec = spectrum(gated_mid, tab)
    y_two = signal(cmul(m_spec, h_two), tab) + skip2 * gated_mid
    product = (gate_two * y_two).astype(jnp.bfloat16)

    grad_two = d_product * gate_two
    d_gate_two = d_product * y_two
    g2_spec = spectrum(grad_two, tab)
    d_mid = signal(cmul(g2_spec, h_two, conj=True), tab) + skip2 * grad_two
    grad_one = d_mid * gate_one
    d_gate_one = d_mid * y_one
    g1_spec = spectrum(grad_one, tab)
    d_value = signal(cmul(g1_spec, h_one, conj=True), tab) + skip1 * grad_one

    corr = jnp.concatenate(
        [
            jnp.sum(cmul(g1_spec, v_spec, conj=True), axis=1, keepdims=True),
            jnp.sum(cmul(g2_spec, m_spec, conj=True), axis=1, keepdims=True),
        ],
        axis=1,
    )
    filt_grad = unfold(signal(corr, tab))

    d_conv = unfold(jnp.concatenate([d_value, d_gate_one, d_gate_two], axis=1))
    next1 = jnp.pad(d_conv, ((0, 0), (0, 1)))[:, 1:]
    next2 = jnp.pad(d_conv, ((0, 0), (0, 2)))[:, 2:]
    d_proj = (
        taps_sel[0][:, None] * d_conv + taps_sel[1][:, None] * next1 + taps_sel[2][:, None] * next2
    ).astype(jnp.bfloat16)

    local_taps = jnp.stack(
        [jnp.sum(d_conv * proj, axis=1), jnp.sum(d_conv * prev1, axis=1), jnp.sum(d_conv * prev2, axis=1)]
    )
    local_skip1 = jnp.sum(grad_one * value, axis=(0, 2))
    local_skip2 = jnp.sum(grad_two * gated_mid, axis=(0, 2))
    prod_sent = jnp.swapaxes(product.reshape(seq_n, half // seq_n, per, LANES), 1, 2)
    prod_sent = prod_sent.reshape(seq_n, per, block)
    dp_sent = jnp.swapaxes(d_proj.reshape(3 * per, seq_n, block), 0, 1)
    back = lax.all_to_all(jnp.concatenate([prod_sent, dp_sent], axis=1), "seq", 0, 0, tiled=True)
    prod_rows = jnp.transpose(back[:, :per], (2, 0, 1)).reshape(block, width)
    dp_rows = jnp.transpose(back[:, per:].reshape(seq_n, 3, per, block), (3, 1, 0, 2))
    dp_rows = dp_rows.reshape(block, 3 * width)
    output = jnp.dot(prod_rows, w_out, preferred_element_type=jnp.float32).astype(jnp.bfloat16)
    output = output.reshape(1, block, width)
    d_series = jnp.einsum(
        "tc,dc->td", dp_rows, w_in, preferred_element_type=jnp.float32
    ).astype(jnp.bfloat16)
    d_series = d_series.reshape(1, block, width)

    local_w_in = jnp.einsum("td,tc->dc", series[0], dp_rows, preferred_element_type=jnp.float32)
    local_w_out = jnp.einsum("tc,td->cd", prod_rows, cotangent[0], preferred_element_type=jnp.float32)
    small = jnp.concatenate(
        [
            local_taps.reshape(3, 3, 1, per),
            jnp.stack([local_skip1, local_skip2, jnp.zeros_like(local_skip1)]).reshape(3, 1, 1, per),
        ],
        axis=1,
    )
    small_full = lax.dynamic_update_slice(
        jnp.zeros((3, 4, seq_n, per), jnp.float32), small, (0, 0, me, 0)
    )
    params = jnp.concatenate([local_w_in.reshape(-1), local_w_out.reshape(-1), small_full.reshape(-1)])
    n_params = params.shape[0]
    chunk = -(-n_params // (seq_n * dp_n))
    params = jnp.pad(params, (0, chunk * seq_n * dp_n - n_params)).reshape(seq_n, dp_n * chunk)

    fg_sent = jnp.swapaxes(filt_grad.reshape(2, seq_n, block), 0, 1).reshape(seq_n, 2 * block)
    got = lax.all_to_all(jnp.concatenate([params, fg_sent], axis=1), "seq", 0, 0, tiled=True)
    p_part = jnp.sum(got[:, : dp_n * chunk], axis=0).reshape(dp_n, chunk)
    f_part = jnp.sum(got[:, dp_n * chunk :].reshape(filters, per_group, 2 * block), axis=1)
    got = lax.all_to_all(jnp.concatenate([p_part, f_part], axis=1), "dp", 0, 0, tiled=True)
    mine = jnp.sum(got, axis=0)
    got = lax.all_to_all(jnp.broadcast_to(mine, (dp_n,) + mine.shape), "dp", 0, 0, tiled=True)
    fg_blocks = jnp.swapaxes(got[:, chunk:].reshape(filters, 2, block), 0, 1)
    p_seq = got[:, :chunk].reshape(1, dp_n * chunk)
    got = lax.all_to_all(jnp.broadcast_to(p_seq, (seq_n, dp_n * chunk)), "seq", 0, 0, tiled=True)
    full = got.reshape(-1)
    sizes = [width * 3 * width, width * width, 3 * 4 * width]
    offsets = np.cumsum([0] + sizes)
    grad_w_in = full[offsets[0] : offsets[1]].reshape(width, 3 * width)
    grad_w_out = full[offsets[1] : offsets[2]].reshape(width, width)
    small_full = full[offsets[2] : offsets[3]].reshape(3, 4, width)
    grad_taps = small_full[:, :3].reshape(3, 3 * width)
    grad_skip_one = small_full[0, 3]
    grad_skip_two = small_full[1, 3]

    return (
        output,
        d_series,
        grad_scale * grad_w_in,
        grad_scale * grad_w_out,
        grad_scale * grad_taps,
        grad_scale * grad_skip_one,
        grad_scale * grad_skip_two,
        grad_scale * fg_blocks[0],
        grad_scale * fg_blocks[1],
    )


def solution(mesh):
    in_specs = (
        P("dp", "seq", None),
        P("dp", "seq", None),
        P(),
        P(),
        P(),
        P(),
        P(),
        P(None, "seq"),
        P(None, "seq"),
    )
    out_specs = (
        P("dp", "seq", None),
        P("dp", "seq", None),
        P(),
        P(),
        P(),
        P(),
        P(),
        P(None, "seq"),
        P(None, "seq"),
    )
    return jax.shard_map(shards, mesh=mesh, in_specs=in_specs, out_specs=out_specs, check_vma=False)
```

```python
import math

import numpy as np

import jax
import jax.numpy as jnp
from jax import lax
from jax.sharding import PartitionSpec as P

HIGHEST = lax.Precision.HIGHEST
LANES = 128


def dft_tables(length):
    size = 2 * length
    rows = size // LANES
    half = length // LANES
    k1 = np.arange(rows)
    f1 = np.exp(-2j * np.pi * (np.outer(k1, np.arange(half)) % rows) / rows)
    turn = np.exp(-2j * np.pi * np.outer(k1, np.arange(LANES)) / size)
    f2 = np.exp(-2j * np.pi * (np.outer(np.arange(LANES), np.arange(LANES)) % LANES) / LANES)
    fwd1 = np.concatenate([f1.real, f1.imag], axis=0)
    fwd2 = np.block([[f2.real, f2.imag], [-f2.imag, f2.real]])
    inv2 = np.block([[f2.real, -f2.imag], [f2.imag, f2.real]])
    inv1 = np.concatenate([f1.real.T, f1.imag.T], axis=1) / size
    as32 = lambda a: jnp.asarray(np.asarray(a, np.float32))
    return {
        "rows": rows,
        "fwd1": as32(fwd1),
        "fwd2": as32(fwd2),
        "inv1": as32(inv1),
        "inv2": as32(inv2),
        "turn_r": as32(turn.real)[:, None, :],
        "turn_i": as32(turn.imag)[:, None, :],
    }


def spectrum(x, tab):
    rows = tab["rows"]
    a = jnp.einsum("kn,ncm->kcm", tab["fwd1"], x, precision=HIGHEST)
    ar, ai = a[:rows], a[rows:]
    tr, ti = tab["turn_r"], tab["turn_i"]
    cat = jnp.concatenate([ar * tr - ai * ti, ar * ti + ai * tr], axis=-1)
    return jnp.einsum("kcm,mj->kcj", cat, tab["fwd2"], precision=HIGHEST)


def signal(s, tab):
    b = jnp.einsum("kcj,jm->kcm", s, tab["inv2"], precision=HIGHEST)
    br, bi = b[..., :LANES], b[..., LANES:]
    tr, ti = tab["turn_r"], tab["turn_i"]
    stacked = jnp.concatenate([br * tr + bi * ti, bi * tr - br * ti], axis=0)
    return jnp.einsum("nk,kcm->ncm", tab["inv1"], stacked, precision=HIGHEST)


def cmul(a, b, conj=False):
    ar, ai = a[..., :LANES], a[..., LANES:]
    br, bi = b[..., :LANES], b[..., LANES:]
    if conj:
        bi = -bi
    return jnp.concatenate([ar * br - ai * bi, ar * bi + ai * br], axis=-1)


def fold(x):
    c, length = x.shape
    return jnp.swapaxes(x.reshape(c, length // LANES, LANES), 0, 1)


def unfold(x):
    half, c, lanes = x.shape
    return jnp.swapaxes(x, 0, 1).reshape(c, half * lanes)


def shards(series, cotangent, w_in, w_out, taps, skip_one, skip_two, filter_one, filter_two):
    _, block, width = series.shape
    seq_n = lax.axis_size("seq")
    dp_n = lax.axis_size("dp")
    length = block * seq_n
    half = length // LANES
    me = lax.axis_index("seq")
    per = width // seq_n
    filters = filter_one.shape[0]
    group_width = width // filters
    per_group = group_width // per
    group = me // per_group
    grad_scale = 1.0 / math.sqrt(dp_n * series.shape[0] * length)
    tab = dft_tables(length)

    taps_sel = lax.dynamic_index_in_dim(
        taps.reshape(3, 3, seq_n, per), me, axis=2, keepdims=False
    ).reshape(3, 3 * per)
    skip1 = lax.dynamic_index_in_dim(skip_one.reshape(seq_n, per), me, axis=0, keepdims=False)
    skip2 = lax.dynamic_index_in_dim(skip_two.reshape(seq_n, per), me, axis=0, keepdims=False)
    skip1 = skip1[None, :, None]
    skip2 = skip2[None, :, None]

    proj_blk = jnp.einsum("td,dc->ct", series[0], w_in, preferred_element_type=jnp.float32)
    proj_blk = jnp.swapaxes(proj_blk.reshape(3, seq_n, per, block), 0, 1).reshape(seq_n, 3 * per, block)
    dprod_blk = jnp.einsum("td,cd->ct", cotangent[0], w_out, preferred_element_type=jnp.float32)
    dprod_blk = dprod_blk.reshape(seq_n, per, block)
    rows_sent = jnp.repeat(jnp.swapaxes(jnp.stack([filter_one, filter_two]), 0, 1), per_group, axis=0)
    got = lax.all_to_all(
        jnp.concatenate([proj_blk, dprod_blk, rows_sent], axis=1), "seq", 0, 0, tiled=True
    )
    proj = jnp.swapaxes(got[:, : 3 * per], 0, 1).reshape(3 * per, length)
    d_product = jnp.swapaxes(
        got[:, 3 * per : 4 * per].reshape(seq_n, per, block // LANES, LANES), 1, 2
    ).reshape(half, per, LANES)
    h_rows = jnp.swapaxes(got[:, 4 * per :], 0, 1).reshape(2, length)
    prev1 = jnp.pad(proj, ((0, 0), (1, 0)))[:, :length]
    prev2 = jnp.pad(proj, ((0, 0), (2, 0)))[:, :length]
    conv = taps_sel[0][:, None] * proj + taps_sel[1][:, None] * prev1 + taps_sel[2][:, None] * prev2
    conv_f = fold(conv)
    value = conv_f[:, :per]
    gate_one = conv_f[:, per : 2 * per]
    gate_two = conv_f[:, 2 * per :]

    h_spec = spectrum(fold(h_rows), tab)
    h_one = h_spec[:, 0:1]
    h_two = h_spec[:, 1:2]

    v_spec = spectrum(value, tab)
    y_one = signal(cmul(v_spec, h_one), tab) + skip1 * value
    gated_mid = gate_one * y_one
    m_spec = spectrum(gated_mid, tab)
    y_two = signal(cmul(m_spec, h_two), tab) + skip2 * gated_mid
    product = (gate_two * y_two).astype(jnp.bfloat16)

    grad_two = d_product * gate_two
    d_gate_two = d_product * y_two
    g2_spec = spectrum(grad_two, tab)
    d_mid = signal(cmul(g2_spec, h_two, conj=True), tab) + skip2 * grad_two
    grad_one = d_mid * gate_one
    d_gate_one = d_mid * y_one
    g1_spec = spectrum(grad_one, tab)
    d_value = signal(cmul(g1_spec, h_one, conj=True), tab) + skip1 * grad_one

    corr = jnp.concatenate(
        [
            jnp.sum(cmul(g1_spec, v_spec, conj=True), axis=1, keepdims=True),
            jnp.sum(cmul(g2_spec, m_spec, conj=True), axis=1, keepdims=True),
        ],
        axis=1,
    )
    filt_grad = unfold(signal(corr, tab))

    d_conv = unfold(jnp.concatenate([d_value, d_gate_one, d_gate_two], axis=1))
    next1 = jnp.pad(d_conv, ((0, 0), (0, 1)))[:, 1:]
    next2 = jnp.pad(d_conv, ((0, 0), (0, 2)))[:, 2:]
    d_proj = (
        taps_sel[0][:, None] * d_conv + taps_sel[1][:, None] * next1 + taps_sel[2][:, None] * next2
    ).astype(jnp.bfloat16)

    local_taps = jnp.stack(
        [jnp.sum(d_conv * proj, axis=1), jnp.sum(d_conv * prev1, axis=1), jnp.sum(d_conv * prev2, axis=1)]
    )
    local_skip1 = jnp.sum(grad_one * value, axis=(0, 2))
    local_skip2 = jnp.sum(grad_two * gated_mid, axis=(0, 2))
    prod_sent = jnp.swapaxes(product.reshape(seq_n, half // seq_n, per, LANES), 1, 2)
    prod_sent = prod_sent.reshape(seq_n, per, block)
    dp_sent = jnp.swapaxes(d_proj.reshape(3 * per, seq_n, block), 0, 1)
    back = lax.all_to_all(jnp.concatenate([prod_sent, dp_sent], axis=1), "seq", 0, 0, tiled=True)
    prod_rows = jnp.transpose(back[:, :per], (2, 0, 1)).reshape(block, width)
    dp_rows = jnp.transpose(back[:, per:].reshape(seq_n, 3, per, block), (3, 1, 0, 2))
    dp_rows = dp_rows.reshape(block, 3 * width)
    output = jnp.dot(prod_rows, w_out, preferred_element_type=jnp.float32).astype(jnp.bfloat16)
    output = output.reshape(1, block, width)
    d_series = jnp.einsum(
        "tc,dc->td", dp_rows, w_in, preferred_element_type=jnp.float32
    ).astype(jnp.bfloat16)
    d_series = d_series.reshape(1, block, width)

    local_w_in = jnp.einsum("td,tc->dc", series[0], dp_rows, preferred_element_type=jnp.float32)
    local_w_out = jnp.einsum("tc,td->cd", prod_rows, cotangent[0], preferred_element_type=jnp.float32)
    small = jnp.concatenate(
        [
            local_taps.reshape(3, 3, 1, per),
            jnp.stack([local_skip1, local_skip2, jnp.zeros_like(local_skip1)]).reshape(3, 1, 1, per),
        ],
        axis=1,
    )
    small_full = lax.dynamic_update_slice(
        jnp.zeros((3, 4, seq_n, per), jnp.float32), small, (0, 0, me, 0)
    )
    params = jnp.concatenate([local_w_in.reshape(-1), local_w_out.reshape(-1), small_full.reshape(-1)])
    n_params = params.shape[0]
    chunk = -(-n_params // (seq_n * dp_n))
    params = jnp.pad(params, (0, chunk * seq_n * dp_n - n_params)).reshape(seq_n, dp_n * chunk)

    fg_sent = jnp.swapaxes(filt_grad.reshape(2, seq_n, block), 0, 1)
    got = lax.all_to_all(fg_sent, "seq", 0, 0, tiled=True)
    f_part = jnp.sum(got.reshape(filters, per_group, 2, block), axis=1)
    params = params.reshape(seq_n * dp_n, chunk)
    got = lax.all_to_all(params, ("dp", "seq"), 0, 0, tiled=True)
    p_mine = jnp.sum(got, axis=0, keepdims=True)
    got = lax.all_to_all(f_part, "dp", 0, 0, tiled=True)
    f_mine = jnp.sum(got, axis=0, keepdims=True)
    got = lax.all_to_all(jnp.broadcast_to(f_mine, (dp_n,) + f_mine.shape[1:]), "dp", 0, 0, tiled=True)
    fg_blocks = jnp.swapaxes(got, 0, 1)
    got = lax.all_to_all(
        jnp.broadcast_to(p_mine, (seq_n * dp_n, chunk)), ("dp", "seq"), 0, 0, tiled=True
    )
    full = got.reshape(-1)
    sizes = [width * 3 * width, width * width, 3 * 4 * width]
    offsets = np.cumsum([0] + sizes)
    grad_w_in = full[offsets[0] : offsets[1]].reshape(width, 3 * width)
    grad_w_out = full[offsets[1] : offsets[2]].reshape(width, width)
    small_full = full[offsets[2] : offsets[3]].reshape(3, 4, width)
    grad_taps = small_full[:, :3].reshape(3, 3 * width)
    grad_skip_one = small_full[0, 3]
    grad_skip_two = small_full[1, 3]

    return (
        output,
        d_series,
        grad_scale * grad_w_in,
        grad_scale * grad_w_out,
        grad_scale * grad_taps,
        grad_scale * grad_skip_one,
        grad_scale * grad_skip_two,
        grad_scale * fg_blocks[0],
        grad_scale * fg_blocks[1],
    )


def solution(mesh):
    in_specs = (
        P("dp", "seq", None),
        P("dp", "seq", None),
        P(),
        P(),
        P(),
        P(),
        P(),
        P(None, "seq"),
        P(None, "seq"),
    )
    out_specs = (
        P("dp", "seq", None),
        P("dp", "seq", None),
        P(),
        P(),
        P(),
        P(),
        P(),
        P(None, "seq"),
        P(None, "seq"),
    )
    return jax.shard_map(shards, mesh=mesh, in_specs=in_specs, out_specs=out_specs, check_vma=False)
```

```python
import math

import numpy as np

import jax
import jax.numpy as jnp
from jax import lax
from jax.sharding import PartitionSpec as P

PRECISION = lax.Precision.HIGH
LANES = 128


def dft_tables(length):
    size = 2 * length
    rows = size // LANES
    half = length // LANES
    k1 = np.arange(rows)
    f1 = np.exp(-2j * np.pi * (np.outer(k1, np.arange(half)) % rows) / rows)
    turn = np.exp(-2j * np.pi * np.outer(k1, np.arange(LANES)) / size)
    f2 = np.exp(-2j * np.pi * (np.outer(np.arange(LANES), np.arange(LANES)) % LANES) / LANES)
    fwd1 = np.concatenate([f1.real, f1.imag], axis=0)
    fwd2 = np.block([[f2.real, f2.imag], [-f2.imag, f2.real]])
    inv2 = np.block([[f2.real, -f2.imag], [f2.imag, f2.real]])
    inv1 = np.concatenate([f1.real.T, f1.imag.T], axis=1) / size
    as32 = lambda a: jnp.asarray(np.asarray(a, np.float32))
    return {
        "rows": rows,
        "fwd1": as32(fwd1),
        "fwd2": as32(fwd2),
        "inv1": as32(inv1),
        "inv2": as32(inv2),
        "turn_r": as32(turn.real)[:, None, :],
        "turn_i": as32(turn.imag)[:, None, :],
    }


def spectrum(x, tab):
    rows = tab["rows"]
    a = jnp.einsum("kn,ncm->kcm", tab["fwd1"], x, precision=PRECISION)
    ar, ai = a[:rows], a[rows:]
    tr, ti = tab["turn_r"], tab["turn_i"]
    cat = jnp.concatenate([ar * tr - ai * ti, ar * ti + ai * tr], axis=-1)
    return jnp.einsum("kcm,mj->kcj", cat, tab["fwd2"], precision=PRECISION)


def signal(s, tab):
    b = jnp.einsum("kcj,jm->kcm", s, tab["inv2"], precision=PRECISION)
    br, bi = b[..., :LANES], b[..., LANES:]
    tr, ti = tab["turn_r"], tab["turn_i"]
    stacked = jnp.concatenate([br * tr + bi * ti, bi * tr - br * ti], axis=0)
    return jnp.einsum("nk,kcm->ncm", tab["inv1"], stacked, precision=PRECISION)


def cmul(a, b, conj=False):
    ar, ai = a[..., :LANES], a[..., LANES:]
    br, bi = b[..., :LANES], b[..., LANES:]
    if conj:
        bi = -bi
    return jnp.concatenate([ar * br - ai * bi, ar * bi + ai * br], axis=-1)


def fold(x):
    c, length = x.shape
    return jnp.swapaxes(x.reshape(c, length // LANES, LANES), 0, 1)


def unfold(x):
    half, c, lanes = x.shape
    return jnp.swapaxes(x, 0, 1).reshape(c, half * lanes)


def shards(series, cotangent, w_in, w_out, taps, skip_one, skip_two, filter_one, filter_two):
    _, block, width = series.shape
    seq_n = lax.axis_size("seq")
    dp_n = lax.axis_size("dp")
    length = block * seq_n
    half = length // LANES
    me = lax.axis_index("seq")
    per = width // seq_n
    filters = filter_one.shape[0]
    group_width = width // filters
    per_group = group_width // per
    group = me // per_group
    grad_scale = 1.0 / math.sqrt(dp_n * series.shape[0] * length)
    tab = dft_tables(length)

    taps_sel = lax.dynamic_index_in_dim(
        taps.reshape(3, 3, seq_n, per), me, axis=2, keepdims=False
    ).reshape(3, 3 * per)
    skip1 = lax.dynamic_index_in_dim(skip_one.reshape(seq_n, per), me, axis=0, keepdims=False)
    skip2 = lax.dynamic_index_in_dim(skip_two.reshape(seq_n, per), me, axis=0, keepdims=False)
    skip1 = skip1[None, :, None]
    skip2 = skip2[None, :, None]

    proj_blk = jnp.einsum("td,dc->ct", series[0], w_in, preferred_element_type=jnp.float32)
    proj_blk = jnp.swapaxes(proj_blk.reshape(3, seq_n, per, block), 0, 1).reshape(seq_n, 3 * per, block)
    dprod_blk = jnp.einsum("td,cd->ct", cotangent[0], w_out, preferred_element_type=jnp.float32)
    dprod_blk = dprod_blk.reshape(seq_n, per, block)
    rows_sent = jnp.repeat(jnp.swapaxes(jnp.stack([filter_one, filter_two]), 0, 1), per_group, axis=0)
    got = lax.all_to_all(
        jnp.concatenate([proj_blk, dprod_blk, rows_sent], axis=1), "seq", 0, 0, tiled=True
    )
    proj = jnp.swapaxes(got[:, : 3 * per], 0, 1).reshape(3 * per, length)
    d_product = jnp.swapaxes(
        got[:, 3 * per : 4 * per].reshape(seq_n, per, block // LANES, LANES), 1, 2
    ).reshape(half, per, LANES)
    h_rows = jnp.swapaxes(got[:, 4 * per :], 0, 1).reshape(2, length)
    prev1 = jnp.pad(proj, ((0, 0), (1, 0)))[:, :length]
    prev2 = jnp.pad(proj, ((0, 0), (2, 0)))[:, :length]
    conv = taps_sel[0][:, None] * proj + taps_sel[1][:, None] * prev1 + taps_sel[2][:, None] * prev2
    conv_f = fold(conv)
    value = conv_f[:, :per]
    gate_one = conv_f[:, per : 2 * per]
    gate_two = conv_f[:, 2 * per :]

    h_spec = spectrum(fold(h_rows), tab)
    h_one = h_spec[:, 0:1]
    h_two = h_spec[:, 1:2]

    v_spec = spectrum(value, tab)
    y_one = signal(cmul(v_spec, h_one), tab) + skip1 * value
    gated_mid = gate_one * y_one
    m_spec = spectrum(gated_mid, tab)
    y_two = signal(cmul(m_spec, h_two), tab) + skip2 * gated_mid
    product = (gate_two * y_two).astype(jnp.bfloat16)

    grad_two = d_product * gate_two
    d_gate_two = d_product * y_two
    g2_spec = spectrum(grad_two, tab)
    d_mid = signal(cmul(g2_spec, h_two, conj=True), tab) + skip2 * grad_two
    grad_one = d_mid * gate_one
    d_gate_one = d_mid * y_one
    g1_spec = spectrum(grad_one, tab)
    d_value = signal(cmul(g1_spec, h_one, conj=True), tab) + skip1 * grad_one

    corr = jnp.concatenate(
        [
            jnp.sum(cmul(g1_spec, v_spec, conj=True), axis=1, keepdims=True),
            jnp.sum(cmul(g2_spec, m_spec, conj=True), axis=1, keepdims=True),
        ],
        axis=1,
    )
    filt_grad = unfold(signal(corr, tab))

    d_conv = unfold(jnp.concatenate([d_value, d_gate_one, d_gate_two], axis=1))
    next1 = jnp.pad(d_conv, ((0, 0), (0, 1)))[:, 1:]
    next2 = jnp.pad(d_conv, ((0, 0), (0, 2)))[:, 2:]
    d_proj = (
        taps_sel[0][:, None] * d_conv + taps_sel[1][:, None] * next1 + taps_sel[2][:, None] * next2
    ).astype(jnp.bfloat16)

    local_taps = jnp.stack(
        [jnp.sum(d_conv * proj, axis=1), jnp.sum(d_conv * prev1, axis=1), jnp.sum(d_conv * prev2, axis=1)]
    )
    local_skip1 = jnp.sum(grad_one * value, axis=(0, 2))
    local_skip2 = jnp.sum(grad_two * gated_mid, axis=(0, 2))
    prod_sent = jnp.swapaxes(product.reshape(seq_n, half // seq_n, per, LANES), 1, 2)
    prod_sent = prod_sent.reshape(seq_n, per, block)
    dp_sent = jnp.swapaxes(d_proj.reshape(3 * per, seq_n, block), 0, 1)
    back = lax.all_to_all(jnp.concatenate([prod_sent, dp_sent], axis=1), "seq", 0, 0, tiled=True)
    prod_rows = jnp.transpose(back[:, :per], (2, 0, 1)).reshape(block, width)
    dp_rows = jnp.transpose(back[:, per:].reshape(seq_n, 3, per, block), (3, 1, 0, 2))
    dp_rows = dp_rows.reshape(block, 3 * width)
    output = jnp.dot(prod_rows, w_out, preferred_element_type=jnp.float32).astype(jnp.bfloat16)
    output = output.reshape(1, block, width)
    d_series = jnp.einsum(
        "tc,dc->td", dp_rows, w_in, preferred_element_type=jnp.float32
    ).astype(jnp.bfloat16)
    d_series = d_series.reshape(1, block, width)

    local_w_in = jnp.einsum("td,tc->dc", series[0], dp_rows, preferred_element_type=jnp.float32)
    local_w_out = jnp.einsum("tc,td->cd", prod_rows, cotangent[0], preferred_element_type=jnp.float32)
    small = jnp.concatenate(
        [
            local_taps.reshape(3, 3, 1, per),
            jnp.stack([local_skip1, local_skip2, jnp.zeros_like(local_skip1)]).reshape(3, 1, 1, per),
        ],
        axis=1,
    )
    small_full = lax.dynamic_update_slice(
        jnp.zeros((3, 4, seq_n, per), jnp.float32), small, (0, 0, me, 0)
    )
    params = jnp.concatenate([local_w_in.reshape(-1), local_w_out.reshape(-1), small_full.reshape(-1)])
    n_params = params.shape[0]
    chunk = -(-n_params // (seq_n * dp_n))
    params = jnp.pad(params, (0, chunk * seq_n * dp_n - n_params)).reshape(seq_n, dp_n * chunk)

    fg_sent = jnp.swapaxes(filt_grad.reshape(2, seq_n, block), 0, 1).reshape(seq_n, 2 * block)
    got = lax.all_to_all(jnp.concatenate([params, fg_sent], axis=1), "seq", 0, 0, tiled=True)
    p_part = jnp.sum(got[:, : dp_n * chunk], axis=0).reshape(dp_n, chunk)
    f_part = jnp.sum(got[:, dp_n * chunk :].reshape(filters, per_group, 2 * block), axis=1)
    got = lax.all_to_all(jnp.concatenate([p_part, f_part], axis=1), "dp", 0, 0, tiled=True)
    mine = jnp.sum(got, axis=0)
    got = lax.all_to_all(jnp.broadcast_to(mine, (dp_n,) + mine.shape), "dp", 0, 0, tiled=True)
    fg_blocks = jnp.swapaxes(got[:, chunk:].reshape(filters, 2, block), 0, 1)
    p_seq = got[:, :chunk].reshape(1, dp_n * chunk)
    got = lax.all_to_all(jnp.broadcast_to(p_seq, (seq_n, dp_n * chunk)), "seq", 0, 0, tiled=True)
    full = got.reshape(-1)
    sizes = [width * 3 * width, width * width, 3 * 4 * width]
    offsets = np.cumsum([0] + sizes)
    grad_w_in = full[offsets[0] : offsets[1]].reshape(width, 3 * width)
    grad_w_out = full[offsets[1] : offsets[2]].reshape(width, width)
    small_full = full[offsets[2] : offsets[3]].reshape(3, 4, width)
    grad_taps = small_full[:, :3].reshape(3, 3 * width)
    grad_skip_one = small_full[0, 3]
    grad_skip_two = small_full[1, 3]

    return (
        output,
        d_series,
        grad_scale * grad_w_in,
        grad_scale * grad_w_out,
        grad_scale * grad_taps,
        grad_scale * grad_skip_one,
        grad_scale * grad_skip_two,
        grad_scale * fg_blocks[0],
        grad_scale * fg_blocks[1],
    )


def solution(mesh):
    in_specs = (
        P("dp", "seq", None),
        P("dp", "seq", None),
        P(),
        P(),
        P(),
        P(),
        P(),
        P(None, "seq"),
        P(None, "seq"),
    )
    out_specs = (
        P("dp", "seq", None),
        P("dp", "seq", None),
        P(),
        P(),
        P(),
        P(),
        P(),
        P(None, "seq"),
        P(None, "seq"),
    )
    return jax.shard_map(shards, mesh=mesh, in_specs=in_specs, out_specs=out_specs, check_vma=False)
```

```python
import math

import numpy as np

import jax
import jax.numpy as jnp
from jax import lax
from jax.experimental import pallas as pl
from jax.experimental.pallas import tpu as pltpu
from jax.sharding import PartitionSpec as P

PRECISION = lax.Precision.HIGH
LANES = 128


def dft_tables(length):
    size = 2 * length
    rows = size // LANES
    half = length // LANES
    k1 = np.arange(rows)
    f1 = np.exp(-2j * np.pi * (np.outer(k1, np.arange(half)) % rows) / rows)
    turn = np.exp(-2j * np.pi * np.outer(k1, np.arange(LANES)) / size)
    f2 = np.exp(-2j * np.pi * (np.outer(np.arange(LANES), np.arange(LANES)) % LANES) / LANES)
    fwd1 = np.concatenate([f1.real, f1.imag], axis=0)
    fwd2 = np.block([[f2.real, f2.imag], [-f2.imag, f2.real]])
    inv2 = np.block([[f2.real, -f2.imag], [f2.imag, f2.real]])
    inv1 = np.concatenate([f1.real.T, f1.imag.T], axis=1) / size
    as32 = lambda a: jnp.asarray(np.asarray(a, np.float32))
    return {
        "rows": rows,
        "fwd1": as32(fwd1),
        "fwd2": as32(fwd2),
        "inv1": as32(inv1),
        "inv2": as32(inv2),
        "turn_r": as32(turn.real)[:, None, :],
        "turn_i": as32(turn.imag)[:, None, :],
    }


def spectrum(x, tab):
    rows = tab["rows"]
    a = jnp.einsum("kn,ncm->kcm", tab["fwd1"], x, precision=PRECISION)
    ar, ai = a[:rows], a[rows:]
    tr, ti = tab["turn_r"], tab["turn_i"]
    cat = jnp.concatenate([ar * tr - ai * ti, ar * ti + ai * tr], axis=-1)
    return jnp.einsum("kcm,mj->kcj", cat, tab["fwd2"], precision=PRECISION)


def signal(s, tab):
    b = jnp.einsum("kcj,jm->kcm", s, tab["inv2"], precision=PRECISION)
    br, bi = b[..., :LANES], b[..., LANES:]
    tr, ti = tab["turn_r"], tab["turn_i"]
    stacked = jnp.concatenate([br * tr + bi * ti, bi * tr - br * ti], axis=0)
    return jnp.einsum("nk,kcm->ncm", tab["inv1"], stacked, precision=PRECISION)


def cmul(a, b, conj=False):
    ar, ai = a[..., :LANES], a[..., LANES:]
    br, bi = b[..., :LANES], b[..., LANES:]
    if conj:
        bi = -bi
    return jnp.concatenate([ar * br - ai * bi, ar * bi + ai * br], axis=-1)


def fold(x):
    c, length = x.shape
    return jnp.swapaxes(x.reshape(c, length // LANES, LANES), 0, 1)


def unfold(x):
    half, c, lanes = x.shape
    return jnp.swapaxes(x, 0, 1).reshape(c, half * lanes)


def exchange(x, axis, ident):
    n = x.shape[0]
    mesh_axes = ("dp", "seq")

    def where(p):
        return tuple(p if name == axis else lax.axis_index(name) for name in mesh_axes)

    def kernel(x_ref, y_ref, send_sem, recv_sem):
        me = lax.axis_index(axis)
        barrier = pltpu.get_barrier_semaphore()
        for k in range(1, n):
            pl.semaphore_signal(
                barrier, inc=1, device_id=where(lax.rem(me + k, n)),
                device_id_type=pl.DeviceIdType.MESH,
            )
        pl.semaphore_wait(barrier, n - 1)
        copies = []
        for k in range(1, n):
            p = lax.rem(me + k, n)
            copy = pltpu.make_async_remote_copy(
                src_ref=x_ref.at[p],
                dst_ref=y_ref.at[me],
                send_sem=send_sem.at[k],
                recv_sem=recv_sem.at[k],
                device_id=where(p),
                device_id_type=pl.DeviceIdType.MESH,
            )
            copy.start()
            copies.append(copy)
        y_ref[pl.ds(me, 1)] = x_ref[pl.ds(me, 1)]
        for copy in copies:
            copy.wait()

    return pl.pallas_call(
        kernel,
        out_shape=jax.ShapeDtypeStruct(x.shape, x.dtype),
        in_specs=[pl.BlockSpec(memory_space=pltpu.VMEM)],
        out_specs=pl.BlockSpec(memory_space=pltpu.VMEM),
        scratch_shapes=[pltpu.SemaphoreType.DMA((n,)), pltpu.SemaphoreType.DMA((n,))],
        compiler_params=pltpu.CompilerParams(collective_id=ident, has_side_effects=True),
    )(x)


def swap_blocks(x, axis, ident):
    shape = x.shape
    flat = x.reshape(shape[0], -1, LANES)
    return exchange(flat, axis, ident).reshape(shape)


def shards(series, cotangent, w_in, w_out, taps, skip_one, skip_two, filter_one, filter_two):
    _, block, width = series.shape
    seq_n = lax.axis_size("seq")
    dp_n = lax.axis_size("dp")
    length = block * seq_n
    half = length // LANES
    me = lax.axis_index("seq")
    per = width // seq_n
    filters = filter_one.shape[0]
    group_width = width // filters
    per_group = group_width // per
    group = me // per_group
    grad_scale = 1.0 / math.sqrt(dp_n * series.shape[0] * length)
    tab = dft_tables(length)

    taps_sel = lax.dynamic_index_in_dim(
        taps.reshape(3, 3, seq_n, per), me, axis=2, keepdims=False
    ).reshape(3, 3 * per)
    skip1 = lax.dynamic_index_in_dim(skip_one.reshape(seq_n, per), me, axis=0, keepdims=False)
    skip2 = lax.dynamic_index_in_dim(skip_two.reshape(seq_n, per), me, axis=0, keepdims=False)
    skip1 = skip1[None, :, None]
    skip2 = skip2[None, :, None]

    proj_blk = jnp.einsum("td,dc->ct", series[0], w_in, preferred_element_type=jnp.float32)
    proj_blk = jnp.swapaxes(proj_blk.reshape(3, seq_n, per, block), 0, 1).reshape(seq_n, 3 * per, block)
    dprod_blk = jnp.einsum("td,cd->ct", cotangent[0], w_out, preferred_element_type=jnp.float32)
    dprod_blk = dprod_blk.reshape(seq_n, per, block)
    rows_sent = jnp.repeat(jnp.swapaxes(jnp.stack([filter_one, filter_two]), 0, 1), per_group, axis=0)
    got = swap_blocks(jnp.concatenate([proj_blk, dprod_blk, rows_sent], axis=1), "seq", 0)
    proj = jnp.swapaxes(got[:, : 3 * per], 0, 1).reshape(3 * per, length)
    d_product = jnp.swapaxes(
        got[:, 3 * per : 4 * per].reshape(seq_n, per, block // LANES, LANES), 1, 2
    ).reshape(half, per, LANES)
    h_rows = jnp.swapaxes(got[:, 4 * per :], 0, 1).reshape(2, length)
    prev1 = jnp.pad(proj, ((0, 0), (1, 0)))[:, :length]
    prev2 = jnp.pad(proj, ((0, 0), (2, 0)))[:, :length]
    conv = taps_sel[0][:, None] * proj + taps_sel[1][:, None] * prev1 + taps_sel[2][:, None] * prev2
    conv_f = fold(conv)
    value = conv_f[:, :per]
    gate_one = conv_f[:, per : 2 * per]
    gate_two = conv_f[:, 2 * per :]

    h_spec = spectrum(fold(h_rows), tab)
    h_one = h_spec[:, 0:1]
    h_two = h_spec[:, 1:2]

    v_spec = spectrum(value, tab)
    y_one = signal(cmul(v_spec, h_one), tab) + skip1 * value
    gated_mid = gate_one * y_one
    m_spec = spectrum(gated_mid, tab)
    y_two = signal(cmul(m_spec, h_two), tab) + skip2 * gated_mid
    product = (gate_two * y_two).astype(jnp.bfloat16)

    grad_two = d_product * gate_two
    d_gate_two = d_product * y_two
    g2_spec = spectrum(grad_two, tab)
    d_mid = signal(cmul(g2_spec, h_two, conj=True), tab) + skip2 * grad_two
    grad_one = d_mid * gate_one
    d_gate_one = d_mid * y_one
    g1_spec = spectrum(grad_one, tab)
    d_value = signal(cmul(g1_spec, h_one, conj=True), tab) + skip1 * grad_one

    corr = jnp.concatenate(
        [
            jnp.sum(cmul(g1_spec, v_spec, conj=True), axis=1, keepdims=True),
            jnp.sum(cmul(g2_spec, m_spec, conj=True), axis=1, keepdims=True),
        ],
        axis=1,
    )
    filt_grad = unfold(signal(corr, tab))

    d_conv = unfold(jnp.concatenate([d_value, d_gate_one, d_gate_two], axis=1))
    next1 = jnp.pad(d_conv, ((0, 0), (0, 1)))[:, 1:]
    next2 = jnp.pad(d_conv, ((0, 0), (0, 2)))[:, 2:]
    d_proj = (
        taps_sel[0][:, None] * d_conv + taps_sel[1][:, None] * next1 + taps_sel[2][:, None] * next2
    ).astype(jnp.bfloat16)

    local_taps = jnp.stack(
        [jnp.sum(d_conv * proj, axis=1), jnp.sum(d_conv * prev1, axis=1), jnp.sum(d_conv * prev2, axis=1)]
    )
    local_skip1 = jnp.sum(grad_one * value, axis=(0, 2))
    local_skip2 = jnp.sum(grad_two * gated_mid, axis=(0, 2))
    prod_sent = jnp.swapaxes(product.reshape(seq_n, half // seq_n, per, LANES), 1, 2)
    prod_sent = prod_sent.reshape(seq_n, per, block)
    dp_sent = jnp.swapaxes(d_proj.reshape(3 * per, seq_n, block), 0, 1)
    back = swap_blocks(jnp.concatenate([prod_sent, dp_sent], axis=1), "seq", 1)
    prod_rows = jnp.transpose(back[:, :per], (2, 0, 1)).reshape(block, width)
    dp_rows = jnp.transpose(back[:, per:].reshape(seq_n, 3, per, block), (3, 1, 0, 2))
    dp_rows = dp_rows.reshape(block, 3 * width)
    output = jnp.dot(prod_rows, w_out, preferred_element_type=jnp.float32).astype(jnp.bfloat16)
    output = output.reshape(1, block, width)
    d_series = jnp.einsum(
        "tc,dc->td", dp_rows, w_in, preferred_element_type=jnp.float32
    ).astype(jnp.bfloat16)
    d_series = d_series.reshape(1, block, width)

    local_w_in = jnp.einsum("td,tc->dc", series[0], dp_rows, preferred_element_type=jnp.float32)
    local_w_out = jnp.einsum("tc,td->cd", prod_rows, cotangent[0], preferred_element_type=jnp.float32)
    small = jnp.concatenate(
        [
            local_taps.reshape(3, 3, 1, per),
            jnp.stack([local_skip1, local_skip2, jnp.zeros_like(local_skip1)]).reshape(3, 1, 1, per),
        ],
        axis=1,
    )
    small_full = lax.dynamic_update_slice(
        jnp.zeros((3, 4, seq_n, per), jnp.float32), small, (0, 0, me, 0)
    )
    params = jnp.concatenate([local_w_in.reshape(-1), local_w_out.reshape(-1), small_full.reshape(-1)])
    n_params = params.shape[0]
    chunk = -(-n_params // (seq_n * dp_n * 8 * LANES)) * 8 * LANES
    params = jnp.pad(params, (0, chunk * seq_n * dp_n - n_params)).reshape(seq_n, dp_n * chunk)

    fg_sent = jnp.swapaxes(filt_grad.reshape(2, seq_n, block), 0, 1).reshape(seq_n, 2 * block)
    got = swap_blocks(jnp.concatenate([params, fg_sent], axis=1), "seq", 2)
    p_part = jnp.sum(got[:, : dp_n * chunk], axis=0).reshape(dp_n, chunk)
    f_part = jnp.sum(got[:, dp_n * chunk :].reshape(filters, per_group, 2 * block), axis=1)
    got = swap_blocks(jnp.concatenate([p_part, f_part], axis=1), "dp", 3)
    mine = jnp.sum(got, axis=0)
    got = swap_blocks(jnp.broadcast_to(mine, (dp_n,) + mine.shape), "dp", 4)
    fg_blocks = jnp.swapaxes(got[:, chunk:].reshape(filters, 2, block), 0, 1)
    p_seq = got[:, :chunk].reshape(1, dp_n * chunk)
    got = swap_blocks(jnp.broadcast_to(p_seq, (seq_n, dp_n * chunk)), "seq", 5)
    full = got.reshape(-1)
    sizes = [width * 3 * width, width * width, 3 * 4 * width]
    offsets = np.cumsum([0] + sizes)
    grad_w_in = full[offsets[0] : offsets[1]].reshape(width, 3 * width)
    grad_w_out = full[offsets[1] : offsets[2]].reshape(width, width)
    small_full = full[offsets[2] : offsets[3]].reshape(3, 4, width)
    grad_taps = small_full[:, :3].reshape(3, 3 * width)
    grad_skip_one = small_full[0, 3]
    grad_skip_two = small_full[1, 3]

    return (
        output,
        d_series,
        grad_scale * grad_w_in,
        grad_scale * grad_w_out,
        grad_scale * grad_taps,
        grad_scale * grad_skip_one,
        grad_scale * grad_skip_two,
        grad_scale * fg_blocks[0],
        grad_scale * fg_blocks[1],
    )


def solution(mesh):
    in_specs = (
        P("dp", "seq", None),
        P("dp", "seq", None),
        P(),
        P(),
        P(),
        P(),
        P(),
        P(None, "seq"),
        P(None, "seq"),
    )
    out_specs = (
        P("dp", "seq", None),
        P("dp", "seq", None),
        P(),
        P(),
        P(),
        P(),
        P(),
        P(None, "seq"),
        P(None, "seq"),
    )
    return jax.shard_map(shards, mesh=mesh, in_specs=in_specs, out_specs=out_specs, check_vma=False)
```

```python
import math

import numpy as np

import jax
import jax.numpy as jnp
from jax import lax
from jax.sharding import PartitionSpec as P

PRECISION = lax.Precision.HIGH
LANES = 128


def dft_tables(length):
    size = 2 * length
    rows = size // LANES
    half = length // LANES
    k1 = np.arange(rows)
    f1 = np.exp(-2j * np.pi * (np.outer(k1, np.arange(half)) % rows) / rows)
    turn = np.exp(-2j * np.pi * np.outer(k1, np.arange(LANES)) / size)
    f2 = np.exp(-2j * np.pi * (np.outer(np.arange(LANES), np.arange(LANES)) % LANES) / LANES)
    fwd1 = np.concatenate([f1.real, f1.imag], axis=0)
    fwd2 = np.block([[f2.real, f2.imag], [-f2.imag, f2.real]])
    inv2 = np.block([[f2.real, -f2.imag], [f2.imag, f2.real]])
    inv1 = np.concatenate([f1.real.T, f1.imag.T], axis=1) / size
    as32 = lambda a: jnp.asarray(np.asarray(a, np.float32))
    return {
        "rows": rows,
        "fwd1": as32(fwd1),
        "fwd2": as32(fwd2),
        "inv1": as32(inv1),
        "inv2": as32(inv2),
        "turn_r": as32(turn.real)[:, None, :],
        "turn_i": as32(turn.imag)[:, None, :],
    }


def spectrum(x, tab):
    rows = tab["rows"]
    a = jnp.einsum("kn,ncm->kcm", tab["fwd1"], x, precision=PRECISION)
    ar, ai = a[:rows], a[rows:]
    tr, ti = tab["turn_r"], tab["turn_i"]
    cat = jnp.concatenate([ar * tr - ai * ti, ar * ti + ai * tr], axis=-1)
    return jnp.einsum("kcm,mj->kcj", cat, tab["fwd2"], precision=PRECISION)


def signal(s, tab):
    b = jnp.einsum("kcj,jm->kcm", s, tab["inv2"], precision=PRECISION)
    br, bi = b[..., :LANES], b[..., LANES:]
    tr, ti = tab["turn_r"], tab["turn_i"]
    stacked = jnp.concatenate([br * tr + bi * ti, bi * tr - br * ti], axis=0)
    return jnp.einsum("nk,kcm->ncm", tab["inv1"], stacked, precision=PRECISION)


def cmul(a, b, conj=False):
    ar, ai = a[..., :LANES], a[..., LANES:]
    br, bi = b[..., :LANES], b[..., LANES:]
    if conj:
        bi = -bi
    return jnp.concatenate([ar * br - ai * bi, ar * bi + ai * br], axis=-1)


def fold(x):
    c, length = x.shape
    return jnp.swapaxes(x.reshape(c, length // LANES, LANES), 0, 1)


def unfold(x):
    half, c, lanes = x.shape
    return jnp.swapaxes(x, 0, 1).reshape(c, half * lanes)


def shards(series, cotangent, w_in, w_out, taps, skip_one, skip_two, filter_one, filter_two):
    _, block, width = series.shape
    seq_n = lax.axis_size("seq")
    dp_n = lax.axis_size("dp")
    length = block * seq_n
    half = length // LANES
    me = lax.axis_index("seq")
    per = width // seq_n
    filters = filter_one.shape[0]
    group_width = width // filters
    per_group = group_width // per
    group = me // per_group
    grad_scale = 1.0 / math.sqrt(dp_n * series.shape[0] * length)
    tab = dft_tables(length)

    taps_sel = lax.dynamic_index_in_dim(
        taps.reshape(3, 3, seq_n, per), me, axis=2, keepdims=False
    ).reshape(3, 3 * per)
    skip1 = lax.dynamic_index_in_dim(skip_one.reshape(seq_n, per), me, axis=0, keepdims=False)
    skip2 = lax.dynamic_index_in_dim(skip_two.reshape(seq_n, per), me, axis=0, keepdims=False)
    skip1 = skip1[None, :, None]
    skip2 = skip2[None, :, None]

    proj_blk = jnp.einsum("td,dc->ct", series[0], w_in, preferred_element_type=jnp.float32)
    proj_blk = jnp.swapaxes(proj_blk.reshape(3, seq_n, per, block), 0, 1).reshape(seq_n, 3 * per, block)
    dprod_blk = jnp.einsum("td,cd->ct", cotangent[0], w_out, preferred_element_type=jnp.float32)
    dprod_blk = dprod_blk.reshape(seq_n, per, block)
    rows_sent = jnp.repeat(jnp.swapaxes(jnp.stack([filter_one, filter_two]), 0, 1), per_group, axis=0)
    got = lax.all_to_all(jnp.concatenate([proj_blk, rows_sent], axis=1), "seq", 0, 0, tiled=True)
    proj = jnp.swapaxes(got[:, : 3 * per], 0, 1).reshape(3 * per, length)
    h_rows = jnp.swapaxes(got[:, 3 * per :], 0, 1).reshape(2, length)
    dprod_got = lax.all_to_all(dprod_blk, "seq", 0, 0, tiled=True)
    d_product = jnp.swapaxes(
        dprod_got.reshape(seq_n, per, block // LANES, LANES), 1, 2
    ).reshape(half, per, LANES)
    prev1 = jnp.pad(proj, ((0, 0), (1, 0)))[:, :length]
    prev2 = jnp.pad(proj, ((0, 0), (2, 0)))[:, :length]
    conv = taps_sel[0][:, None] * proj + taps_sel[1][:, None] * prev1 + taps_sel[2][:, None] * prev2
    conv_f = fold(conv)
    value = conv_f[:, :per]
    gate_one = conv_f[:, per : 2 * per]
    gate_two = conv_f[:, 2 * per :]

    h_spec = spectrum(fold(h_rows), tab)
    h_one = h_spec[:, 0:1]
    h_two = h_spec[:, 1:2]

    v_spec = spectrum(value, tab)
    y_one = signal(cmul(v_spec, h_one), tab) + skip1 * value
    gated_mid = gate_one * y_one
    m_spec = spectrum(gated_mid, tab)
    y_two = signal(cmul(m_spec, h_two), tab) + skip2 * gated_mid
    product = (gate_two * y_two).astype(jnp.bfloat16)

    grad_two = d_product * gate_two
    d_gate_two = d_product * y_two
    g2_spec = spectrum(grad_two, tab)
    d_mid = signal(cmul(g2_spec, h_two, conj=True), tab) + skip2 * grad_two
    grad_one = d_mid * gate_one
    d_gate_one = d_mid * y_one
    g1_spec = spectrum(grad_one, tab)
    d_value = signal(cmul(g1_spec, h_one, conj=True), tab) + skip1 * grad_one

    corr = jnp.concatenate(
        [
            jnp.sum(cmul(g1_spec, v_spec, conj=True), axis=1, keepdims=True),
            jnp.sum(cmul(g2_spec, m_spec, conj=True), axis=1, keepdims=True),
        ],
        axis=1,
    )
    filt_grad = unfold(signal(corr, tab))

    d_conv = unfold(jnp.concatenate([d_value, d_gate_one, d_gate_two], axis=1))
    next1 = jnp.pad(d_conv, ((0, 0), (0, 1)))[:, 1:]
    next2 = jnp.pad(d_conv, ((0, 0), (0, 2)))[:, 2:]
    d_proj = (
        taps_sel[0][:, None] * d_conv + taps_sel[1][:, None] * next1 + taps_sel[2][:, None] * next2
    ).astype(jnp.bfloat16)

    local_taps = jnp.stack(
        [jnp.sum(d_conv * proj, axis=1), jnp.sum(d_conv * prev1, axis=1), jnp.sum(d_conv * prev2, axis=1)]
    )
    local_skip1 = jnp.sum(grad_one * value, axis=(0, 2))
    local_skip2 = jnp.sum(grad_two * gated_mid, axis=(0, 2))
    prod_sent = jnp.swapaxes(product.reshape(seq_n, half // seq_n, per, LANES), 1, 2)
    prod_sent = prod_sent.reshape(seq_n, per, block)
    prod_got = lax.all_to_all(prod_sent, "seq", 0, 0, tiled=True)
    dp_sent = jnp.swapaxes(d_proj.reshape(3 * per, seq_n, block), 0, 1)
    dp_got = lax.all_to_all(dp_sent, "seq", 0, 0, tiled=True)
    prod_rows = jnp.transpose(prod_got, (2, 0, 1)).reshape(block, width)
    dp_rows = jnp.transpose(dp_got.reshape(seq_n, 3, per, block), (3, 1, 0, 2))
    dp_rows = dp_rows.reshape(block, 3 * width)
    output = jnp.dot(prod_rows, w_out, preferred_element_type=jnp.float32).astype(jnp.bfloat16)
    output = output.reshape(1, block, width)
    d_series = jnp.einsum(
        "tc,dc->td", dp_rows, w_in, preferred_element_type=jnp.float32
    ).astype(jnp.bfloat16)
    d_series = d_series.reshape(1, block, width)

    local_w_in = jnp.einsum("td,tc->dc", series[0], dp_rows, preferred_element_type=jnp.float32)
    local_w_out = jnp.einsum("tc,td->cd", prod_rows, cotangent[0], preferred_element_type=jnp.float32)
    small = jnp.concatenate(
        [
            local_taps.reshape(3, 3, 1, per),
            jnp.stack([local_skip1, local_skip2, jnp.zeros_like(local_skip1)]).reshape(3, 1, 1, per),
        ],
        axis=1,
    )
    small_full = lax.dynamic_update_slice(
        jnp.zeros((3, 4, seq_n, per), jnp.float32), small, (0, 0, me, 0)
    )
    params = jnp.concatenate([local_w_in.reshape(-1), local_w_out.reshape(-1), small_full.reshape(-1)])
    n_params = params.shape[0]
    chunk = -(-n_params // (seq_n * dp_n))
    params = jnp.pad(params, (0, chunk * seq_n * dp_n - n_params)).reshape(seq_n, dp_n * chunk)

    fg_sent = jnp.swapaxes(filt_grad.reshape(2, seq_n, block), 0, 1).reshape(seq_n, 2 * block)
    got = lax.all_to_all(jnp.concatenate([params, fg_sent], axis=1), "seq", 0, 0, tiled=True)
    p_part = jnp.sum(got[:, : dp_n * chunk], axis=0).reshape(dp_n, chunk)
    f_part = jnp.sum(got[:, dp_n * chunk :].reshape(filters, per_group, 2 * block), axis=1)
    got = lax.all_to_all(jnp.concatenate([p_part, f_part], axis=1), "dp", 0, 0, tiled=True)
    mine = jnp.sum(got, axis=0)
    got = lax.all_to_all(jnp.broadcast_to(mine, (dp_n,) + mine.shape), "dp", 0, 0, tiled=True)
    fg_blocks = jnp.swapaxes(got[:, chunk:].reshape(filters, 2, block), 0, 1)
    p_seq = got[:, :chunk].reshape(1, dp_n * chunk)
    got = lax.all_to_all(jnp.broadcast_to(p_seq, (seq_n, dp_n * chunk)), "seq", 0, 0, tiled=True)
    full = got.reshape(-1)
    sizes = [width * 3 * width, width * width, 3 * 4 * width]
    offsets = np.cumsum([0] + sizes)
    grad_w_in = full[offsets[0] : offsets[1]].reshape(width, 3 * width)
    grad_w_out = full[offsets[1] : offsets[2]].reshape(width, width)
    small_full = full[offsets[2] : offsets[3]].reshape(3, 4, width)
    grad_taps = small_full[:, :3].reshape(3, 3 * width)
    grad_skip_one = small_full[0, 3]
    grad_skip_two = small_full[1, 3]

    return (
        output,
        d_series,
        grad_scale * grad_w_in,
        grad_scale * grad_w_out,
        grad_scale * grad_taps,
        grad_scale * grad_skip_one,
        grad_scale * grad_skip_two,
        grad_scale * fg_blocks[0],
        grad_scale * fg_blocks[1],
    )


def solution(mesh):
    in_specs = (
        P("dp", "seq", None),
        P("dp", "seq", None),
        P(),
        P(),
        P(),
        P(),
        P(),
        P(None, "seq"),
        P(None, "seq"),
    )
    out_specs = (
        P("dp", "seq", None),
        P("dp", "seq", None),
        P(),
        P(),
        P(),
        P(),
        P(),
        P(None, "seq"),
        P(None, "seq"),
    )
    return jax.shard_map(shards, mesh=mesh, in_specs=in_specs, out_specs=out_specs, check_vma=False)
```

```python
import math

import numpy as np

import jax
import jax.numpy as jnp
from jax import lax
from jax.sharding import PartitionSpec as P

PRECISION = lax.Precision.HIGH
LANES = 128


def dft_tables(length):
    size = 2 * length
    rows = size // LANES
    half = length // LANES
    k1 = np.arange(rows)
    f1 = np.exp(-2j * np.pi * (np.outer(k1, np.arange(half)) % rows) / rows)
    turn = np.exp(-2j * np.pi * np.outer(k1, np.arange(LANES)) / size)
    f2 = np.exp(-2j * np.pi * (np.outer(np.arange(LANES), np.arange(LANES)) % LANES) / LANES)
    fwd1 = np.concatenate([f1.real, f1.imag], axis=0)
    fwd2 = np.block([[f2.real, f2.imag], [-f2.imag, f2.real]])
    inv2 = np.block([[f2.real, -f2.imag], [f2.imag, f2.real]])
    inv1 = np.concatenate([f1.real.T, f1.imag.T], axis=1) / size
    as32 = lambda a: jnp.asarray(np.asarray(a, np.float32))
    return {
        "rows": rows,
        "fwd1": as32(fwd1),
        "fwd2": as32(fwd2),
        "inv1": as32(inv1),
        "inv2": as32(inv2),
        "turn_r": as32(turn.real)[:, None, :],
        "turn_i": as32(turn.imag)[:, None, :],
    }


def spectrum(x, tab):
    rows = tab["rows"]
    a = jnp.einsum("kn,ncm->kcm", tab["fwd1"], x, precision=PRECISION)
    ar, ai = a[:rows], a[rows:]
    tr, ti = tab["turn_r"], tab["turn_i"]
    cat = jnp.concatenate([ar * tr - ai * ti, ar * ti + ai * tr], axis=-1)
    return jnp.einsum("kcm,mj->kcj", cat, tab["fwd2"], precision=PRECISION)


def signal(s, tab):
    b = jnp.einsum("kcj,jm->kcm", s, tab["inv2"], precision=PRECISION)
    br, bi = b[..., :LANES], b[..., LANES:]
    tr, ti = tab["turn_r"], tab["turn_i"]
    stacked = jnp.concatenate([br * tr + bi * ti, bi * tr - br * ti], axis=0)
    return jnp.einsum("nk,kcm->ncm", tab["inv1"], stacked, precision=PRECISION)


def cmul(a, b, conj=False):
    ar, ai = a[..., :LANES], a[..., LANES:]
    br, bi = b[..., :LANES], b[..., LANES:]
    if conj:
        bi = -bi
    return jnp.concatenate([ar * br - ai * bi, ar * bi + ai * br], axis=-1)


def fold(x):
    c, length = x.shape
    return jnp.swapaxes(x.reshape(c, length // LANES, LANES), 0, 1)


def unfold(x):
    half, c, lanes = x.shape
    return jnp.swapaxes(x, 0, 1).reshape(c, half * lanes)


def shards(series, cotangent, w_in, w_out, taps, skip_one, skip_two, filter_one, filter_two):
    _, block, width = series.shape
    seq_n = lax.axis_size("seq")
    dp_n = lax.axis_size("dp")
    length = block * seq_n
    half = length // LANES
    me = lax.axis_index("seq")
    per = width // seq_n
    filters = filter_one.shape[0]
    group_width = width // filters
    per_group = group_width // per
    group = me // per_group
    grad_scale = 1.0 / math.sqrt(dp_n * series.shape[0] * length)
    tab = dft_tables(length)

    taps_sel = lax.dynamic_index_in_dim(
        taps.reshape(3, 3, seq_n, per), me, axis=2, keepdims=False
    ).reshape(3, 3 * per)
    skip1 = lax.dynamic_index_in_dim(skip_one.reshape(seq_n, per), me, axis=0, keepdims=False)
    skip2 = lax.dynamic_index_in_dim(skip_two.reshape(seq_n, per), me, axis=0, keepdims=False)
    skip1 = skip1[None, :, None]
    skip2 = skip2[None, :, None]

    proj_blk = jnp.einsum("td,dc->ct", series[0], w_in, preferred_element_type=jnp.float32)
    proj_blk = jnp.swapaxes(proj_blk.reshape(3, seq_n, per, block), 0, 1).reshape(seq_n, 3 * per, block)
    dprod_blk = jnp.einsum("td,cd->ct", cotangent[0], w_out, preferred_element_type=jnp.float32)
    dprod_blk = dprod_blk.reshape(seq_n, per, block)
    rows_sent = jnp.repeat(jnp.swapaxes(jnp.stack([filter_one, filter_two]), 0, 1), per_group, axis=0)
    got = lax.all_to_all(
        jnp.concatenate([proj_blk, dprod_blk, rows_sent], axis=1), "seq", 0, 0, tiled=True
    )
    proj = jnp.swapaxes(got[:, : 3 * per], 0, 1).reshape(3 * per, length)
    d_product = jnp.swapaxes(
        got[:, 3 * per : 4 * per].reshape(seq_n, per, block // LANES, LANES), 1, 2
    ).reshape(half, per, LANES)
    h_rows = jnp.swapaxes(got[:, 4 * per :], 0, 1).reshape(2, length)
    prev1 = jnp.pad(proj, ((0, 0), (1, 0)))[:, :length]
    prev2 = jnp.pad(proj, ((0, 0), (2, 0)))[:, :length]
    conv = taps_sel[0][:, None] * proj + taps_sel[1][:, None] * prev1 + taps_sel[2][:, None] * prev2
    conv_f = fold(conv)
    value = conv_f[:, :per]
    gate_one = conv_f[:, per : 2 * per]
    gate_two = conv_f[:, 2 * per :]

    h_spec = spectrum(fold(h_rows), tab)
    h_one = h_spec[:, 0:1]
    h_two = h_spec[:, 1:2]

    v_spec = spectrum(value, tab)
    y_one = signal(cmul(v_spec, h_one), tab) + skip1 * value
    gated_mid = gate_one * y_one
    m_spec = spectrum(gated_mid, tab)
    y_two = signal(cmul(m_spec, h_two), tab) + skip2 * gated_mid
    product = (gate_two * y_two).astype(jnp.bfloat16)

    grad_two = d_product * gate_two
    d_gate_two = d_product * y_two
    g2_spec = spectrum(grad_two, tab)
    d_mid = signal(cmul(g2_spec, h_two, conj=True), tab) + skip2 * grad_two
    grad_one = d_mid * gate_one
    d_gate_one = d_mid * y_one
    g1_spec = spectrum(grad_one, tab)
    d_value = signal(cmul(g1_spec, h_one, conj=True), tab) + skip1 * grad_one

    corr = jnp.concatenate(
        [
            jnp.sum(cmul(g1_spec, v_spec, conj=True), axis=1, keepdims=True),
            jnp.sum(cmul(g2_spec, m_spec, conj=True), axis=1, keepdims=True),
        ],
        axis=1,
    )
    filt_grad = unfold(signal(corr, tab))

    d_conv = unfold(jnp.concatenate([d_value, d_gate_one, d_gate_two], axis=1))
    next1 = jnp.pad(d_conv, ((0, 0), (0, 1)))[:, 1:]
    next2 = jnp.pad(d_conv, ((0, 0), (0, 2)))[:, 2:]
    d_proj = (
        taps_sel[0][:, None] * d_conv + taps_sel[1][:, None] * next1 + taps_sel[2][:, None] * next2
    ).astype(jnp.bfloat16)

    local_taps = jnp.stack(
        [jnp.sum(d_conv * proj, axis=1), jnp.sum(d_conv * prev1, axis=1), jnp.sum(d_conv * prev2, axis=1)]
    )
    local_skip1 = jnp.sum(grad_one * value, axis=(0, 2))
    local_skip2 = jnp.sum(grad_two * gated_mid, axis=(0, 2))
    prod_sent = jnp.swapaxes(product.reshape(seq_n, half // seq_n, per, LANES), 1, 2)
    prod_sent = prod_sent.reshape(seq_n, per, block)
    dp_sent = jnp.swapaxes(d_proj.reshape(3 * per, seq_n, block), 0, 1)
    back = lax.all_to_all(jnp.concatenate([prod_sent, dp_sent], axis=1), "seq", 0, 0, tiled=True)
    prod_rows = jnp.transpose(back[:, :per], (2, 0, 1)).reshape(block, width)
    dp_rows = jnp.transpose(back[:, per:].reshape(seq_n, 3, per, block), (3, 1, 0, 2))
    dp_rows = dp_rows.reshape(block, 3 * width)
    output = jnp.dot(prod_rows, w_out, preferred_element_type=jnp.float32).astype(jnp.bfloat16)
    output = output.reshape(1, block, width)
    d_series = jnp.einsum(
        "tc,dc->td", dp_rows, w_in, preferred_element_type=jnp.float32
    ).astype(jnp.bfloat16)
    d_series = d_series.reshape(1, block, width)

    local_w_in = jnp.einsum("td,tc->dc", series[0], dp_rows, preferred_element_type=jnp.float32)
    local_w_out = jnp.einsum("tc,td->cd", prod_rows, cotangent[0], preferred_element_type=jnp.float32)
    small = jnp.concatenate(
        [
            local_taps.reshape(3, 3, 1, per),
            jnp.stack([local_skip1, local_skip2, jnp.zeros_like(local_skip1)]).reshape(3, 1, 1, per),
        ],
        axis=1,
    )
    small_full = lax.dynamic_update_slice(
        jnp.zeros((3, 4, seq_n, per), jnp.float32), small, (0, 0, me, 0)
    )
    params = jnp.concatenate([local_w_in.reshape(-1), local_w_out.reshape(-1), small_full.reshape(-1)])
    n_params = params.shape[0]
    chunk = -(-n_params // (seq_n * dp_n))
    params = jnp.pad(params, (0, chunk * seq_n * dp_n - n_params)).reshape(seq_n, dp_n * chunk)

    fg_sent = jnp.swapaxes(filt_grad.reshape(2, seq_n, block), 0, 1).reshape(seq_n, 2 * block)
    got = lax.all_to_all(jnp.concatenate([params, fg_sent], axis=1), "seq", 0, 0, tiled=True)
    p_part = jnp.sum(got[:, : dp_n * chunk], axis=0).reshape(dp_n, chunk)
    f_part = jnp.sum(got[:, dp_n * chunk :].reshape(filters, per_group, 2 * block), axis=1)
    both = jnp.concatenate([p_part, f_part], axis=1)
    got = lax.all_to_all(jnp.broadcast_to(both, (dp_n,) + both.shape), "dp", 0, 0, tiled=True)
    got = jnp.sum(got.reshape((dp_n,) + both.shape), axis=0)
    fg_blocks = jnp.swapaxes(got[:, chunk:].reshape(filters, 2, block), 0, 1)
    p_seq = got[:, :chunk].reshape(1, dp_n * chunk)
    got = lax.all_to_all(jnp.broadcast_to(p_seq, (seq_n, dp_n * chunk)), "seq", 0, 0, tiled=True)
    full = got.reshape(-1)
    sizes = [width * 3 * width, width * width, 3 * 4 * width]
    offsets = np.cumsum([0] + sizes)
    grad_w_in = full[offsets[0] : offsets[1]].reshape(width, 3 * width)
    grad_w_out = full[offsets[1] : offsets[2]].reshape(width, width)
    small_full = full[offsets[2] : offsets[3]].reshape(3, 4, width)
    grad_taps = small_full[:, :3].reshape(3, 3 * width)
    grad_skip_one = small_full[0, 3]
    grad_skip_two = small_full[1, 3]

    return (
        output,
        d_series,
        grad_scale * grad_w_in,
        grad_scale * grad_w_out,
        grad_scale * grad_taps,
        grad_scale * grad_skip_one,
        grad_scale * grad_skip_two,
        grad_scale * fg_blocks[0],
        grad_scale * fg_blocks[1],
    )


def solution(mesh):
    in_specs = (
        P("dp", "seq", None),
        P("dp", "seq", None),
        P(),
        P(),
        P(),
        P(),
        P(),
        P(None, "seq"),
        P(None, "seq"),
    )
    out_specs = (
        P("dp", "seq", None),
        P("dp", "seq", None),
        P(),
        P(),
        P(),
        P(),
        P(),
        P(None, "seq"),
        P(None, "seq"),
    )
    return jax.shard_map(shards, mesh=mesh, in_specs=in_specs, out_specs=out_specs, check_vma=False)
```

```python
import math

import numpy as np

import jax
import jax.numpy as jnp
from jax import lax
from jax.experimental import pallas as pl
from jax.experimental.pallas import tpu as pltpu
from jax.sharding import PartitionSpec as P

PRECISION = lax.Precision.HIGH
LANES = 128


def dft_tables(length):
    size = 2 * length
    rows = size // LANES
    half = length // LANES
    k1 = np.arange(rows)
    f1 = np.exp(-2j * np.pi * (np.outer(k1, np.arange(half)) % rows) / rows)
    turn = np.exp(-2j * np.pi * np.outer(k1, np.arange(LANES)) / size)
    f2 = np.exp(-2j * np.pi * (np.outer(np.arange(LANES), np.arange(LANES)) % LANES) / LANES)
    fwd1 = np.concatenate([f1.real, f1.imag], axis=0)
    fwd2 = np.block([[f2.real, f2.imag], [-f2.imag, f2.real]])
    inv2 = np.block([[f2.real, -f2.imag], [f2.imag, f2.real]])
    inv1 = np.concatenate([f1.real.T, f1.imag.T], axis=1) / size
    as32 = lambda a: jnp.asarray(np.asarray(a, np.float32))
    return {
        "rows": rows,
        "fwd1": as32(fwd1),
        "fwd2": as32(fwd2),
        "inv1": as32(inv1),
        "inv2": as32(inv2),
        "turn_r": as32(turn.real)[:, None, :],
        "turn_i": as32(turn.imag)[:, None, :],
    }


def spectrum(x, tab):
    rows = tab["rows"]
    a = jnp.einsum("kn,ncm->kcm", tab["fwd1"], x, precision=PRECISION)
    ar, ai = a[:rows], a[rows:]
    tr, ti = tab["turn_r"], tab["turn_i"]
    cat = jnp.concatenate([ar * tr - ai * ti, ar * ti + ai * tr], axis=-1)
    return jnp.einsum("kcm,mj->kcj", cat, tab["fwd2"], precision=PRECISION)


def signal(s, tab):
    b = jnp.einsum("kcj,jm->kcm", s, tab["inv2"], precision=PRECISION)
    br, bi = b[..., :LANES], b[..., LANES:]
    tr, ti = tab["turn_r"], tab["turn_i"]
    stacked = jnp.concatenate([br * tr + bi * ti, bi * tr - br * ti], axis=0)
    return jnp.einsum("nk,kcm->ncm", tab["inv1"], stacked, precision=PRECISION)


def cmul(a, b, conj=False):
    ar, ai = a[..., :LANES], a[..., LANES:]
    br, bi = b[..., :LANES], b[..., LANES:]
    if conj:
        bi = -bi
    return jnp.concatenate([ar * br - ai * bi, ar * bi + ai * br], axis=-1)


def fold(x):
    c, length = x.shape
    return jnp.swapaxes(x.reshape(c, length // LANES, LANES), 0, 1)


def unfold(x):
    half, c, lanes = x.shape
    return jnp.swapaxes(x, 0, 1).reshape(c, half * lanes)


def reduce_rounds(msg, param_rows, pair, dp_n):
    seq_n, msg_rows, lanes = msg.shape
    filter_rows = msg_rows - param_rows
    groups = seq_n // pair
    mesh = pl.DeviceIdType.MESH

    def kernel(msg_ref, full_ref, fg_ref, rs_buf, ag_buf, sems):
        ms = lax.axis_index("seq")
        md = lax.axis_index("dp")
        barrier = pltpu.get_barrier_semaphore()
        for k in range(1, seq_n):
            pl.semaphore_signal(barrier, inc=1, device_id=(md, lax.rem(ms + k, seq_n)), device_id_type=mesh)
        for k in range(1, dp_n):
            pl.semaphore_signal(barrier, inc=1, device_id=(lax.rem(md + k, dp_n), ms), device_id_type=mesh)
        pl.semaphore_wait(barrier, seq_n + dp_n - 2)

        def send_all(count, src, dst, stage, where):
            copies = []
            for k in range(1, count):
                copy = pltpu.make_async_remote_copy(
                    src_ref=src(k), dst_ref=dst, send_sem=sems.at[stage, 0, k],
                    recv_sem=sems.at[stage, 1, k], device_id=where(k), device_id_type=mesh,
                )
                copy.start()
                copies.append(copy)
            return copies

        seq_peer = lambda k: (md, lax.rem(ms + k, seq_n))
        dp_peer = lambda k: (lax.rem(md + k, dp_n), ms)

        copies = send_all(seq_n, lambda k: msg_ref.at[lax.rem(ms + k, seq_n)], rs_buf.at[ms], 0, seq_peer)
        rs_buf[pl.ds(ms, 1)] = msg_ref[pl.ds(ms, 1)]
        for copy in copies:
            copy.wait()
        got = rs_buf[...]
        p_sum = jnp.sum(got[:, :param_rows], axis=0)
        f_sum = jnp.sum(got[:, param_rows:].reshape(groups, pair, filter_rows, lanes), axis=1)
        mine = jnp.concatenate([p_sum, f_sum.reshape(groups * filter_rows, lanes)], axis=0)

        ag_buf[pl.ds(md, 1)] = mine[None]
        copies = send_all(dp_n, lambda k: ag_buf.at[md], ag_buf.at[md], 1, dp_peer)
        for copy in copies:
            copy.wait()
        total = jnp.sum(ag_buf[...], axis=0)
        fg_ref[...] = total[param_rows:].reshape(groups, filter_rows, lanes)

        full_ref[pl.ds(ms, 1)] = total[:param_rows][None]
        copies = send_all(seq_n, lambda k: full_ref.at[ms], full_ref.at[ms], 2, seq_peer)
        for copy in copies:
            copy.wait()

    ag_rows = param_rows + groups * filter_rows
    return pl.pallas_call(
        kernel,
        out_shape=(
            jax.ShapeDtypeStruct((seq_n, param_rows, lanes), msg.dtype),
            jax.ShapeDtypeStruct((groups, filter_rows, lanes), msg.dtype),
        ),
        in_specs=[pl.BlockSpec(memory_space=pltpu.VMEM)],
        out_specs=(pl.BlockSpec(memory_space=pltpu.VMEM), pl.BlockSpec(memory_space=pltpu.VMEM)),
        scratch_shapes=[
            pltpu.VMEM((seq_n, msg_rows, lanes), msg.dtype),
            pltpu.VMEM((dp_n, ag_rows, lanes), msg.dtype),
            pltpu.SemaphoreType.DMA((3, 2, max(seq_n, dp_n))),
        ],
        compiler_params=pltpu.CompilerParams(collective_id=0, has_side_effects=True),
    )(msg)


def shards(series, cotangent, w_in, w_out, taps, skip_one, skip_two, filter_one, filter_two):
    _, block, width = series.shape
    seq_n = lax.axis_size("seq")
    dp_n = lax.axis_size("dp")
    length = block * seq_n
    half = length // LANES
    me = lax.axis_index("seq")
    per = width // seq_n
    filters = filter_one.shape[0]
    group_width = width // filters
    per_group = group_width // per
    group = me // per_group
    grad_scale = 1.0 / math.sqrt(dp_n * series.shape[0] * length)
    tab = dft_tables(length)

    taps_sel = lax.dynamic_index_in_dim(
        taps.reshape(3, 3, seq_n, per), me, axis=2, keepdims=False
    ).reshape(3, 3 * per)
    skip1 = lax.dynamic_index_in_dim(skip_one.reshape(seq_n, per), me, axis=0, keepdims=False)
    skip2 = lax.dynamic_index_in_dim(skip_two.reshape(seq_n, per), me, axis=0, keepdims=False)
    skip1 = skip1[None, :, None]
    skip2 = skip2[None, :, None]

    proj_blk = jnp.einsum("td,dc->ct", series[0], w_in, preferred_element_type=jnp.float32)
    proj_blk = jnp.swapaxes(proj_blk.reshape(3, seq_n, per, block), 0, 1).reshape(seq_n, 3 * per, block)
    dprod_blk = jnp.einsum("td,cd->ct", cotangent[0], w_out, preferred_element_type=jnp.float32)
    dprod_blk = dprod_blk.reshape(seq_n, per, block)
    rows_sent = jnp.repeat(jnp.swapaxes(jnp.stack([filter_one, filter_two]), 0, 1), per_group, axis=0)
    got = lax.all_to_all(
        jnp.concatenate([proj_blk, dprod_blk, rows_sent], axis=1), "seq", 0, 0, tiled=True
    )
    proj = jnp.swapaxes(got[:, : 3 * per], 0, 1).reshape(3 * per, length)
    d_product = jnp.swapaxes(
        got[:, 3 * per : 4 * per].reshape(seq_n, per, block // LANES, LANES), 1, 2
    ).reshape(half, per, LANES)
    h_rows = jnp.swapaxes(got[:, 4 * per :], 0, 1).reshape(2, length)
    prev1 = jnp.pad(proj, ((0, 0), (1, 0)))[:, :length]
    prev2 = jnp.pad(proj, ((0, 0), (2, 0)))[:, :length]
    conv = taps_sel[0][:, None] * proj + taps_sel[1][:, None] * prev1 + taps_sel[2][:, None] * prev2
    conv_f = fold(conv)
    value = conv_f[:, :per]
    gate_one = conv_f[:, per : 2 * per]
    gate_two = conv_f[:, 2 * per :]

    h_spec = spectrum(fold(h_rows), tab)
    h_one = h_spec[:, 0:1]
    h_two = h_spec[:, 1:2]

    v_spec = spectrum(value, tab)
    y_one = signal(cmul(v_spec, h_one), tab) + skip1 * value
    gated_mid = gate_one * y_one
    m_spec = spectrum(gated_mid, tab)
    y_two = signal(cmul(m_spec, h_two), tab) + skip2 * gated_mid
    product = (gate_two * y_two).astype(jnp.bfloat16)

    grad_two = d_product * gate_two
    d_gate_two = d_product * y_two
    g2_spec = spectrum(grad_two, tab)
    d_mid = signal(cmul(g2_spec, h_two, conj=True), tab) + skip2 * grad_two
    grad_one = d_mid * gate_one
    d_gate_one = d_mid * y_one
    g1_spec = spectrum(grad_one, tab)
    d_value = signal(cmul(g1_spec, h_one, conj=True), tab) + skip1 * grad_one

    corr = jnp.concatenate(
        [
            jnp.sum(cmul(g1_spec, v_spec, conj=True), axis=1, keepdims=True),
            jnp.sum(cmul(g2_spec, m_spec, conj=True), axis=1, keepdims=True),
        ],
        axis=1,
    )
    filt_grad = unfold(signal(corr, tab))

    d_conv = unfold(jnp.concatenate([d_value, d_gate_one, d_gate_two], axis=1))
    next1 = jnp.pad(d_conv, ((0, 0), (0, 1)))[:, 1:]
    next2 = jnp.pad(d_conv, ((0, 0), (0, 2)))[:, 2:]
    d_proj = (
        taps_sel[0][:, None] * d_conv + taps_sel[1][:, None] * next1 + taps_sel[2][:, None] * next2
    ).astype(jnp.bfloat16)

    local_taps = jnp.stack(
        [jnp.sum(d_conv * proj, axis=1), jnp.sum(d_conv * prev1, axis=1), jnp.sum(d_conv * prev2, axis=1)]
    )
    local_skip1 = jnp.sum(grad_one * value, axis=(0, 2))
    local_skip2 = jnp.sum(grad_two * gated_mid, axis=(0, 2))
    prod_sent = jnp.swapaxes(product.reshape(seq_n, half // seq_n, per, LANES), 1, 2)
    prod_sent = prod_sent.reshape(seq_n, per, block)
    dp_sent = jnp.swapaxes(d_proj.reshape(3 * per, seq_n, block), 0, 1)
    back = lax.all_to_all(jnp.concatenate([prod_sent, dp_sent], axis=1), "seq", 0, 0, tiled=True)
    prod_rows = jnp.transpose(back[:, :per], (2, 0, 1)).reshape(block, width)
    dp_rows = jnp.transpose(back[:, per:].reshape(seq_n, 3, per, block), (3, 1, 0, 2))
    dp_rows = dp_rows.reshape(block, 3 * width)
    output = jnp.dot(prod_rows, w_out, preferred_element_type=jnp.float32).astype(jnp.bfloat16)
    output = output.reshape(1, block, width)
    d_series = jnp.einsum(
        "tc,dc->td", dp_rows, w_in, preferred_element_type=jnp.float32
    ).astype(jnp.bfloat16)
    d_series = d_series.reshape(1, block, width)

    local_w_in = jnp.einsum("td,tc->dc", series[0], dp_rows, preferred_element_type=jnp.float32)
    local_w_out = jnp.einsum("tc,td->cd", prod_rows, cotangent[0], preferred_element_type=jnp.float32)
    small = jnp.concatenate(
        [
            local_taps.reshape(3, 3, 1, per),
            jnp.stack([local_skip1, local_skip2, jnp.zeros_like(local_skip1)]).reshape(3, 1, 1, per),
        ],
        axis=1,
    )
    small_full = lax.dynamic_update_slice(
        jnp.zeros((3, 4, seq_n, per), jnp.float32), small, (0, 0, me, 0)
    )
    params = jnp.concatenate([local_w_in.reshape(-1), local_w_out.reshape(-1), small_full.reshape(-1)])
    n_params = params.shape[0]
    chunk = -(-n_params // (seq_n * dp_n * 8 * LANES)) * 8 * LANES
    params = jnp.pad(params, (0, chunk * seq_n * dp_n - n_params)).reshape(seq_n, -1, LANES)
    fg_sent = jnp.swapaxes(filt_grad.reshape(2, seq_n, block), 0, 1).reshape(seq_n, -1, LANES)
    full, fg = reduce_rounds(jnp.concatenate([params, fg_sent], axis=1), params.shape[1], per_group, dp_n)
    fg_blocks = jnp.swapaxes(fg.reshape(filters, 2, block), 0, 1)
    full = full.reshape(-1)
    sizes = [width * 3 * width, width * width, 3 * 4 * width]
    offsets = np.cumsum([0] + sizes)
    grad_w_in = full[offsets[0] : offsets[1]].reshape(width, 3 * width)
    grad_w_out = full[offsets[1] : offsets[2]].reshape(width, width)
    small_full = full[offsets[2] : offsets[3]].reshape(3, 4, width)
    grad_taps = small_full[:, :3].reshape(3, 3 * width)
    grad_skip_one = small_full[0, 3]
    grad_skip_two = small_full[1, 3]

    return (
        output,
        d_series,
        grad_scale * grad_w_in,
        grad_scale * grad_w_out,
        grad_scale * grad_taps,
        grad_scale * grad_skip_one,
        grad_scale * grad_skip_two,
        grad_scale * fg_blocks[0],
        grad_scale * fg_blocks[1],
    )


def solution(mesh):
    in_specs = (
        P("dp", "seq", None),
        P("dp", "seq", None),
        P(),
        P(),
        P(),
        P(),
        P(),
        P(None, "seq"),
        P(None, "seq"),
    )
    out_specs = (
        P("dp", "seq", None),
        P("dp", "seq", None),
        P(),
        P(),
        P(),
        P(),
        P(),
        P(None, "seq"),
        P(None, "seq"),
    )
    return jax.shard_map(shards, mesh=mesh, in_specs=in_specs, out_specs=out_specs, check_vma=False)
```

```python
import math

import numpy as np

import jax
import jax.numpy as jnp
from jax import lax
from jax.experimental import pallas as pl
from jax.experimental.pallas import tpu as pltpu
from jax.sharding import PartitionSpec as P

PRECISION = lax.Precision.HIGH
LANES = 128


def dft_tables(length):
    size = 2 * length
    rows = size // LANES
    half = length // LANES
    k1 = np.arange(rows)
    f1 = np.exp(-2j * np.pi * (np.outer(k1, np.arange(half)) % rows) / rows)
    turn = np.exp(-2j * np.pi * np.outer(k1, np.arange(LANES)) / size)
    f2 = np.exp(-2j * np.pi * (np.outer(np.arange(LANES), np.arange(LANES)) % LANES) / LANES)
    fwd1 = np.concatenate([f1.real, f1.imag], axis=0)
    fwd2 = np.block([[f2.real, f2.imag], [-f2.imag, f2.real]])
    inv2 = np.block([[f2.real, -f2.imag], [f2.imag, f2.real]])
    inv1 = np.concatenate([f1.real.T, f1.imag.T], axis=1) / size
    as32 = lambda a: jnp.asarray(np.asarray(a, np.float32))
    return {
        "rows": rows,
        "fwd1": as32(fwd1),
        "fwd2": as32(fwd2),
        "inv1": as32(inv1),
        "inv2": as32(inv2),
        "turn_r": as32(turn.real)[:, None, :],
        "turn_i": as32(turn.imag)[:, None, :],
    }


def spectrum(x, tab):
    rows = tab["rows"]
    a = jnp.einsum("kn,ncm->kcm", tab["fwd1"], x, precision=PRECISION)
    ar, ai = a[:rows], a[rows:]
    tr, ti = tab["turn_r"], tab["turn_i"]
    cat = jnp.concatenate([ar * tr - ai * ti, ar * ti + ai * tr], axis=-1)
    return jnp.einsum("kcm,mj->kcj", cat, tab["fwd2"], precision=PRECISION)


def signal(s, tab):
    b = jnp.einsum("kcj,jm->kcm", s, tab["inv2"], precision=PRECISION)
    br, bi = b[..., :LANES], b[..., LANES:]
    tr, ti = tab["turn_r"], tab["turn_i"]
    stacked = jnp.concatenate([br * tr + bi * ti, bi * tr - br * ti], axis=0)
    return jnp.einsum("nk,kcm->ncm", tab["inv1"], stacked, precision=PRECISION)


def cmul(a, b, conj=False):
    ar, ai = a[..., :LANES], a[..., LANES:]
    br, bi = b[..., :LANES], b[..., LANES:]
    if conj:
        bi = -bi
    return jnp.concatenate([ar * br - ai * bi, ar * bi + ai * br], axis=-1)


def fold(x):
    c, length = x.shape
    return jnp.swapaxes(x.reshape(c, length // LANES, LANES), 0, 1)


def unfold(x):
    half, c, lanes = x.shape
    return jnp.swapaxes(x, 0, 1).reshape(c, half * lanes)


def reduce_rounds(msg, param_rows, pair, dp_n):
    seq_n, msg_rows, lanes = msg.shape
    filter_rows = msg_rows - param_rows
    groups = seq_n // pair
    mesh = pl.DeviceIdType.MESH

    def kernel(msg_ref, full_ref, fg_ref, rs_buf, ag_buf, sems):
        ms = lax.axis_index("seq")
        md = lax.axis_index("dp")
        barrier = pltpu.get_barrier_semaphore()
        for k in range(1, seq_n):
            pl.semaphore_signal(barrier, inc=1, device_id=(md, lax.rem(ms + k, seq_n)), device_id_type=mesh)
        for k in range(1, dp_n):
            pl.semaphore_signal(barrier, inc=1, device_id=(lax.rem(md + k, dp_n), ms), device_id_type=mesh)
        pl.semaphore_wait(barrier, seq_n + dp_n - 2)

        def send_all(count, src, dst, stage, where):
            copies = []
            for k in range(1, count):
                copy = pltpu.make_async_remote_copy(
                    src_ref=src(k), dst_ref=dst, send_sem=sems.at[stage, 0, k],
                    recv_sem=sems.at[stage, 1, k], device_id=where(k), device_id_type=mesh,
                )
                copy.start()
                copies.append(copy)
            return copies

        seq_peer = lambda k: (md, lax.rem(ms + k, seq_n))
        dp_peer = lambda k: (lax.rem(md + k, dp_n), ms)

        copies = send_all(seq_n, lambda k: msg_ref.at[lax.rem(ms + k, seq_n)], rs_buf.at[ms], 0, seq_peer)
        rs_buf[pl.ds(ms, 1)] = msg_ref[pl.ds(ms, 1)]
        for copy in copies:
            copy.wait()
        got = rs_buf[...]
        p_sum = jnp.sum(got[:, :param_rows], axis=0)
        f_sum = jnp.sum(got[:, param_rows:].reshape(groups, pair, filter_rows, lanes), axis=1)
        mine = jnp.concatenate([p_sum, f_sum.reshape(groups * filter_rows, lanes)], axis=0)

        ag_buf[pl.ds(md, 1)] = mine[None]
        copies = send_all(dp_n, lambda k: ag_buf.at[md], ag_buf.at[md], 1, dp_peer)
        for copy in copies:
            copy.wait()
        total = jnp.sum(ag_buf[...], axis=0)
        fg_ref[...] = total[param_rows:].reshape(groups, filter_rows, lanes)

        full_ref[pl.ds(ms, 1)] = total[:param_rows][None]
        copies = send_all(seq_n, lambda k: full_ref.at[ms], full_ref.at[ms], 2, seq_peer)
        for copy in copies:
            copy.wait()

    ag_rows = param_rows + groups * filter_rows
    return pl.pallas_call(
        kernel,
        out_shape=(
            jax.ShapeDtypeStruct((seq_n, param_rows, lanes), msg.dtype),
            jax.ShapeDtypeStruct((groups, filter_rows, lanes), msg.dtype),
        ),
        in_specs=[pl.BlockSpec(memory_space=pltpu.VMEM)],
        out_specs=(pl.BlockSpec(memory_space=pltpu.VMEM), pl.BlockSpec(memory_space=pltpu.VMEM)),
        scratch_shapes=[
            pltpu.VMEM((seq_n, msg_rows, lanes), msg.dtype),
            pltpu.VMEM((dp_n, ag_rows, lanes), msg.dtype),
            pltpu.SemaphoreType.DMA((3, 2, max(seq_n, dp_n))),
        ],
        compiler_params=pltpu.CompilerParams(collective_id=0, has_side_effects=True),
    )(msg)


def shards(series, cotangent, w_in, w_out, taps, skip_one, skip_two, filter_one, filter_two):
    _, block, width = series.shape
    seq_n = lax.axis_size("seq")
    dp_n = lax.axis_size("dp")
    length = block * seq_n
    half = length // LANES
    me = lax.axis_index("seq")
    per = width // seq_n
    filters = filter_one.shape[0]
    group_width = width // filters
    per_group = group_width // per
    group = me // per_group
    grad_scale = 1.0 / math.sqrt(dp_n * series.shape[0] * length)
    tab = dft_tables(length)

    taps_sel = lax.dynamic_index_in_dim(
        taps.reshape(3, 3, seq_n, per), me, axis=2, keepdims=False
    ).reshape(3, 3 * per)
    skip1 = lax.dynamic_index_in_dim(skip_one.reshape(seq_n, per), me, axis=0, keepdims=False)
    skip2 = lax.dynamic_index_in_dim(skip_two.reshape(seq_n, per), me, axis=0, keepdims=False)
    skip1 = skip1[None, :, None]
    skip2 = skip2[None, :, None]

    proj_blk = jnp.einsum("td,dc->ct", series[0], w_in, preferred_element_type=jnp.float32)
    proj_blk = jnp.swapaxes(proj_blk.reshape(3, seq_n, per, block), 0, 1).reshape(seq_n, 3 * per, block)
    dprod_blk = jnp.einsum("td,cd->ct", cotangent[0], w_out, preferred_element_type=jnp.float32)
    dprod_blk = dprod_blk.reshape(seq_n, per, block)
    rows_sent = jnp.repeat(jnp.swapaxes(jnp.stack([filter_one, filter_two]), 0, 1), per_group, axis=0)
    got = lax.all_to_all(
        jnp.concatenate([proj_blk, dprod_blk, rows_sent], axis=1), "seq", 0, 0, tiled=True
    )
    proj = jnp.swapaxes(got[:, : 3 * per], 0, 1).reshape(3 * per, length)
    d_product = jnp.swapaxes(
        got[:, 3 * per : 4 * per].reshape(seq_n, per, block // LANES, LANES), 1, 2
    ).reshape(half, per, LANES)
    h_rows = jnp.swapaxes(got[:, 4 * per :], 0, 1).reshape(2, length)
    prev1 = jnp.pad(proj, ((0, 0), (1, 0)))[:, :length]
    prev2 = jnp.pad(proj, ((0, 0), (2, 0)))[:, :length]
    conv = taps_sel[0][:, None] * proj + taps_sel[1][:, None] * prev1 + taps_sel[2][:, None] * prev2
    conv_f = fold(conv)
    value = conv_f[:, :per]
    gate_one = conv_f[:, per : 2 * per]
    gate_two = conv_f[:, 2 * per :]

    h_spec = spectrum(fold(h_rows), tab)
    h_one = h_spec[:, 0:1]
    h_two = h_spec[:, 1:2]

    v_spec = spectrum(value, tab)
    y_one = signal(cmul(v_spec, h_one), tab) + skip1 * value
    gated_mid = gate_one * y_one
    m_spec = spectrum(gated_mid, tab)
    y_two = signal(cmul(m_spec, h_two), tab) + skip2 * gated_mid
    product = (gate_two * y_two).astype(jnp.bfloat16)

    grad_two = d_product * gate_two
    d_gate_two = d_product * y_two
    g2_spec = spectrum(grad_two, tab)
    d_mid = signal(cmul(g2_spec, h_two, conj=True), tab) + skip2 * grad_two
    grad_one = d_mid * gate_one
    d_gate_one = d_mid * y_one
    g1_spec = spectrum(grad_one, tab)
    d_value = signal(cmul(g1_spec, h_one, conj=True), tab) + skip1 * grad_one

    corr = jnp.concatenate(
        [
            jnp.sum(cmul(g1_spec, v_spec, conj=True), axis=1, keepdims=True),
            jnp.sum(cmul(g2_spec, m_spec, conj=True), axis=1, keepdims=True),
        ],
        axis=1,
    )
    filt_grad = unfold(signal(corr, tab))

    d_conv = unfold(jnp.concatenate([d_value, d_gate_one, d_gate_two], axis=1))
    next1 = jnp.pad(d_conv, ((0, 0), (0, 1)))[:, 1:]
    next2 = jnp.pad(d_conv, ((0, 0), (0, 2)))[:, 2:]
    d_proj = (
        taps_sel[0][:, None] * d_conv + taps_sel[1][:, None] * next1 + taps_sel[2][:, None] * next2
    ).astype(jnp.bfloat16)

    local_taps = jnp.stack(
        [jnp.sum(d_conv * proj, axis=1), jnp.sum(d_conv * prev1, axis=1), jnp.sum(d_conv * prev2, axis=1)]
    )
    local_skip1 = jnp.sum(grad_one * value, axis=(0, 2))
    local_skip2 = jnp.sum(grad_two * gated_mid, axis=(0, 2))
    prod_sent = jnp.swapaxes(product.reshape(seq_n, half // seq_n, per, LANES), 1, 2)
    prod_sent = prod_sent.reshape(seq_n, per, block)
    dp_sent = jnp.swapaxes(d_proj.reshape(3 * per, seq_n, block), 0, 1)
    back = lax.all_to_all(jnp.concatenate([prod_sent, dp_sent], axis=1), "seq", 0, 0, tiled=True)
    prod_rows = jnp.transpose(back[:, :per], (2, 0, 1)).reshape(block, width)
    dp_rows = jnp.transpose(back[:, per:].reshape(seq_n, 3, per, block), (3, 1, 0, 2))
    dp_rows = dp_rows.reshape(block, 3 * width)
    output = jnp.dot(prod_rows, w_out, preferred_element_type=jnp.float32).astype(jnp.bfloat16)
    output = output.reshape(1, block, width)
    d_series = jnp.einsum(
        "tc,dc->td", dp_rows, w_in, preferred_element_type=jnp.float32
    ).astype(jnp.bfloat16)
    d_series = d_series.reshape(1, block, width)

    local_w_in = jnp.einsum("td,tc->dc", series[0], dp_rows, preferred_element_type=jnp.float32)
    local_w_out = jnp.einsum("tc,td->cd", prod_rows, cotangent[0], preferred_element_type=jnp.float32)
    small = jnp.concatenate(
        [
            local_taps.reshape(3, 3, 1, per),
            jnp.stack([local_skip1, local_skip2, jnp.zeros_like(local_skip1)]).reshape(3, 1, 1, per),
        ],
        axis=1,
    )
    small_full = lax.dynamic_update_slice(
        jnp.zeros((3, 4, seq_n, per), jnp.float32), small, (0, 0, me, 0)
    )
    params = jnp.concatenate([local_w_in.reshape(-1), local_w_out.reshape(-1), small_full.reshape(-1)])
    n_params = params.shape[0]
    chunk = -(-n_params // (seq_n * 8 * LANES)) * 8 * LANES
    params = jnp.pad(params, (0, chunk * seq_n - n_params)).reshape(seq_n, -1, LANES)
    fg_sent = jnp.swapaxes(filt_grad.reshape(2, seq_n, block), 0, 1).reshape(seq_n, -1, LANES)
    full, fg = reduce_rounds(jnp.concatenate([params, fg_sent], axis=1), params.shape[1], per_group, dp_n)
    fg_blocks = jnp.swapaxes(fg.reshape(filters, 2, block), 0, 1)
    full = full.reshape(-1)
    sizes = [width * 3 * width, width * width, 3 * 4 * width]
    offsets = np.cumsum([0] + sizes)
    grad_w_in = full[offsets[0] : offsets[1]].reshape(width, 3 * width)
    grad_w_out = full[offsets[1] : offsets[2]].reshape(width, width)
    small_full = full[offsets[2] : offsets[3]].reshape(3, 4, width)
    grad_taps = small_full[:, :3].reshape(3, 3 * width)
    grad_skip_one = small_full[0, 3]
    grad_skip_two = small_full[1, 3]

    return (
        output,
        d_series,
        grad_scale * grad_w_in,
        grad_scale * grad_w_out,
        grad_scale * grad_taps,
        grad_scale * grad_skip_one,
        grad_scale * grad_skip_two,
        grad_scale * fg_blocks[0],
        grad_scale * fg_blocks[1],
    )


def solution(mesh):
    in_specs = (
        P("dp", "seq", None),
        P("dp", "seq", None),
        P(),
        P(),
        P(),
        P(),
        P(),
        P(None, "seq"),
        P(None, "seq"),
    )
    out_specs = (
        P("dp", "seq", None),
        P("dp", "seq", None),
        P(),
        P(),
        P(),
        P(),
        P(),
        P(None, "seq"),
        P(None, "seq"),
    )
    return jax.shard_map(shards, mesh=mesh, in_specs=in_specs, out_specs=out_specs, check_vma=False)
```

```python
import math

import numpy as np

import jax
import jax.numpy as jnp
from jax import lax
from jax.experimental import pallas as pl
from jax.experimental.pallas import tpu as pltpu
from jax.sharding import PartitionSpec as P

PRECISION = lax.Precision.HIGH
LANES = 128


def dft_tables(length):
    size = 2 * length
    rows = size // LANES
    half = length // LANES
    k1 = np.arange(rows)
    f1 = np.exp(-2j * np.pi * (np.outer(k1, np.arange(half)) % rows) / rows)
    turn = np.exp(-2j * np.pi * np.outer(k1, np.arange(LANES)) / size)
    f2 = np.exp(-2j * np.pi * (np.outer(np.arange(LANES), np.arange(LANES)) % LANES) / LANES)
    fwd1 = np.concatenate([f1.real, f1.imag], axis=0)
    fwd2 = np.block([[f2.real, f2.imag], [-f2.imag, f2.real]])
    inv2 = np.block([[f2.real, -f2.imag], [f2.imag, f2.real]])
    inv1 = np.concatenate([f1.real.T, f1.imag.T], axis=1) / size
    as32 = lambda a: jnp.asarray(np.asarray(a, np.float32))
    return {
        "rows": rows,
        "fwd1": as32(fwd1),
        "fwd2": as32(fwd2),
        "inv1": as32(inv1),
        "inv2": as32(inv2),
        "turn_r": as32(turn.real)[:, None, :],
        "turn_i": as32(turn.imag)[:, None, :],
    }


def spectrum(x, tab):
    rows = tab["rows"]
    a = jnp.einsum("kn,ncm->kcm", tab["fwd1"], x, precision=PRECISION)
    ar, ai = a[:rows], a[rows:]
    tr, ti = tab["turn_r"], tab["turn_i"]
    cat = jnp.concatenate([ar * tr - ai * ti, ar * ti + ai * tr], axis=-1)
    return jnp.einsum("kcm,mj->kcj", cat, tab["fwd2"], precision=PRECISION)


def signal(s, tab):
    b = jnp.einsum("kcj,jm->kcm", s, tab["inv2"], precision=PRECISION)
    br, bi = b[..., :LANES], b[..., LANES:]
    tr, ti = tab["turn_r"], tab["turn_i"]
    stacked = jnp.concatenate([br * tr + bi * ti, bi * tr - br * ti], axis=0)
    return jnp.einsum("nk,kcm->ncm", tab["inv1"], stacked, precision=PRECISION)


def cmul(a, b, conj=False):
    ar, ai = a[..., :LANES], a[..., LANES:]
    br, bi = b[..., :LANES], b[..., LANES:]
    if conj:
        bi = -bi
    return jnp.concatenate([ar * br - ai * bi, ar * bi + ai * br], axis=-1)


def fold(x):
    c, length = x.shape
    return jnp.swapaxes(x.reshape(c, length // LANES, LANES), 0, 1)


def unfold(x):
    half, c, lanes = x.shape
    return jnp.swapaxes(x, 0, 1).reshape(c, half * lanes)


def exchange(x, axis, ident):
    n = x.shape[0]
    mesh_axes = ("dp", "seq")

    def where(p):
        return tuple(p if name == axis else lax.axis_index(name) for name in mesh_axes)

    def kernel(x_ref, y_ref, send_sem, recv_sem):
        me = lax.axis_index(axis)
        barrier = pltpu.get_barrier_semaphore()
        for k in range(1, n):
            pl.semaphore_signal(
                barrier, inc=1, device_id=where(lax.rem(me + k, n)),
                device_id_type=pl.DeviceIdType.MESH,
            )
        pl.semaphore_wait(barrier, n - 1)
        copies = []
        for k in range(1, n):
            p = lax.rem(me + k, n)
            copy = pltpu.make_async_remote_copy(
                src_ref=x_ref.at[p],
                dst_ref=y_ref.at[me],
                send_sem=send_sem.at[k],
                recv_sem=recv_sem.at[k],
                device_id=where(p),
                device_id_type=pl.DeviceIdType.MESH,
            )
            copy.start()
            copies.append(copy)
        y_ref[pl.ds(me, 1)] = x_ref[pl.ds(me, 1)]
        for copy in copies:
            copy.wait()

    return pl.pallas_call(
        kernel,
        out_shape=jax.ShapeDtypeStruct(x.shape, x.dtype),
        in_specs=[pl.BlockSpec(memory_space=pltpu.VMEM)],
        out_specs=pl.BlockSpec(memory_space=pltpu.VMEM),
        scratch_shapes=[pltpu.SemaphoreType.DMA((n,)), pltpu.SemaphoreType.DMA((n,))],
        compiler_params=pltpu.CompilerParams(collective_id=ident, has_side_effects=True),
    )(x)


def swap_blocks(x, axis, ident):
    shape = x.shape
    flat = x.reshape(shape[0], -1, LANES)
    return exchange(flat, axis, ident).reshape(shape)


def reduce_rounds(msg, param_rows, pair, dp_n):
    seq_n, msg_rows, lanes = msg.shape
    filter_rows = msg_rows - param_rows
    groups = seq_n // pair
    mesh = pl.DeviceIdType.MESH

    def kernel(msg_ref, full_ref, fg_ref, rs_buf, ag_buf, sems):
        ms = lax.axis_index("seq")
        md = lax.axis_index("dp")
        barrier = pltpu.get_barrier_semaphore()
        for k in range(1, seq_n):
            pl.semaphore_signal(barrier, inc=1, device_id=(md, lax.rem(ms + k, seq_n)), device_id_type=mesh)
        for k in range(1, dp_n):
            pl.semaphore_signal(barrier, inc=1, device_id=(lax.rem(md + k, dp_n), ms), device_id_type=mesh)
        pl.semaphore_wait(barrier, seq_n + dp_n - 2)

        def send_all(count, src, dst, stage, where):
            copies = []
            for k in range(1, count):
                copy = pltpu.make_async_remote_copy(
                    src_ref=src(k), dst_ref=dst, send_sem=sems.at[stage, 0, k],
                    recv_sem=sems.at[stage, 1, k], device_id=where(k), device_id_type=mesh,
                )
                copy.start()
                copies.append(copy)
            return copies

        seq_peer = lambda k: (md, lax.rem(ms + k, seq_n))
        dp_peer = lambda k: (lax.rem(md + k, dp_n), ms)

        copies = send_all(seq_n, lambda k: msg_ref.at[lax.rem(ms + k, seq_n)], rs_buf.at[ms], 0, seq_peer)
        rs_buf[pl.ds(ms, 1)] = msg_ref[pl.ds(ms, 1)]
        for copy in copies:
            copy.wait()
        got = rs_buf[...]
        p_sum = jnp.sum(got[:, :param_rows], axis=0)
        f_sum = jnp.sum(got[:, param_rows:].reshape(groups, pair, filter_rows, lanes), axis=1)
        mine = jnp.concatenate([p_sum, f_sum.reshape(groups * filter_rows, lanes)], axis=0)

        ag_buf[pl.ds(md, 1)] = mine[None]
        copies = send_all(dp_n, lambda k: ag_buf.at[md], ag_buf.at[md], 1, dp_peer)
        for copy in copies:
            copy.wait()
        total = jnp.sum(ag_buf[...], axis=0)
        fg_ref[...] = total[param_rows:].reshape(groups, filter_rows, lanes)

        full_ref[pl.ds(ms, 1)] = total[:param_rows][None]
        copies = send_all(seq_n, lambda k: full_ref.at[ms], full_ref.at[ms], 2, seq_peer)
        for copy in copies:
            copy.wait()

    ag_rows = param_rows + groups * filter_rows
    return pl.pallas_call(
        kernel,
        out_shape=(
            jax.ShapeDtypeStruct((seq_n, param_rows, lanes), msg.dtype),
            jax.ShapeDtypeStruct((groups, filter_rows, lanes), msg.dtype),
        ),
        in_specs=[pl.BlockSpec(memory_space=pltpu.VMEM)],
        out_specs=(pl.BlockSpec(memory_space=pltpu.VMEM), pl.BlockSpec(memory_space=pltpu.VMEM)),
        scratch_shapes=[
            pltpu.VMEM((seq_n, msg_rows, lanes), msg.dtype),
            pltpu.VMEM((dp_n, ag_rows, lanes), msg.dtype),
            pltpu.SemaphoreType.DMA((3, 2, max(seq_n, dp_n))),
        ],
        compiler_params=pltpu.CompilerParams(collective_id=0, has_side_effects=True),
    )(msg)


def shards(series, cotangent, w_in, w_out, taps, skip_one, skip_two, filter_one, filter_two):
    _, block, width = series.shape
    seq_n = lax.axis_size("seq")
    dp_n = lax.axis_size("dp")
    length = block * seq_n
    half = length // LANES
    me = lax.axis_index("seq")
    per = width // seq_n
    filters = filter_one.shape[0]
    group_width = width // filters
    per_group = group_width // per
    group = me // per_group
    grad_scale = 1.0 / math.sqrt(dp_n * series.shape[0] * length)
    tab = dft_tables(length)

    taps_sel = lax.dynamic_index_in_dim(
        taps.reshape(3, 3, seq_n, per), me, axis=2, keepdims=False
    ).reshape(3, 3 * per)
    skip1 = lax.dynamic_index_in_dim(skip_one.reshape(seq_n, per), me, axis=0, keepdims=False)
    skip2 = lax.dynamic_index_in_dim(skip_two.reshape(seq_n, per), me, axis=0, keepdims=False)
    skip1 = skip1[None, :, None]
    skip2 = skip2[None, :, None]

    proj_blk = jnp.einsum("td,dc->ct", series[0], w_in, preferred_element_type=jnp.float32)
    proj_blk = jnp.swapaxes(proj_blk.reshape(3, seq_n, per, block), 0, 1).reshape(seq_n, 3 * per, block)
    dprod_blk = jnp.einsum("td,cd->ct", cotangent[0], w_out, preferred_element_type=jnp.float32)
    dprod_blk = dprod_blk.reshape(seq_n, per, block)
    rows_sent = jnp.repeat(jnp.swapaxes(jnp.stack([filter_one, filter_two]), 0, 1), per_group, axis=0)
    got = swap_blocks(jnp.concatenate([proj_blk, dprod_blk, rows_sent], axis=1), "seq", 1)
    proj = jnp.swapaxes(got[:, : 3 * per], 0, 1).reshape(3 * per, length)
    d_product = jnp.swapaxes(
        got[:, 3 * per : 4 * per].reshape(seq_n, per, block // LANES, LANES), 1, 2
    ).reshape(half, per, LANES)
    h_rows = jnp.swapaxes(got[:, 4 * per :], 0, 1).reshape(2, length)
    prev1 = jnp.pad(proj, ((0, 0), (1, 0)))[:, :length]
    prev2 = jnp.pad(proj, ((0, 0), (2, 0)))[:, :length]
    conv = taps_sel[0][:, None] * proj + taps_sel[1][:, None] * prev1 + taps_sel[2][:, None] * prev2
    conv_f = fold(conv)
    value = conv_f[:, :per]
    gate_one = conv_f[:, per : 2 * per]
    gate_two = conv_f[:, 2 * per :]

    h_spec = spectrum(fold(h_rows), tab)
    h_one = h_spec[:, 0:1]
    h_two = h_spec[:, 1:2]

    v_spec = spectrum(value, tab)
    y_one = signal(cmul(v_spec, h_one), tab) + skip1 * value
    gated_mid = gate_one * y_one
    m_spec = spectrum(gated_mid, tab)
    y_two = signal(cmul(m_spec, h_two), tab) + skip2 * gated_mid
    product = (gate_two * y_two).astype(jnp.bfloat16)

    grad_two = d_product * gate_two
    d_gate_two = d_product * y_two
    g2_spec = spectrum(grad_two, tab)
    d_mid = signal(cmul(g2_spec, h_two, conj=True), tab) + skip2 * grad_two
    grad_one = d_mid * gate_one
    d_gate_one = d_mid * y_one
    g1_spec = spectrum(grad_one, tab)
    d_value = signal(cmul(g1_spec, h_one, conj=True), tab) + skip1 * grad_one

    corr = jnp.concatenate(
        [
            jnp.sum(cmul(g1_spec, v_spec, conj=True), axis=1, keepdims=True),
            jnp.sum(cmul(g2_spec, m_spec, conj=True), axis=1, keepdims=True),
        ],
        axis=1,
    )
    filt_grad = unfold(signal(corr, tab))

    d_conv = unfold(jnp.concatenate([d_value, d_gate_one, d_gate_two], axis=1))
    next1 = jnp.pad(d_conv, ((0, 0), (0, 1)))[:, 1:]
    next2 = jnp.pad(d_conv, ((0, 0), (0, 2)))[:, 2:]
    d_proj = (
        taps_sel[0][:, None] * d_conv + taps_sel[1][:, None] * next1 + taps_sel[2][:, None] * next2
    ).astype(jnp.bfloat16)

    local_taps = jnp.stack(
        [jnp.sum(d_conv * proj, axis=1), jnp.sum(d_conv * prev1, axis=1), jnp.sum(d_conv * prev2, axis=1)]
    )
    local_skip1 = jnp.sum(grad_one * value, axis=(0, 2))
    local_skip2 = jnp.sum(grad_two * gated_mid, axis=(0, 2))
    prod_sent = jnp.swapaxes(product.reshape(seq_n, half // seq_n, per, LANES), 1, 2)
    prod_sent = prod_sent.reshape(seq_n, per, block)
    dp_sent = jnp.swapaxes(d_proj.reshape(3 * per, seq_n, block), 0, 1)
    back = swap_blocks(jnp.concatenate([prod_sent, dp_sent], axis=1), "seq", 2)
    prod_rows = jnp.transpose(back[:, :per], (2, 0, 1)).reshape(block, width)
    dp_rows = jnp.transpose(back[:, per:].reshape(seq_n, 3, per, block), (3, 1, 0, 2))
    dp_rows = dp_rows.reshape(block, 3 * width)
    output = jnp.dot(prod_rows, w_out, preferred_element_type=jnp.float32).astype(jnp.bfloat16)
    output = output.reshape(1, block, width)
    d_series = jnp.einsum(
        "tc,dc->td", dp_rows, w_in, preferred_element_type=jnp.float32
    ).astype(jnp.bfloat16)
    d_series = d_series.reshape(1, block, width)

    local_w_in = jnp.einsum("td,tc->dc", series[0], dp_rows, preferred_element_type=jnp.float32)
    local_w_out = jnp.einsum("tc,td->cd", prod_rows, cotangent[0], preferred_element_type=jnp.float32)
    small = jnp.concatenate(
        [
            local_taps.reshape(3, 3, 1, per),
            jnp.stack([local_skip1, local_skip2, jnp.zeros_like(local_skip1)]).reshape(3, 1, 1, per),
        ],
        axis=1,
    )
    small_full = lax.dynamic_update_slice(
        jnp.zeros((3, 4, seq_n, per), jnp.float32), small, (0, 0, me, 0)
    )
    params = jnp.concatenate([local_w_in.reshape(-1), local_w_out.reshape(-1), small_full.reshape(-1)])
    n_params = params.shape[0]
    chunk = -(-n_params // (seq_n * 8 * LANES)) * 8 * LANES
    params = jnp.pad(params, (0, chunk * seq_n - n_params)).reshape(seq_n, -1, LANES)
    fg_sent = jnp.swapaxes(filt_grad.reshape(2, seq_n, block), 0, 1).reshape(seq_n, -1, LANES)
    full, fg = reduce_rounds(jnp.concatenate([params, fg_sent], axis=1), params.shape[1], per_group, dp_n)
    fg_blocks = jnp.swapaxes(fg.reshape(filters, 2, block), 0, 1)
    full = full.reshape(-1)
    sizes = [width * 3 * width, width * width, 3 * 4 * width]
    offsets = np.cumsum([0] + sizes)
    grad_w_in = full[offsets[0] : offsets[1]].reshape(width, 3 * width)
    grad_w_out = full[offsets[1] : offsets[2]].reshape(width, width)
    small_full = full[offsets[2] : offsets[3]].reshape(3, 4, width)
    grad_taps = small_full[:, :3].reshape(3, 3 * width)
    grad_skip_one = small_full[0, 3]
    grad_skip_two = small_full[1, 3]

    return (
        output,
        d_series,
        grad_scale * grad_w_in,
        grad_scale * grad_w_out,
        grad_scale * grad_taps,
        grad_scale * grad_skip_one,
        grad_scale * grad_skip_two,
        grad_scale * fg_blocks[0],
        grad_scale * fg_blocks[1],
    )


def solution(mesh):
    in_specs = (
        P("dp", "seq", None),
        P("dp", "seq", None),
        P(),
        P(),
        P(),
        P(),
        P(),
        P(None, "seq"),
        P(None, "seq"),
    )
    out_specs = (
        P("dp", "seq", None),
        P("dp", "seq", None),
        P(),
        P(),
        P(),
        P(),
        P(),
        P(None, "seq"),
        P(None, "seq"),
    )
    return jax.shard_map(shards, mesh=mesh, in_specs=in_specs, out_specs=out_specs, check_vma=False)
```

```python
import math

import numpy as np

import jax
import jax.numpy as jnp
from jax import lax
from jax.experimental import pallas as pl
from jax.experimental.pallas import tpu as pltpu
from jax.sharding import PartitionSpec as P

PRECISION = lax.Precision.HIGH
LANES = 128


def dft_tables(length):
    size = 2 * length
    rows = size // LANES
    half = length // LANES
    k1 = np.arange(rows)
    f1 = np.exp(-2j * np.pi * (np.outer(k1, np.arange(half)) % rows) / rows)
    turn = np.exp(-2j * np.pi * np.outer(k1, np.arange(LANES)) / size)
    f2 = np.exp(-2j * np.pi * (np.outer(np.arange(LANES), np.arange(LANES)) % LANES) / LANES)
    fwd1 = np.concatenate([f1.real, f1.imag], axis=0)
    fwd2 = np.block([[f2.real, f2.imag], [-f2.imag, f2.real]])
    inv2 = np.block([[f2.real, -f2.imag], [f2.imag, f2.real]])
    inv1 = np.concatenate([f1.real.T, f1.imag.T], axis=1) / size
    as32 = lambda a: jnp.asarray(np.asarray(a, np.float32))
    return {
        "rows": rows,
        "fwd1": as32(fwd1),
        "fwd2": as32(fwd2),
        "inv1": as32(inv1),
        "inv2": as32(inv2),
        "turn_r": as32(turn.real)[:, None, :],
        "turn_i": as32(turn.imag)[:, None, :],
    }


def spectrum(x, tab):
    rows = tab["rows"]
    a = jnp.einsum("kn,ncm->kcm", tab["fwd1"], x, precision=PRECISION)
    ar, ai = a[:rows], a[rows:]
    tr, ti = tab["turn_r"], tab["turn_i"]
    cat = jnp.concatenate([ar * tr - ai * ti, ar * ti + ai * tr], axis=-1)
    return jnp.einsum("kcm,mj->kcj", cat, tab["fwd2"], precision=PRECISION)


def signal(s, tab):
    b = jnp.einsum("kcj,jm->kcm", s, tab["inv2"], precision=PRECISION)
    br, bi = b[..., :LANES], b[..., LANES:]
    tr, ti = tab["turn_r"], tab["turn_i"]
    stacked = jnp.concatenate([br * tr + bi * ti, bi * tr - br * ti], axis=0)
    return jnp.einsum("nk,kcm->ncm", tab["inv1"], stacked, precision=PRECISION)


def cmul(a, b, conj=False):
    ar, ai = a[..., :LANES], a[..., LANES:]
    br, bi = b[..., :LANES], b[..., LANES:]
    if conj:
        bi = -bi
    return jnp.concatenate([ar * br - ai * bi, ar * bi + ai * br], axis=-1)


def fold(x):
    c, length = x.shape
    return jnp.swapaxes(x.reshape(c, length // LANES, LANES), 0, 1)


def unfold(x):
    half, c, lanes = x.shape
    return jnp.swapaxes(x, 0, 1).reshape(c, half * lanes)


def reduce_rounds(msg, param_rows, pair, dp_n):
    seq_n, msg_rows, lanes = msg.shape
    filter_rows = msg_rows - param_rows
    groups = seq_n // pair
    mesh = pl.DeviceIdType.MESH

    def kernel(msg_ref, full_ref, fg_ref, rs_buf, ag_buf, sems):
        ms = lax.axis_index("seq")
        md = lax.axis_index("dp")
        barrier = pltpu.get_barrier_semaphore()
        for k in range(1, seq_n):
            pl.semaphore_signal(barrier, inc=1, device_id=(md, lax.rem(ms + k, seq_n)), device_id_type=mesh)
        for k in range(1, dp_n):
            pl.semaphore_signal(barrier, inc=1, device_id=(lax.rem(md + k, dp_n), ms), device_id_type=mesh)
        pl.semaphore_wait(barrier, seq_n + dp_n - 2)

        def send_all(count, src, dst, stage, where):
            copies = []
            for k in range(1, count):
                copy = pltpu.make_async_remote_copy(
                    src_ref=src(k), dst_ref=dst, send_sem=sems.at[stage, 0, k],
                    recv_sem=sems.at[stage, 1, k], device_id=where(k), device_id_type=mesh,
                )
                copy.start()
                copies.append(copy)
            return copies

        seq_peer = lambda k: (md, lax.rem(ms + k, seq_n))
        dp_peer = lambda k: (lax.rem(md + k, dp_n), ms)

        copies = send_all(seq_n, lambda k: msg_ref.at[lax.rem(ms + k, seq_n)], rs_buf.at[ms], 0, seq_peer)
        rs_buf[pl.ds(ms, 1)] = msg_ref[pl.ds(ms, 1)]
        for copy in copies:
            copy.wait()
        got = rs_buf[...]
        p_sum = jnp.sum(got[:, :param_rows], axis=0)
        f_sum = jnp.sum(got[:, param_rows:].reshape(groups, pair, filter_rows, lanes), axis=1)
        mine = jnp.concatenate([p_sum, f_sum.reshape(groups * filter_rows, lanes)], axis=0)

        ag_buf[pl.ds(md, 1)] = mine[None]
        copies = send_all(dp_n, lambda k: ag_buf.at[md], ag_buf.at[md], 1, dp_peer)
        for copy in copies:
            copy.wait()
        total = jnp.sum(ag_buf[...], axis=0)
        fg_ref[...] = total[param_rows:].reshape(groups, filter_rows, lanes)

        full_ref[pl.ds(ms, 1)] = total[:param_rows][None]
        copies = send_all(seq_n, lambda k: full_ref.at[ms], full_ref.at[ms], 2, seq_peer)
        for copy in copies:
            copy.wait()

    ag_rows = param_rows + groups * filter_rows
    return pl.pallas_call(
        kernel,
        out_shape=(
            jax.ShapeDtypeStruct((seq_n, param_rows, lanes), msg.dtype),
            jax.ShapeDtypeStruct((groups, filter_rows, lanes), msg.dtype),
        ),
        in_specs=[pl.BlockSpec(memory_space=pltpu.VMEM)],
        out_specs=(pl.BlockSpec(memory_space=pltpu.VMEM), pl.BlockSpec(memory_space=pltpu.VMEM)),
        scratch_shapes=[
            pltpu.VMEM((seq_n, msg_rows, lanes), msg.dtype),
            pltpu.VMEM((dp_n, ag_rows, lanes), msg.dtype),
            pltpu.SemaphoreType.DMA((3, 2, max(seq_n, dp_n))),
        ],
        compiler_params=pltpu.CompilerParams(collective_id=0, has_side_effects=True),
    )(msg)


def shards(series, cotangent, w_in, w_out, taps, skip_one, skip_two, filter_one, filter_two):
    _, block, width = series.shape
    seq_n = lax.axis_size("seq")
    dp_n = lax.axis_size("dp")
    length = block * seq_n
    half = length // LANES
    me = lax.axis_index("seq")
    per = width // seq_n
    filters = filter_one.shape[0]
    group_width = width // filters
    per_group = group_width // per
    group = me // per_group
    grad_scale = 1.0 / math.sqrt(dp_n * series.shape[0] * length)
    tab = dft_tables(length)

    taps_sel = lax.dynamic_index_in_dim(
        taps.reshape(3, 3, seq_n, per), me, axis=2, keepdims=False
    ).reshape(3, 3 * per)
    skip1 = lax.dynamic_index_in_dim(skip_one.reshape(seq_n, per), me, axis=0, keepdims=False)
    skip2 = lax.dynamic_index_in_dim(skip_two.reshape(seq_n, per), me, axis=0, keepdims=False)
    skip1 = skip1[None, :, None]
    skip2 = skip2[None, :, None]

    proj_blk = jnp.einsum("td,dc->ct", series[0], w_in, preferred_element_type=jnp.float32)
    proj_blk = jnp.swapaxes(proj_blk.reshape(3, seq_n, per, block), 0, 1).reshape(seq_n, 3 * per, block)
    dprod_blk = jnp.einsum("td,cd->ct", cotangent[0], w_out, preferred_element_type=jnp.float32)
    dprod_blk = dprod_blk.reshape(seq_n, per, block)
    rows_sent = jnp.repeat(jnp.swapaxes(jnp.stack([filter_one, filter_two]), 0, 1), per_group, axis=0)
    got = lax.all_to_all(
        jnp.concatenate([proj_blk, dprod_blk, rows_sent], axis=1), "seq", 0, 0, tiled=True
    )
    proj = jnp.swapaxes(got[:, : 3 * per], 0, 1).reshape(3 * per, length)
    d_product = jnp.swapaxes(
        got[:, 3 * per : 4 * per].reshape(seq_n, per, block // LANES, LANES), 1, 2
    ).reshape(half, per, LANES)
    h_rows = jnp.swapaxes(got[:, 4 * per :], 0, 1).reshape(2, length)
    prev1 = jnp.pad(proj, ((0, 0), (1, 0)))[:, :length]
    prev2 = jnp.pad(proj, ((0, 0), (2, 0)))[:, :length]
    conv = taps_sel[0][:, None] * proj + taps_sel[1][:, None] * prev1 + taps_sel[2][:, None] * prev2
    conv_f = fold(conv)
    value = conv_f[:, :per]
    gate_one = conv_f[:, per : 2 * per]
    gate_two = conv_f[:, 2 * per :]

    h_spec = spectrum(fold(h_rows), tab)
    h_one = h_spec[:, 0:1]
    h_two = h_spec[:, 1:2]

    v_spec = spectrum(value, tab)
    y_one = signal(cmul(v_spec, h_one), tab) + skip1 * value
    gated_mid = gate_one * y_one
    m_spec = spectrum(gated_mid, tab)
    y_two = signal(cmul(m_spec, h_two), tab) + skip2 * gated_mid
    product = (gate_two * y_two).astype(jnp.bfloat16)

    grad_two = d_product * gate_two
    d_gate_two = d_product * y_two
    g2_spec = spectrum(grad_two, tab)
    d_mid = signal(cmul(g2_spec, h_two, conj=True), tab) + skip2 * grad_two
    grad_one = d_mid * gate_one
    d_gate_one = d_mid * y_one
    g1_spec = spectrum(grad_one, tab)
    d_value = signal(cmul(g1_spec, h_one, conj=True), tab) + skip1 * grad_one

    corr = jnp.concatenate(
        [
            jnp.sum(cmul(g1_spec, v_spec, conj=True), axis=1, keepdims=True),
            jnp.sum(cmul(g2_spec, m_spec, conj=True), axis=1, keepdims=True),
        ],
        axis=1,
    )
    filt_grad = unfold(signal(corr, tab))

    d_conv = unfold(jnp.concatenate([d_value, d_gate_one, d_gate_two], axis=1))
    next1 = jnp.pad(d_conv, ((0, 0), (0, 1)))[:, 1:]
    next2 = jnp.pad(d_conv, ((0, 0), (0, 2)))[:, 2:]
    d_proj = (
        taps_sel[0][:, None] * d_conv + taps_sel[1][:, None] * next1 + taps_sel[2][:, None] * next2
    ).astype(jnp.bfloat16)

    local_taps = jnp.stack(
        [jnp.sum(d_conv * proj, axis=1), jnp.sum(d_conv * prev1, axis=1), jnp.sum(d_conv * prev2, axis=1)]
    )
    local_skip1 = jnp.sum(grad_one * value, axis=(0, 2))
    local_skip2 = jnp.sum(grad_two * gated_mid, axis=(0, 2))
    prod_sent = jnp.swapaxes(product.reshape(seq_n, half // seq_n, per, LANES), 1, 2)
    prod_sent = prod_sent.reshape(seq_n, per, block)
    dp_sent = jnp.swapaxes(d_proj.reshape(3 * per, seq_n, block), 0, 1)
    back = lax.all_to_all(jnp.concatenate([prod_sent, dp_sent], axis=1), "seq", 0, 0, tiled=True)
    prod_rows = jnp.transpose(back[:, :per], (2, 0, 1)).reshape(block, width)
    dp_rows = jnp.transpose(back[:, per:].reshape(seq_n, 3, per, block), (3, 1, 0, 2))
    dp_rows = dp_rows.reshape(block, 3 * width)
    output = jnp.dot(prod_rows, w_out, preferred_element_type=jnp.float32).astype(jnp.bfloat16)
    output = output.reshape(1, block, width)
    d_series = jnp.einsum(
        "tc,dc->td", dp_rows, w_in, preferred_element_type=jnp.float32
    ).astype(jnp.bfloat16)
    d_series = d_series.reshape(1, block, width)

    local_w_in = jnp.einsum("td,tc->dc", series[0], dp_rows, preferred_element_type=jnp.float32)
    local_w_out = jnp.einsum("tc,td->cd", prod_rows, cotangent[0], preferred_element_type=jnp.float32)
    small = jnp.concatenate(
        [
            local_taps.reshape(3, 3, 1, per),
            jnp.stack([local_skip1, local_skip2, jnp.zeros_like(local_skip1)]).reshape(3, 1, 1, per),
        ],
        axis=1,
    )
    small_full = lax.dynamic_update_slice(
        jnp.zeros((3, 4, seq_n, per), jnp.float32), small, (0, 0, me, 0)
    )
    params = grad_scale * jnp.concatenate(
        [local_w_in.reshape(-1), local_w_out.reshape(-1), small_full.reshape(-1)]
    )
    n_params = params.shape[0]
    chunk = -(-n_params // (seq_n * 8 * LANES)) * 8 * LANES
    params = jnp.pad(params, (0, chunk * seq_n - n_params)).reshape(seq_n, -1, LANES)
    fg_sent = jnp.swapaxes(grad_scale * filt_grad.reshape(2, seq_n, block), 0, 1)
    fg_sent = fg_sent.reshape(seq_n, -1, LANES)
    full, fg = reduce_rounds(jnp.concatenate([params, fg_sent], axis=1), params.shape[1], per_group, dp_n)
    fg_blocks = jnp.swapaxes(fg.reshape(filters, 2, block), 0, 1)
    full = full.reshape(-1)
    sizes = [width * 3 * width, width * width, 3 * 4 * width]
    offsets = np.cumsum([0] + sizes)
    grad_w_in = full[offsets[0] : offsets[1]].reshape(width, 3 * width)
    grad_w_out = full[offsets[1] : offsets[2]].reshape(width, width)
    small_full = full[offsets[2] : offsets[3]].reshape(3, 4, width)
    grad_taps = small_full[:, :3].reshape(3, 3 * width)
    grad_skip_one = small_full[0, 3]
    grad_skip_two = small_full[1, 3]

    return (
        output,
        d_series,
        grad_w_in,
        grad_w_out,
        grad_taps,
        grad_skip_one,
        grad_skip_two,
        fg_blocks[0],
        fg_blocks[1],
    )


def solution(mesh):
    in_specs = (
        P("dp", "seq", None),
        P("dp", "seq", None),
        P(),
        P(),
        P(),
        P(),
        P(),
        P(None, "seq"),
        P(None, "seq"),
    )
    out_specs = (
        P("dp", "seq", None),
        P("dp", "seq", None),
        P(),
        P(),
        P(),
        P(),
        P(),
        P(None, "seq"),
        P(None, "seq"),
    )
    return jax.shard_map(shards, mesh=mesh, in_specs=in_specs, out_specs=out_specs, check_vma=False)
```

```python
import math

import numpy as np

import jax
import jax.numpy as jnp
from jax import lax
from jax.experimental import pallas as pl
from jax.experimental.pallas import tpu as pltpu
from jax.sharding import PartitionSpec as P

PRECISION = lax.Precision.HIGH
LANES = 128


def dft_tables(length):
    size = 2 * length
    rows = size // LANES
    half = length // LANES
    k1 = np.arange(rows)
    f1 = np.exp(-2j * np.pi * (np.outer(k1, np.arange(half)) % rows) / rows)
    turn = np.exp(-2j * np.pi * np.outer(k1, np.arange(LANES)) / size)
    f2 = np.exp(-2j * np.pi * (np.outer(np.arange(LANES), np.arange(LANES)) % LANES) / LANES)
    fwd1 = np.concatenate([f1.real, f1.imag], axis=0)
    fwd2 = np.block([[f2.real, f2.imag], [-f2.imag, f2.real]])
    inv2 = np.block([[f2.real, -f2.imag], [f2.imag, f2.real]])
    inv1 = np.concatenate([f1.real.T, f1.imag.T], axis=1) / size
    as32 = lambda a: jnp.asarray(np.asarray(a, np.float32))
    return {
        "rows": rows,
        "fwd1": as32(fwd1),
        "fwd2": as32(fwd2),
        "inv1": as32(inv1),
        "inv2": as32(inv2),
        "turn_r": as32(turn.real)[:, None, :],
        "turn_i": as32(turn.imag)[:, None, :],
    }


def spectrum(x, tab):
    rows = tab["rows"]
    a = jnp.einsum("kn,ncm->kcm", tab["fwd1"], x, precision=PRECISION)
    ar, ai = a[:rows], a[rows:]
    tr, ti = tab["turn_r"], tab["turn_i"]
    cat = jnp.concatenate([ar * tr - ai * ti, ar * ti + ai * tr], axis=-1)
    return jnp.einsum("kcm,mj->kcj", cat, tab["fwd2"], precision=PRECISION)


def signal(s, tab):
    b = jnp.einsum("kcj,jm->kcm", s, tab["inv2"], precision=PRECISION)
    br, bi = b[..., :LANES], b[..., LANES:]
    tr, ti = tab["turn_r"], tab["turn_i"]
    stacked = jnp.concatenate([br * tr + bi * ti, bi * tr - br * ti], axis=0)
    return jnp.einsum("nk,kcm->ncm", tab["inv1"], stacked, precision=PRECISION)


def cmul(a, b, conj=False):
    ar, ai = a[..., :LANES], a[..., LANES:]
    br, bi = b[..., :LANES], b[..., LANES:]
    if conj:
        bi = -bi
    return jnp.concatenate([ar * br - ai * bi, ar * bi + ai * br], axis=-1)


def fold(x):
    c, length = x.shape
    return jnp.swapaxes(x.reshape(c, length // LANES, LANES), 0, 1)


def unfold(x):
    half, c, lanes = x.shape
    return jnp.swapaxes(x, 0, 1).reshape(c, half * lanes)


def tail_rounds(out_msg, series_blk, cot_blk, side, scale, pair, dp_n):
    seq_n, out_rows, block = out_msg.shape
    per = out_rows // 4
    width = series_blk.shape[1]
    side_rows = side.shape[1]
    filter_rows = side_rows // 2
    param_rows = 3 * per + per + filter_rows
    msg_rows = param_rows + filter_rows
    groups = seq_n // pair
    ag_rows = param_rows + groups * filter_rows
    mesh = pl.DeviceIdType.MESH

    def kernel(out_ref, ser_ref, cot_ref, side_ref, back_ref, full_ref, fg_ref,
               msg_buf, rs_buf, ag_buf, sems):
        ms = lax.axis_index("seq")
        md = lax.axis_index("dp")
        barrier = pltpu.get_barrier_semaphore()
        for k in range(1, seq_n):
            pl.semaphore_signal(barrier, inc=1, device_id=(md, lax.rem(ms + k, seq_n)), device_id_type=mesh)
        for k in range(1, dp_n):
            pl.semaphore_signal(barrier, inc=1, device_id=(lax.rem(md + k, dp_n), ms), device_id_type=mesh)
        pl.semaphore_wait(barrier, seq_n + dp_n - 2)

        def send_all(count, src, dst, stage, where):
            copies = []
            for k in range(1, count):
                copy = pltpu.make_async_remote_copy(
                    src_ref=src(k), dst_ref=dst, send_sem=sems.at[stage, 0, k],
                    recv_sem=sems.at[stage, 1, k], device_id=where(k), device_id_type=mesh,
                )
                copy.start()
                copies.append(copy)
            return copies

        seq_peer = lambda k: (md, lax.rem(ms + k, seq_n))
        dp_peer = lambda k: (lax.rem(md + k, dp_n), ms)

        copies = send_all(seq_n, lambda k: out_ref.at[lax.rem(ms + k, seq_n)], back_ref.at[ms], 3, seq_peer)
        back_ref[pl.ds(ms, 1)] = out_ref[pl.ds(ms, 1)]
        for copy in copies:
            copy.wait()
        ser = ser_ref[...].astype(jnp.float32)
        cot = cot_ref[...].astype(jnp.float32)
        for j in range(seq_n):
            rows = back_ref[j].astype(jnp.float32)
            msg_buf[j, : 3 * per] = scale * jnp.dot(rows[per:], ser, preferred_element_type=jnp.float32)
            msg_buf[j, 3 * per : 4 * per] = scale * jnp.dot(rows[:per], cot, preferred_element_type=jnp.float32)
        msg_buf[:, 4 * per :] = side_ref[...]

        copies = send_all(seq_n, lambda k: msg_buf.at[lax.rem(ms + k, seq_n)], rs_buf.at[ms], 0, seq_peer)
        rs_buf[pl.ds(ms, 1)] = msg_buf[pl.ds(ms, 1)]
        for copy in copies:
            copy.wait()
        got = rs_buf[...]
        p_sum = jnp.sum(got[:, :param_rows], axis=0)
        f_sum = jnp.sum(got[:, param_rows:].reshape(groups, pair, filter_rows, width), axis=1)
        mine = jnp.concatenate([p_sum, f_sum.reshape(groups * filter_rows, width)], axis=0)

        ag_buf[pl.ds(md, 1)] = mine[None]
        copies = send_all(dp_n, lambda k: ag_buf.at[md], ag_buf.at[md], 1, dp_peer)
        for copy in copies:
            copy.wait()
        total = jnp.sum(ag_buf[...], axis=0)
        fg_ref[...] = total[param_rows:].reshape(groups, filter_rows, width)

        full_ref[pl.ds(ms, 1)] = total[:param_rows][None]
        copies = send_all(seq_n, lambda k: full_ref.at[ms], full_ref.at[ms], 2, seq_peer)
        for copy in copies:
            copy.wait()

    vmem = pl.BlockSpec(memory_space=pltpu.VMEM)
    return pl.pallas_call(
        kernel,
        out_shape=(
            jax.ShapeDtypeStruct(out_msg.shape, out_msg.dtype),
            jax.ShapeDtypeStruct((seq_n, param_rows, width), jnp.float32),
            jax.ShapeDtypeStruct((groups, filter_rows, width), jnp.float32),
        ),
        in_specs=[vmem] * 4,
        out_specs=(vmem, vmem, vmem),
        scratch_shapes=[
            pltpu.VMEM((seq_n, msg_rows, width), jnp.float32),
            pltpu.VMEM((seq_n, msg_rows, width), jnp.float32),
            pltpu.VMEM((dp_n, ag_rows, width), jnp.float32),
            pltpu.SemaphoreType.DMA((4, 2, max(seq_n, dp_n))),
        ],
        compiler_params=pltpu.CompilerParams(collective_id=0, has_side_effects=True),
    )(out_msg, series_blk, cot_blk, side)


def shards(series, cotangent, w_in, w_out, taps, skip_one, skip_two, filter_one, filter_two):
    _, block, width = series.shape
    seq_n = lax.axis_size("seq")
    dp_n = lax.axis_size("dp")
    length = block * seq_n
    half = length // LANES
    me = lax.axis_index("seq")
    per = width // seq_n
    filters = filter_one.shape[0]
    group_width = width // filters
    per_group = group_width // per
    group = me // per_group
    grad_scale = 1.0 / math.sqrt(dp_n * series.shape[0] * length)
    tab = dft_tables(length)

    taps_sel = lax.dynamic_index_in_dim(
        taps.reshape(3, 3, seq_n, per), me, axis=2, keepdims=False
    ).reshape(3, 3 * per)
    skip1 = lax.dynamic_index_in_dim(skip_one.reshape(seq_n, per), me, axis=0, keepdims=False)
    skip2 = lax.dynamic_index_in_dim(skip_two.reshape(seq_n, per), me, axis=0, keepdims=False)
    skip1 = skip1[None, :, None]
    skip2 = skip2[None, :, None]

    proj_blk = jnp.einsum("td,dc->ct", series[0], w_in, preferred_element_type=jnp.float32)
    proj_blk = jnp.swapaxes(proj_blk.reshape(3, seq_n, per, block), 0, 1).reshape(seq_n, 3 * per, block)
    dprod_blk = jnp.einsum("td,cd->ct", cotangent[0], w_out, preferred_element_type=jnp.float32)
    dprod_blk = dprod_blk.reshape(seq_n, per, block)
    rows_sent = jnp.repeat(jnp.swapaxes(jnp.stack([filter_one, filter_two]), 0, 1), per_group, axis=0)
    got = lax.all_to_all(
        jnp.concatenate([proj_blk, dprod_blk, rows_sent], axis=1), "seq", 0, 0, tiled=True
    )
    proj = jnp.swapaxes(got[:, : 3 * per], 0, 1).reshape(3 * per, length)
    d_product = jnp.swapaxes(
        got[:, 3 * per : 4 * per].reshape(seq_n, per, block // LANES, LANES), 1, 2
    ).reshape(half, per, LANES)
    h_rows = jnp.swapaxes(got[:, 4 * per :], 0, 1).reshape(2, length)
    prev1 = jnp.pad(proj, ((0, 0), (1, 0)))[:, :length]
    prev2 = jnp.pad(proj, ((0, 0), (2, 0)))[:, :length]
    conv = taps_sel[0][:, None] * proj + taps_sel[1][:, None] * prev1 + taps_sel[2][:, None] * prev2
    conv_f = fold(conv)
    value = conv_f[:, :per]
    gate_one = conv_f[:, per : 2 * per]
    gate_two = conv_f[:, 2 * per :]

    h_spec = spectrum(fold(h_rows), tab)
    h_one = h_spec[:, 0:1]
    h_two = h_spec[:, 1:2]

    v_spec = spectrum(value, tab)
    y_one = signal(cmul(v_spec, h_one), tab) + skip1 * value
    gated_mid = gate_one * y_one
    m_spec = spectrum(gated_mid, tab)
    y_two = signal(cmul(m_spec, h_two), tab) + skip2 * gated_mid
    product = (gate_two * y_two).astype(jnp.bfloat16)

    grad_two = d_product * gate_two
    d_gate_two = d_product * y_two
    g2_spec = spectrum(grad_two, tab)
    d_mid = signal(cmul(g2_spec, h_two, conj=True), tab) + skip2 * grad_two
    grad_one = d_mid * gate_one
    d_gate_one = d_mid * y_one
    g1_spec = spectrum(grad_one, tab)
    d_value = signal(cmul(g1_spec, h_one, conj=True), tab) + skip1 * grad_one

    corr = jnp.concatenate(
        [
            jnp.sum(cmul(g1_spec, v_spec, conj=True), axis=1, keepdims=True),
            jnp.sum(cmul(g2_spec, m_spec, conj=True), axis=1, keepdims=True),
        ],
        axis=1,
    )
    filt_grad = unfold(signal(corr, tab))

    d_conv = unfold(jnp.concatenate([d_value, d_gate_one, d_gate_two], axis=1))
    next1 = jnp.pad(d_conv, ((0, 0), (0, 1)))[:, 1:]
    next2 = jnp.pad(d_conv, ((0, 0), (0, 2)))[:, 2:]
    d_proj = (
        taps_sel[0][:, None] * d_conv + taps_sel[1][:, None] * next1 + taps_sel[2][:, None] * next2
    ).astype(jnp.bfloat16)

    local_taps = jnp.stack(
        [jnp.sum(d_conv * proj, axis=1), jnp.sum(d_conv * prev1, axis=1), jnp.sum(d_conv * prev2, axis=1)]
    )
    local_skip1 = jnp.sum(grad_one * value, axis=(0, 2))
    local_skip2 = jnp.sum(grad_two * gated_mid, axis=(0, 2))
    prod_sent = jnp.swapaxes(product.reshape(seq_n, half // seq_n, per, LANES), 1, 2)
    prod_sent = prod_sent.reshape(seq_n, per, block)
    dp_sent = jnp.swapaxes(d_proj.reshape(3 * per, seq_n, block), 0, 1)
    small = jnp.concatenate(
        [
            local_taps.reshape(3, 3, 1, per),
            jnp.stack([local_skip1, local_skip2, jnp.zeros_like(local_skip1)]).reshape(3, 1, 1, per),
        ],
        axis=1,
    )
    small_full = lax.dynamic_update_slice(
        jnp.zeros((3, 4, seq_n, per), jnp.float32), small, (0, 0, me, 0)
    )
    small_sent = jnp.transpose(grad_scale * small_full, (2, 0, 1, 3)).reshape(seq_n, -1)
    small_sent = jnp.pad(small_sent, ((0, 0), (0, 2 * block - small_sent.shape[1])))
    fg_sent = jnp.swapaxes(grad_scale * filt_grad.reshape(2, seq_n, block), 0, 1)
    side = jnp.concatenate([small_sent, fg_sent.reshape(seq_n, -1)], axis=1).reshape(seq_n, -1, LANES)
    back, full, fg = tail_rounds(
        jnp.concatenate([prod_sent, dp_sent], axis=1), series[0], cotangent[0], side,
        grad_scale, per_group, dp_n,
    )
    prod_rows = jnp.transpose(back[:, :per], (2, 0, 1)).reshape(block, width)
    dp_rows = jnp.transpose(back[:, per:].reshape(seq_n, 3, per, block), (3, 1, 0, 2))
    dp_rows = dp_rows.reshape(block, 3 * width)
    output = jnp.dot(prod_rows, w_out, preferred_element_type=jnp.float32).astype(jnp.bfloat16)
    output = output.reshape(1, block, width)
    d_series = jnp.einsum(
        "tc,dc->td", dp_rows, w_in, preferred_element_type=jnp.float32
    ).astype(jnp.bfloat16)
    d_series = d_series.reshape(1, block, width)

    fg_blocks = jnp.swapaxes(fg.reshape(filters, 2, block), 0, 1)
    grad_w_in = jnp.transpose(full[:, : 3 * per].reshape(seq_n, 3, per, width), (3, 1, 0, 2))
    grad_w_in = grad_w_in.reshape(width, 3 * width)
    grad_w_out = full[:, 3 * per : 4 * per].reshape(width, width)
    small_all = full[:, 4 * per :].reshape(seq_n, -1)[:, : 3 * 4 * per].reshape(seq_n, 3, 4, per)
    small_all = jnp.transpose(small_all, (1, 2, 0, 3)).reshape(3, 4, width)
    grad_taps = small_all[:, :3].reshape(3, 3 * width)
    grad_skip_one = small_all[0, 3]
    grad_skip_two = small_all[1, 3]

    return (
        output,
        d_series,
        grad_w_in,
        grad_w_out,
        grad_taps,
        grad_skip_one,
        grad_skip_two,
        fg_blocks[0],
        fg_blocks[1],
    )


def solution(mesh):
    in_specs = (
        P("dp", "seq", None),
        P("dp", "seq", None),
        P(),
        P(),
        P(),
        P(),
        P(),
        P(None, "seq"),
        P(None, "seq"),
    )
    out_specs = (
        P("dp", "seq", None),
        P("dp", "seq", None),
        P(),
        P(),
        P(),
        P(),
        P(),
        P(None, "seq"),
        P(None, "seq"),
    )
    return jax.shard_map(shards, mesh=mesh, in_specs=in_specs, out_specs=out_specs, check_vma=False)
```

```python
import math

import numpy as np

import jax
import jax.numpy as jnp
from jax import lax
from jax.experimental import pallas as pl
from jax.experimental.pallas import tpu as pltpu
from jax.sharding import PartitionSpec as P

PRECISION = lax.Precision.HIGH
LANES = 128


def dft_tables(length):
    size = 2 * length
    rows = size // LANES
    half = length // LANES
    k1 = np.arange(rows)
    f1 = np.exp(-2j * np.pi * (np.outer(k1, np.arange(half)) % rows) / rows)
    turn = np.exp(-2j * np.pi * np.outer(k1, np.arange(LANES)) / size)
    f2 = np.exp(-2j * np.pi * (np.outer(np.arange(LANES), np.arange(LANES)) % LANES) / LANES)
    fwd1 = np.concatenate([f1.real, f1.imag], axis=0)
    fwd2 = np.block([[f2.real, f2.imag], [-f2.imag, f2.real]])
    inv2 = np.block([[f2.real, -f2.imag], [f2.imag, f2.real]])
    inv1 = np.concatenate([f1.real.T, f1.imag.T], axis=1) / size
    as32 = lambda a: jnp.asarray(np.asarray(a, np.float32))
    return {
        "rows": rows,
        "fwd1": as32(fwd1),
        "fwd2": as32(fwd2),
        "inv1": as32(inv1),
        "inv2": as32(inv2),
        "turn_r": as32(turn.real)[:, None, :],
        "turn_i": as32(turn.imag)[:, None, :],
    }


def spectrum(x, tab):
    rows = tab["rows"]
    a = jnp.einsum("kn,ncm->kcm", tab["fwd1"], x, precision=PRECISION)
    ar, ai = a[:rows], a[rows:]
    tr, ti = tab["turn_r"], tab["turn_i"]
    cat = jnp.concatenate([ar * tr - ai * ti, ar * ti + ai * tr], axis=-1)
    return jnp.einsum("kcm,mj->kcj", cat, tab["fwd2"], precision=PRECISION)


def signal(s, tab):
    b = jnp.einsum("kcj,jm->kcm", s, tab["inv2"], precision=PRECISION)
    br, bi = b[..., :LANES], b[..., LANES:]
    tr, ti = tab["turn_r"], tab["turn_i"]
    stacked = jnp.concatenate([br * tr + bi * ti, bi * tr - br * ti], axis=0)
    return jnp.einsum("nk,kcm->ncm", tab["inv1"], stacked, precision=PRECISION)


def cmul(a, b, conj=False):
    ar, ai = a[..., :LANES], a[..., LANES:]
    br, bi = b[..., :LANES], b[..., LANES:]
    if conj:
        bi = -bi
    return jnp.concatenate([ar * br - ai * bi, ar * bi + ai * br], axis=-1)


def fold(x):
    c, length = x.shape
    return jnp.swapaxes(x.reshape(c, length // LANES, LANES), 0, 1)


def unfold(x):
    half, c, lanes = x.shape
    return jnp.swapaxes(x, 0, 1).reshape(c, half * lanes)


def exchange(x, axis, ident):
    n = x.shape[0]
    mesh_axes = ("dp", "seq")

    def where(p):
        return tuple(p if name == axis else lax.axis_index(name) for name in mesh_axes)

    def kernel(x_ref, y_ref, send_sem, recv_sem):
        me = lax.axis_index(axis)
        barrier = pltpu.get_barrier_semaphore()
        for k in range(1, n):
            pl.semaphore_signal(
                barrier, inc=1, device_id=where(lax.rem(me + k, n)),
                device_id_type=pl.DeviceIdType.MESH,
            )
        pl.semaphore_wait(barrier, n - 1)
        copies = []
        for k in range(1, n):
            p = lax.rem(me + k, n)
            copy = pltpu.make_async_remote_copy(
                src_ref=x_ref.at[p],
                dst_ref=y_ref.at[me],
                send_sem=send_sem.at[k],
                recv_sem=recv_sem.at[k],
                device_id=where(p),
                device_id_type=pl.DeviceIdType.MESH,
            )
            copy.start()
            copies.append(copy)
        y_ref[pl.ds(me, 1)] = x_ref[pl.ds(me, 1)]
        for copy in copies:
            copy.wait()

    return pl.pallas_call(
        kernel,
        out_shape=jax.ShapeDtypeStruct(x.shape, x.dtype),
        in_specs=[pl.BlockSpec(memory_space=pltpu.VMEM)],
        out_specs=pl.BlockSpec(memory_space=pltpu.VMEM),
        scratch_shapes=[pltpu.SemaphoreType.DMA((n,)), pltpu.SemaphoreType.DMA((n,))],
        compiler_params=pltpu.CompilerParams(collective_id=ident, has_side_effects=True),
    )(x)


def swap_blocks(x, axis, ident):
    shape = x.shape
    flat = x.reshape(shape[0], -1, LANES)
    return exchange(flat, axis, ident).reshape(shape)


def tail_rounds(out_msg, series_blk, cot_blk, side, scale, pair, dp_n):
    seq_n, out_rows, block = out_msg.shape
    per = out_rows // 4
    width = series_blk.shape[1]
    side_rows = side.shape[1]
    filter_rows = side_rows // 2
    param_rows = 3 * per + per + filter_rows
    msg_rows = param_rows + filter_rows
    groups = seq_n // pair
    ag_rows = param_rows + groups * filter_rows
    mesh = pl.DeviceIdType.MESH

    def kernel(out_ref, ser_ref, cot_ref, side_ref, back_ref, full_ref, fg_ref,
               msg_buf, rs_buf, ag_buf, sems):
        ms = lax.axis_index("seq")
        md = lax.axis_index("dp")
        barrier = pltpu.get_barrier_semaphore()
        for k in range(1, seq_n):
            pl.semaphore_signal(barrier, inc=1, device_id=(md, lax.rem(ms + k, seq_n)), device_id_type=mesh)
        for k in range(1, dp_n):
            pl.semaphore_signal(barrier, inc=1, device_id=(lax.rem(md + k, dp_n), ms), device_id_type=mesh)
        pl.semaphore_wait(barrier, seq_n + dp_n - 2)

        def send_all(count, src, dst, stage, where):
            copies = []
            for k in range(1, count):
                copy = pltpu.make_async_remote_copy(
                    src_ref=src(k), dst_ref=dst, send_sem=sems.at[stage, 0, k],
                    recv_sem=sems.at[stage, 1, k], device_id=where(k), device_id_type=mesh,
                )
                copy.start()
                copies.append(copy)
            return copies

        seq_peer = lambda k: (md, lax.rem(ms + k, seq_n))
        dp_peer = lambda k: (lax.rem(md + k, dp_n), ms)

        copies = send_all(seq_n, lambda k: out_ref.at[lax.rem(ms + k, seq_n)], back_ref.at[ms], 3, seq_peer)
        back_ref[pl.ds(ms, 1)] = out_ref[pl.ds(ms, 1)]
        for copy in copies:
            copy.wait()
        ser = ser_ref[...].astype(jnp.float32)
        cot = cot_ref[...].astype(jnp.float32)
        for j in range(seq_n):
            rows = back_ref[j].astype(jnp.float32)
            msg_buf[j, : 3 * per] = scale * jnp.dot(rows[per:], ser, preferred_element_type=jnp.float32)
            msg_buf[j, 3 * per : 4 * per] = scale * jnp.dot(rows[:per], cot, preferred_element_type=jnp.float32)
        msg_buf[:, 4 * per :] = side_ref[...]

        copies = send_all(seq_n, lambda k: msg_buf.at[lax.rem(ms + k, seq_n)], rs_buf.at[ms], 0, seq_peer)
        rs_buf[pl.ds(ms, 1)] = msg_buf[pl.ds(ms, 1)]
        for copy in copies:
            copy.wait()
        got = rs_buf[...]
        p_sum = jnp.sum(got[:, :param_rows], axis=0)
        f_sum = jnp.sum(got[:, param_rows:].reshape(groups, pair, filter_rows, width), axis=1)
        mine = jnp.concatenate([p_sum, f_sum.reshape(groups * filter_rows, width)], axis=0)

        ag_buf[pl.ds(md, 1)] = mine[None]
        copies = send_all(dp_n, lambda k: ag_buf.at[md], ag_buf.at[md], 1, dp_peer)
        for copy in copies:
            copy.wait()
        total = jnp.sum(ag_buf[...], axis=0)
        fg_ref[...] = total[param_rows:].reshape(groups, filter_rows, width)

        full_ref[pl.ds(ms, 1)] = total[:param_rows][None]
        copies = send_all(seq_n, lambda k: full_ref.at[ms], full_ref.at[ms], 2, seq_peer)
        for copy in copies:
            copy.wait()

    vmem = pl.BlockSpec(memory_space=pltpu.VMEM)
    return pl.pallas_call(
        kernel,
        out_shape=(
            jax.ShapeDtypeStruct(out_msg.shape, out_msg.dtype),
            jax.ShapeDtypeStruct((seq_n, param_rows, width), jnp.float32),
            jax.ShapeDtypeStruct((groups, filter_rows, width), jnp.float32),
        ),
        in_specs=[vmem] * 4,
        out_specs=(vmem, vmem, vmem),
        scratch_shapes=[
            pltpu.VMEM((seq_n, msg_rows, width), jnp.float32),
            pltpu.VMEM((seq_n, msg_rows, width), jnp.float32),
            pltpu.VMEM((dp_n, ag_rows, width), jnp.float32),
            pltpu.SemaphoreType.DMA((4, 2, max(seq_n, dp_n))),
        ],
        compiler_params=pltpu.CompilerParams(collective_id=0, has_side_effects=True),
    )(out_msg, series_blk, cot_blk, side)


def shards(series, cotangent, w_in, w_out, taps, skip_one, skip_two, filter_one, filter_two):
    _, block, width = series.shape
    seq_n = lax.axis_size("seq")
    dp_n = lax.axis_size("dp")
    length = block * seq_n
    half = length // LANES
    me = lax.axis_index("seq")
    per = width // seq_n
    filters = filter_one.shape[0]
    group_width = width // filters
    per_group = group_width // per
    group = me // per_group
    grad_scale = 1.0 / math.sqrt(dp_n * series.shape[0] * length)
    tab = dft_tables(length)

    taps_sel = lax.dynamic_index_in_dim(
        taps.reshape(3, 3, seq_n, per), me, axis=2, keepdims=False
    ).reshape(3, 3 * per)
    skip1 = lax.dynamic_index_in_dim(skip_one.reshape(seq_n, per), me, axis=0, keepdims=False)
    skip2 = lax.dynamic_index_in_dim(skip_two.reshape(seq_n, per), me, axis=0, keepdims=False)
    skip1 = skip1[None, :, None]
    skip2 = skip2[None, :, None]

    proj_blk = jnp.einsum("td,dc->ct", series[0], w_in, preferred_element_type=jnp.float32)
    proj_blk = jnp.swapaxes(proj_blk.reshape(3, seq_n, per, block), 0, 1).reshape(seq_n, 3 * per, block)
    dprod_blk = jnp.einsum("td,cd->ct", cotangent[0], w_out, preferred_element_type=jnp.float32)
    dprod_blk = dprod_blk.reshape(seq_n, per, block)
    rows_sent = jnp.repeat(jnp.swapaxes(jnp.stack([filter_one, filter_two]), 0, 1), per_group, axis=0)
    got = swap_blocks(jnp.concatenate([proj_blk, dprod_blk, rows_sent], axis=1), "seq", 1)
    proj = jnp.swapaxes(got[:, : 3 * per], 0, 1).reshape(3 * per, length)
    d_product = jnp.swapaxes(
        got[:, 3 * per : 4 * per].reshape(seq_n, per, block // LANES, LANES), 1, 2
    ).reshape(half, per, LANES)
    h_rows = jnp.swapaxes(got[:, 4 * per :], 0, 1).reshape(2, length)
    prev1 = jnp.pad(proj, ((0, 0), (1, 0)))[:, :length]
    prev2 = jnp.pad(proj, ((0, 0), (2, 0)))[:, :length]
    conv = taps_sel[0][:, None] * proj + taps_sel[1][:, None] * prev1 + taps_sel[2][:, None] * prev2
    conv_f = fold(conv)
    value = conv_f[:, :per]
    gate_one = conv_f[:, per : 2 * per]
    gate_two = conv_f[:, 2 * per :]

    h_spec = spectrum(fold(h_rows), tab)
    h_one = h_spec[:, 0:1]
    h_two = h_spec[:, 1:2]

    v_spec = spectrum(value, tab)
    y_one = signal(cmul(v_spec, h_one), tab) + skip1 * value
    gated_mid = gate_one * y_one
    m_spec = spectrum(gated_mid, tab)
    y_two = signal(cmul(m_spec, h_two), tab) + skip2 * gated_mid
    product = (gate_two * y_two).astype(jnp.bfloat16)

    grad_two = d_product * gate_two
    d_gate_two = d_product * y_two
    g2_spec = spectrum(grad_two, tab)
    d_mid = signal(cmul(g2_spec, h_two, conj=True), tab) + skip2 * grad_two
    grad_one = d_mid * gate_one
    d_gate_one = d_mid * y_one
    g1_spec = spectrum(grad_one, tab)
    d_value = signal(cmul(g1_spec, h_one, conj=True), tab) + skip1 * grad_one

    corr = jnp.concatenate(
        [
            jnp.sum(cmul(g1_spec, v_spec, conj=True), axis=1, keepdims=True),
            jnp.sum(cmul(g2_spec, m_spec, conj=True), axis=1, keepdims=True),
        ],
        axis=1,
    )
    filt_grad = unfold(signal(corr, tab))

    d_conv = unfold(jnp.concatenate([d_value, d_gate_one, d_gate_two], axis=1))
    next1 = jnp.pad(d_conv, ((0, 0), (0, 1)))[:, 1:]
    next2 = jnp.pad(d_conv, ((0, 0), (0, 2)))[:, 2:]
    d_proj = (
        taps_sel[0][:, None] * d_conv + taps_sel[1][:, None] * next1 + taps_sel[2][:, None] * next2
    ).astype(jnp.bfloat16)

    local_taps = jnp.stack(
        [jnp.sum(d_conv * proj, axis=1), jnp.sum(d_conv * prev1, axis=1), jnp.sum(d_conv * prev2, axis=1)]
    )
    local_skip1 = jnp.sum(grad_one * value, axis=(0, 2))
    local_skip2 = jnp.sum(grad_two * gated_mid, axis=(0, 2))
    prod_sent = jnp.swapaxes(product.reshape(seq_n, half // seq_n, per, LANES), 1, 2)
    prod_sent = prod_sent.reshape(seq_n, per, block)
    dp_sent = jnp.swapaxes(d_proj.reshape(3 * per, seq_n, block), 0, 1)
    small = jnp.concatenate(
        [
            local_taps.reshape(3, 3, 1, per),
            jnp.stack([local_skip1, local_skip2, jnp.zeros_like(local_skip1)]).reshape(3, 1, 1, per),
        ],
        axis=1,
    )
    small_full = lax.dynamic_update_slice(
        jnp.zeros((3, 4, seq_n, per), jnp.float32), small, (0, 0, me, 0)
    )
    small_sent = jnp.transpose(grad_scale * small_full, (2, 0, 1, 3)).reshape(seq_n, -1)
    small_sent = jnp.pad(small_sent, ((0, 0), (0, 2 * block - small_sent.shape[1])))
    fg_sent = jnp.swapaxes(grad_scale * filt_grad.reshape(2, seq_n, block), 0, 1)
    side = jnp.concatenate([small_sent, fg_sent.reshape(seq_n, -1)], axis=1).reshape(seq_n, -1, LANES)
    back, full, fg = tail_rounds(
        jnp.concatenate([prod_sent, dp_sent], axis=1), series[0], cotangent[0], side,
        grad_scale, per_group, dp_n,
    )
    prod_rows = jnp.transpose(back[:, :per], (2, 0, 1)).reshape(block, width)
    dp_rows = jnp.transpose(back[:, per:].reshape(seq_n, 3, per, block), (3, 1, 0, 2))
    dp_rows = dp_rows.reshape(block, 3 * width)
    output = jnp.dot(prod_rows, w_out, preferred_element_type=jnp.float32).astype(jnp.bfloat16)
    output = output.reshape(1, block, width)
    d_series = jnp.einsum(
        "tc,dc->td", dp_rows, w_in, preferred_element_type=jnp.float32
    ).astype(jnp.bfloat16)
    d_series = d_series.reshape(1, block, width)

    fg_blocks = jnp.swapaxes(fg.reshape(filters, 2, block), 0, 1)
    grad_w_in = jnp.transpose(full[:, : 3 * per].reshape(seq_n, 3, per, width), (3, 1, 0, 2))
    grad_w_in = grad_w_in.reshape(width, 3 * width)
    grad_w_out = full[:, 3 * per : 4 * per].reshape(width, width)
    small_all = full[:, 4 * per :].reshape(seq_n, -1)[:, : 3 * 4 * per].reshape(seq_n, 3, 4, per)
    small_all = jnp.transpose(small_all, (1, 2, 0, 3)).reshape(3, 4, width)
    grad_taps = small_all[:, :3].reshape(3, 3 * width)
    grad_skip_one = small_all[0, 3]
    grad_skip_two = small_all[1, 3]

    return (
        output,
        d_series,
        grad_w_in,
        grad_w_out,
        grad_taps,
        grad_skip_one,
        grad_skip_two,
        fg_blocks[0],
        fg_blocks[1],
    )


def solution(mesh):
    in_specs = (
        P("dp", "seq", None),
        P("dp", "seq", None),
        P(),
        P(),
        P(),
        P(),
        P(),
        P(None, "seq"),
        P(None, "seq"),
    )
    out_specs = (
        P("dp", "seq", None),
        P("dp", "seq", None),
        P(),
        P(),
        P(),
        P(),
        P(),
        P(None, "seq"),
        P(None, "seq"),
    )
    return jax.shard_map(shards, mesh=mesh, in_specs=in_specs, out_specs=out_specs, check_vma=False)
```

```python
import math

import numpy as np

import jax
import jax.numpy as jnp
from jax import lax
from jax.experimental import pallas as pl
from jax.experimental.pallas import tpu as pltpu
from jax.sharding import PartitionSpec as P

PRECISION = lax.Precision.HIGH
LANES = 128


def dft_tables(length):
    size = 2 * length
    rows = size // LANES
    half = length // LANES
    k1 = np.arange(rows)
    f1 = np.exp(-2j * np.pi * (np.outer(k1, np.arange(half)) % rows) / rows)
    turn = np.exp(-2j * np.pi * np.outer(k1, np.arange(LANES)) / size)
    f2 = np.exp(-2j * np.pi * (np.outer(np.arange(LANES), np.arange(LANES)) % LANES) / LANES)
    fwd1 = np.concatenate([f1.real, f1.imag], axis=0)
    fwd2 = np.block([[f2.real, f2.imag], [-f2.imag, f2.real]])
    inv2 = np.block([[f2.real, -f2.imag], [f2.imag, f2.real]])
    inv1 = np.concatenate([f1.real.T, f1.imag.T], axis=1) / size
    as32 = lambda a: jnp.asarray(np.asarray(a, np.float32))
    return {
        "rows": rows,
        "fwd1": as32(fwd1),
        "fwd2": as32(fwd2),
        "inv1": as32(inv1),
        "inv2": as32(inv2),
        "turn_r": as32(turn.real)[:, None, :],
        "turn_i": as32(turn.imag)[:, None, :],
    }


def spectrum(x, tab):
    rows = tab["rows"]
    a = jnp.einsum("kn,ncm->kcm", tab["fwd1"], x, precision=PRECISION)
    ar, ai = a[:rows], a[rows:]
    tr, ti = tab["turn_r"], tab["turn_i"]
    cat = jnp.concatenate([ar * tr - ai * ti, ar * ti + ai * tr], axis=-1)
    return jnp.einsum("kcm,mj->kcj", cat, tab["fwd2"], precision=PRECISION)


def signal(s, tab):
    b = jnp.einsum("kcj,jm->kcm", s, tab["inv2"], precision=PRECISION)
    br, bi = b[..., :LANES], b[..., LANES:]
    tr, ti = tab["turn_r"], tab["turn_i"]
    stacked = jnp.concatenate([br * tr + bi * ti, bi * tr - br * ti], axis=0)
    return jnp.einsum("nk,kcm->ncm", tab["inv1"], stacked, precision=PRECISION)


def cmul(a, b, conj=False):
    ar, ai = a[..., :LANES], a[..., LANES:]
    br, bi = b[..., :LANES], b[..., LANES:]
    if conj:
        bi = -bi
    return jnp.concatenate([ar * br - ai * bi, ar * bi + ai * br], axis=-1)


def fold(x):
    c, length = x.shape
    return jnp.swapaxes(x.reshape(c, length // LANES, LANES), 0, 1)


def unfold(x):
    half, c, lanes = x.shape
    return jnp.swapaxes(x, 0, 1).reshape(c, half * lanes)


def tail_rounds(out_msg, series_blk, cot_blk, side, w_out, w_in_rows, scale, pair, dp_n):
    seq_n, out_rows, block = out_msg.shape
    per = out_rows // 4
    width = series_blk.shape[1]
    side_rows = side.shape[1]
    filter_rows = side_rows // 2
    param_rows = 3 * per + per + filter_rows
    msg_rows = param_rows + filter_rows
    groups = seq_n // pair
    ag_rows = param_rows + groups * filter_rows
    mesh = pl.DeviceIdType.MESH

    def kernel(out_ref, ser_ref, cot_ref, side_ref, wo_ref, wi_ref, back_ref, full_ref, fg_ref,
               o_ref, ds_ref, msg_buf, rs_buf, ag_buf, sems):
        ms = lax.axis_index("seq")
        md = lax.axis_index("dp")
        barrier = pltpu.get_barrier_semaphore()
        for k in range(1, seq_n):
            pl.semaphore_signal(barrier, inc=1, device_id=(md, lax.rem(ms + k, seq_n)), device_id_type=mesh)
        for k in range(1, dp_n):
            pl.semaphore_signal(barrier, inc=1, device_id=(lax.rem(md + k, dp_n), ms), device_id_type=mesh)
        pl.semaphore_wait(barrier, seq_n + dp_n - 2)

        def send_all(count, src, dst, stage, where):
            copies = []
            for k in range(1, count):
                copy = pltpu.make_async_remote_copy(
                    src_ref=src(k), dst_ref=dst, send_sem=sems.at[stage, 0, k],
                    recv_sem=sems.at[stage, 1, k], device_id=where(k), device_id_type=mesh,
                )
                copy.start()
                copies.append(copy)
            return copies

        seq_peer = lambda k: (md, lax.rem(ms + k, seq_n))
        dp_peer = lambda k: (lax.rem(md + k, dp_n), ms)

        copies = send_all(seq_n, lambda k: out_ref.at[lax.rem(ms + k, seq_n)], back_ref.at[ms], 3, seq_peer)
        back_ref[pl.ds(ms, 1)] = out_ref[pl.ds(ms, 1)]
        for copy in copies:
            copy.wait()
        ser = ser_ref[...].astype(jnp.float32)
        cot = cot_ref[...].astype(jnp.float32)
        for j in range(seq_n):
            rows = back_ref[j].astype(jnp.float32)
            msg_buf[j, : 3 * per] = scale * jnp.dot(rows[per:], ser, preferred_element_type=jnp.float32)
            msg_buf[j, 3 * per : 4 * per] = scale * jnp.dot(rows[:per], cot, preferred_element_type=jnp.float32)
        msg_buf[:, 4 * per :] = side_ref[...]
        every = back_ref[...].astype(jnp.float32)
        prod_t = every[:, :per].reshape(seq_n * per, block).T
        o_ref[...] = jnp.dot(
            prod_t, wo_ref[...].astype(jnp.float32), preferred_element_type=jnp.float32
        ).astype(o_ref.dtype)
        dp_t = every[:, per:].reshape(seq_n * 3 * per, block).T
        ds_ref[...] = jnp.dot(
            dp_t, wi_ref[...].astype(jnp.float32), preferred_element_type=jnp.float32
        ).astype(ds_ref.dtype)

        copies = send_all(seq_n, lambda k: msg_buf.at[lax.rem(ms + k, seq_n)], rs_buf.at[ms], 0, seq_peer)
        rs_buf[pl.ds(ms, 1)] = msg_buf[pl.ds(ms, 1)]
        for copy in copies:
            copy.wait()
        got = rs_buf[...]
        p_sum = jnp.sum(got[:, :param_rows], axis=0)
        f_sum = jnp.sum(got[:, param_rows:].reshape(groups, pair, filter_rows, width), axis=1)
        mine = jnp.concatenate([p_sum, f_sum.reshape(groups * filter_rows, width)], axis=0)

        ag_buf[pl.ds(md, 1)] = mine[None]
        copies = send_all(dp_n, lambda k: ag_buf.at[md], ag_buf.at[md], 1, dp_peer)
        for copy in copies:
            copy.wait()
        total = jnp.sum(ag_buf[...], axis=0)
        fg_ref[...] = total[param_rows:].reshape(groups, filter_rows, width)

        full_ref[pl.ds(ms, 1)] = total[:param_rows][None]
        copies = send_all(seq_n, lambda k: full_ref.at[ms], full_ref.at[ms], 2, seq_peer)
        for copy in copies:
            copy.wait()

    vmem = pl.BlockSpec(memory_space=pltpu.VMEM)
    return pl.pallas_call(
        kernel,
        out_shape=(
            jax.ShapeDtypeStruct(out_msg.shape, out_msg.dtype),
            jax.ShapeDtypeStruct((seq_n, param_rows, width), jnp.float32),
            jax.ShapeDtypeStruct((groups, filter_rows, width), jnp.float32),
            jax.ShapeDtypeStruct((block, width), jnp.bfloat16),
            jax.ShapeDtypeStruct((block, width), jnp.bfloat16),
        ),
        in_specs=[vmem] * 6,
        out_specs=(vmem, vmem, vmem, vmem, vmem),
        scratch_shapes=[
            pltpu.VMEM((seq_n, msg_rows, width), jnp.float32),
            pltpu.VMEM((seq_n, msg_rows, width), jnp.float32),
            pltpu.VMEM((dp_n, ag_rows, width), jnp.float32),
            pltpu.SemaphoreType.DMA((4, 2, max(seq_n, dp_n))),
        ],
        compiler_params=pltpu.CompilerParams(collective_id=0, has_side_effects=True),
    )(out_msg, series_blk, cot_blk, side, w_out, w_in_rows)


def shards(series, cotangent, w_in, w_out, taps, skip_one, skip_two, filter_one, filter_two):
    _, block, width = series.shape
    seq_n = lax.axis_size("seq")
    dp_n = lax.axis_size("dp")
    length = block * seq_n
    half = length // LANES
    me = lax.axis_index("seq")
    per = width // seq_n
    filters = filter_one.shape[0]
    group_width = width // filters
    per_group = group_width // per
    group = me // per_group
    grad_scale = 1.0 / math.sqrt(dp_n * series.shape[0] * length)
    tab = dft_tables(length)

    taps_sel = lax.dynamic_index_in_dim(
        taps.reshape(3, 3, seq_n, per), me, axis=2, keepdims=False
    ).reshape(3, 3 * per)
    skip1 = lax.dynamic_index_in_dim(skip_one.reshape(seq_n, per), me, axis=0, keepdims=False)
    skip2 = lax.dynamic_index_in_dim(skip_two.reshape(seq_n, per), me, axis=0, keepdims=False)
    skip1 = skip1[None, :, None]
    skip2 = skip2[None, :, None]

    proj_blk = jnp.einsum("td,dc->ct", series[0], w_in, preferred_element_type=jnp.float32)
    proj_blk = jnp.swapaxes(proj_blk.reshape(3, seq_n, per, block), 0, 1).reshape(seq_n, 3 * per, block)
    dprod_blk = jnp.einsum("td,cd->ct", cotangent[0], w_out, preferred_element_type=jnp.float32)
    dprod_blk = dprod_blk.reshape(seq_n, per, block)
    rows_sent = jnp.repeat(jnp.swapaxes(jnp.stack([filter_one, filter_two]), 0, 1), per_group, axis=0)
    got = lax.all_to_all(
        jnp.concatenate([proj_blk, dprod_blk, rows_sent], axis=1), "seq", 0, 0, tiled=True
    )
    proj = jnp.swapaxes(got[:, : 3 * per], 0, 1).reshape(3 * per, length)
    d_product = jnp.swapaxes(
        got[:, 3 * per : 4 * per].reshape(seq_n, per, block // LANES, LANES), 1, 2
    ).reshape(half, per, LANES)
    h_rows = jnp.swapaxes(got[:, 4 * per :], 0, 1).reshape(2, length)
    prev1 = jnp.pad(proj, ((0, 0), (1, 0)))[:, :length]
    prev2 = jnp.pad(proj, ((0, 0), (2, 0)))[:, :length]
    conv = taps_sel[0][:, None] * proj + taps_sel[1][:, None] * prev1 + taps_sel[2][:, None] * prev2
    conv_f = fold(conv)
    value = conv_f[:, :per]
    gate_one = conv_f[:, per : 2 * per]
    gate_two = conv_f[:, 2 * per :]

    h_spec = spectrum(fold(h_rows), tab)
    h_one = h_spec[:, 0:1]
    h_two = h_spec[:, 1:2]

    v_spec = spectrum(value, tab)
    y_one = signal(cmul(v_spec, h_one), tab) + skip1 * value
    gated_mid = gate_one * y_one
    m_spec = spectrum(gated_mid, tab)
    y_two = signal(cmul(m_spec, h_two), tab) + skip2 * gated_mid
    product = (gate_two * y_two).astype(jnp.bfloat16)

    grad_two = d_product * gate_two
    d_gate_two = d_product * y_two
    g2_spec = spectrum(grad_two, tab)
    d_mid = signal(cmul(g2_spec, h_two, conj=True), tab) + skip2 * grad_two
    grad_one = d_mid * gate_one
    d_gate_one = d_mid * y_one
    g1_spec = spectrum(grad_one, tab)
    d_value = signal(cmul(g1_spec, h_one, conj=True), tab) + skip1 * grad_one

    corr = jnp.concatenate(
        [
            jnp.sum(cmul(g1_spec, v_spec, conj=True), axis=1, keepdims=True),
            jnp.sum(cmul(g2_spec, m_spec, conj=True), axis=1, keepdims=True),
        ],
        axis=1,
    )
    filt_grad = unfold(signal(corr, tab))

    d_conv = unfold(jnp.concatenate([d_value, d_gate_one, d_gate_two], axis=1))
    next1 = jnp.pad(d_conv, ((0, 0), (0, 1)))[:, 1:]
    next2 = jnp.pad(d_conv, ((0, 0), (0, 2)))[:, 2:]
    d_proj = (
        taps_sel[0][:, None] * d_conv + taps_sel[1][:, None] * next1 + taps_sel[2][:, None] * next2
    ).astype(jnp.bfloat16)

    local_taps = jnp.stack(
        [jnp.sum(d_conv * proj, axis=1), jnp.sum(d_conv * prev1, axis=1), jnp.sum(d_conv * prev2, axis=1)]
    )
    local_skip1 = jnp.sum(grad_one * value, axis=(0, 2))
    local_skip2 = jnp.sum(grad_two * gated_mid, axis=(0, 2))
    prod_sent = jnp.swapaxes(product.reshape(seq_n, half // seq_n, per, LANES), 1, 2)
    prod_sent = prod_sent.reshape(seq_n, per, block)
    dp_sent = jnp.swapaxes(d_proj.reshape(3 * per, seq_n, block), 0, 1)
    small = jnp.concatenate(
        [
            local_taps.reshape(3, 3, 1, per),
            jnp.stack([local_skip1, local_skip2, jnp.zeros_like(local_skip1)]).reshape(3, 1, 1, per),
        ],
        axis=1,
    )
    small_full = lax.dynamic_update_slice(
        jnp.zeros((3, 4, seq_n, per), jnp.float32), small, (0, 0, me, 0)
    )
    small_sent = jnp.transpose(grad_scale * small_full, (2, 0, 1, 3)).reshape(seq_n, -1)
    small_sent = jnp.pad(small_sent, ((0, 0), (0, 2 * block - small_sent.shape[1])))
    fg_sent = jnp.swapaxes(grad_scale * filt_grad.reshape(2, seq_n, block), 0, 1)
    side = jnp.concatenate([small_sent, fg_sent.reshape(seq_n, -1)], axis=1).reshape(seq_n, -1, LANES)
    w_in_rows = jnp.transpose(w_in.reshape(width, 3, seq_n, per), (2, 1, 3, 0)).reshape(3 * width, width)
    _, full, fg, output, d_series = tail_rounds(
        jnp.concatenate([prod_sent, dp_sent], axis=1), series[0], cotangent[0], side,
        w_out, w_in_rows, grad_scale, per_group, dp_n,
    )
    output = output.reshape(1, block, width)
    d_series = d_series.reshape(1, block, width)

    fg_blocks = jnp.swapaxes(fg.reshape(filters, 2, block), 0, 1)
    grad_w_in = jnp.transpose(full[:, : 3 * per].reshape(seq_n, 3, per, width), (3, 1, 0, 2))
    grad_w_in = grad_w_in.reshape(width, 3 * width)
    grad_w_out = full[:, 3 * per : 4 * per].reshape(width, width)
    small_all = full[:, 4 * per :].reshape(seq_n, -1)[:, : 3 * 4 * per].reshape(seq_n, 3, 4, per)
    small_all = jnp.transpose(small_all, (1, 2, 0, 3)).reshape(3, 4, width)
    grad_taps = small_all[:, :3].reshape(3, 3 * width)
    grad_skip_one = small_all[0, 3]
    grad_skip_two = small_all[1, 3]

    return (
        output,
        d_series,
        grad_w_in,
        grad_w_out,
        grad_taps,
        grad_skip_one,
        grad_skip_two,
        fg_blocks[0],
        fg_blocks[1],
    )


def solution(mesh):
    in_specs = (
        P("dp", "seq", None),
        P("dp", "seq", None),
        P(),
        P(),
        P(),
        P(),
        P(),
        P(None, "seq"),
        P(None, "seq"),
    )
    out_specs = (
        P("dp", "seq", None),
        P("dp", "seq", None),
        P(),
        P(),
        P(),
        P(),
        P(),
        P(None, "seq"),
        P(None, "seq"),
    )
    return jax.shard_map(shards, mesh=mesh, in_specs=in_specs, out_specs=out_specs, check_vma=False)
```

```python
import math

import numpy as np

import jax
import jax.numpy as jnp
from jax import lax
from jax.experimental import pallas as pl
from jax.experimental.pallas import tpu as pltpu
from jax.sharding import PartitionSpec as P

PRECISION = lax.Precision.HIGH
LANES = 128


def dft_tables(length):
    size = 2 * length
    rows = size // LANES
    half = length // LANES
    k1 = np.arange(rows)
    f1 = np.exp(-2j * np.pi * (np.outer(k1, np.arange(half)) % rows) / rows)
    turn = np.exp(-2j * np.pi * np.outer(k1, np.arange(LANES)) / size)
    f2 = np.exp(-2j * np.pi * (np.outer(np.arange(LANES), np.arange(LANES)) % LANES) / LANES)
    fwd1 = np.concatenate([f1.real, f1.imag], axis=0)
    fwd2 = np.block([[f2.real, f2.imag], [-f2.imag, f2.real]])
    inv2 = np.block([[f2.real, -f2.imag], [f2.imag, f2.real]])
    inv1 = np.concatenate([f1.real.T, f1.imag.T], axis=1) / size
    as32 = lambda a: jnp.asarray(np.asarray(a, np.float32))
    return {
        "rows": rows,
        "fwd1": as32(fwd1),
        "fwd2": as32(fwd2),
        "inv1": as32(inv1),
        "inv2": as32(inv2),
        "turn_r": as32(turn.real)[:, None, :],
        "turn_i": as32(turn.imag)[:, None, :],
    }


def spectrum(x, tab):
    rows = tab["rows"]
    a = jnp.einsum("kn,ncm->kcm", tab["fwd1"], x, precision=PRECISION)
    ar, ai = a[:rows], a[rows:]
    tr, ti = tab["turn_r"], tab["turn_i"]
    cat = jnp.concatenate([ar * tr - ai * ti, ar * ti + ai * tr], axis=-1)
    return jnp.einsum("kcm,mj->kcj", cat, tab["fwd2"], precision=PRECISION)


def signal(s, tab):
    b = jnp.einsum("kcj,jm->kcm", s, tab["inv2"], precision=PRECISION)
    br, bi = b[..., :LANES], b[..., LANES:]
    tr, ti = tab["turn_r"], tab["turn_i"]
    stacked = jnp.concatenate([br * tr + bi * ti, bi * tr - br * ti], axis=0)
    return jnp.einsum("nk,kcm->ncm", tab["inv1"], stacked, precision=PRECISION)


def cmul(a, b, conj=False):
    ar, ai = a[..., :LANES], a[..., LANES:]
    br, bi = b[..., :LANES], b[..., LANES:]
    if conj:
        bi = -bi
    return jnp.concatenate([ar * br - ai * bi, ar * bi + ai * br], axis=-1)


def fold(x):
    c, length = x.shape
    return jnp.swapaxes(x.reshape(c, length // LANES, LANES), 0, 1)


def unfold(x):
    half, c, lanes = x.shape
    return jnp.swapaxes(x, 0, 1).reshape(c, half * lanes)


def tail_rounds(out_msg, series_blk, cot_blk, side, scale, pair, dp_n):
    seq_n, out_rows, block = out_msg.shape
    per = out_rows // 4
    width = series_blk.shape[1]
    side_rows = side.shape[1]
    filter_rows = side_rows // 2
    param_rows = 3 * per + per + filter_rows
    msg_rows = param_rows + filter_rows
    groups = seq_n // pair
    ag_rows = param_rows + groups * filter_rows
    mesh = pl.DeviceIdType.MESH

    def kernel(out_ref, ser_ref, cot_ref, side_ref, back_ref, full_ref, fg_ref,
               msg_buf, rs_buf, ag_buf, sems):
        ms = lax.axis_index("seq")
        md = lax.axis_index("dp")
        barrier = pltpu.get_barrier_semaphore()
        for k in range(1, seq_n):
            pl.semaphore_signal(barrier, inc=1, device_id=(md, lax.rem(ms + k, seq_n)), device_id_type=mesh)
        for k in range(1, dp_n):
            pl.semaphore_signal(barrier, inc=1, device_id=(lax.rem(md + k, dp_n), ms), device_id_type=mesh)
        pl.semaphore_wait(barrier, seq_n + dp_n - 2)

        def send_all(count, src, dst, stage, where):
            copies = []
            for k in range(1, count):
                copy = pltpu.make_async_remote_copy(
                    src_ref=src(k), dst_ref=dst, send_sem=sems.at[stage, 0, k],
                    recv_sem=sems.at[stage, 1, k], device_id=where(k), device_id_type=mesh,
                )
                copy.start()
                copies.append(copy)
            return copies

        seq_peer = lambda k: (md, lax.rem(ms + k, seq_n))
        dp_peer = lambda k: (lax.rem(md + k, dp_n), ms)

        copies = send_all(seq_n, lambda k: out_ref.at[lax.rem(ms + k, seq_n)], back_ref.at[ms], 3, seq_peer)
        back_ref[pl.ds(ms, 1)] = out_ref[pl.ds(ms, 1)]
        for copy in copies:
            copy.wait()
        ser = ser_ref[...].astype(jnp.float32)
        cot = cot_ref[...].astype(jnp.float32)
        for j in range(seq_n):
            rows = back_ref[j].astype(jnp.float32)
            msg_buf[j, : 3 * per] = scale * jnp.dot(rows[per:], ser, preferred_element_type=jnp.float32)
            msg_buf[j, 3 * per : 4 * per] = scale * jnp.dot(rows[:per], cot, preferred_element_type=jnp.float32)
        msg_buf[:, 4 * per :] = side_ref[...]

        copies = send_all(seq_n, lambda k: msg_buf.at[lax.rem(ms + k, seq_n)], rs_buf.at[ms], 0, seq_peer)
        rs_buf[pl.ds(ms, 1)] = msg_buf[pl.ds(ms, 1)]
        for copy in copies:
            copy.wait()
        got = rs_buf[...]
        p_sum = jnp.sum(got[:, :param_rows], axis=0)
        f_sum = jnp.sum(got[:, param_rows:].reshape(groups, pair, filter_rows, width), axis=1)
        mine = jnp.concatenate([p_sum, f_sum.reshape(groups * filter_rows, width)], axis=0)

        ag_buf[pl.ds(md, 1)] = mine[None]
        copies = send_all(dp_n, lambda k: ag_buf.at[md], ag_buf.at[md], 1, dp_peer)
        for copy in copies:
            copy.wait()
        total = jnp.sum(ag_buf[...], axis=0)
        fg_ref[...] = total[param_rows:].reshape(groups, filter_rows, width)

        full_ref[pl.ds(ms, 1)] = total[:param_rows][None]
        copies = send_all(seq_n, lambda k: full_ref.at[ms], full_ref.at[ms], 2, seq_peer)
        for copy in copies:
            copy.wait()

    vmem = pl.BlockSpec(memory_space=pltpu.VMEM)
    return pl.pallas_call(
        kernel,
        out_shape=(
            jax.ShapeDtypeStruct(out_msg.shape, out_msg.dtype),
            jax.ShapeDtypeStruct((seq_n, param_rows, width), jnp.float32),
            jax.ShapeDtypeStruct((groups, filter_rows, width), jnp.float32),
        ),
        in_specs=[vmem] * 4,
        out_specs=(vmem, vmem, vmem),
        scratch_shapes=[
            pltpu.VMEM((seq_n, msg_rows, width), jnp.float32),
            pltpu.VMEM((seq_n, msg_rows, width), jnp.float32),
            pltpu.VMEM((dp_n, ag_rows, width), jnp.float32),
            pltpu.SemaphoreType.DMA((4, 2, max(seq_n, dp_n))),
        ],
        compiler_params=pltpu.CompilerParams(collective_id=0, has_side_effects=True),
    )(out_msg, series_blk, cot_blk, side)


def shards(series, cotangent, w_in, w_out, taps, skip_one, skip_two, filter_one, filter_two):
    _, block, width = series.shape
    seq_n = lax.axis_size("seq")
    dp_n = lax.axis_size("dp")
    length = block * seq_n
    half = length // LANES
    me = lax.axis_index("seq")
    per = width // seq_n
    filters = filter_one.shape[0]
    group_width = width // filters
    per_group = group_width // per
    group = me // per_group
    grad_scale = 1.0 / math.sqrt(dp_n * series.shape[0] * length)
    tab = dft_tables(length)

    taps_sel = lax.dynamic_index_in_dim(
        taps.reshape(3, 3, seq_n, per), me, axis=2, keepdims=False
    ).reshape(3, 3 * per)
    skip1 = lax.dynamic_index_in_dim(skip_one.reshape(seq_n, per), me, axis=0, keepdims=False)
    skip2 = lax.dynamic_index_in_dim(skip_two.reshape(seq_n, per), me, axis=0, keepdims=False)
    skip1 = skip1[None, :, None]
    skip2 = skip2[None, :, None]

    proj_blk = jnp.einsum("td,dc->ct", series[0], w_in, preferred_element_type=jnp.float32)
    proj_blk = jnp.swapaxes(proj_blk.reshape(3, seq_n, per, block), 0, 1).reshape(seq_n, 3 * per, block)
    dprod_blk = jnp.einsum("td,cd->ct", cotangent[0], w_out, preferred_element_type=jnp.float32)
    dprod_blk = dprod_blk.reshape(seq_n, per, block)
    rows_sent = jnp.repeat(jnp.swapaxes(jnp.stack([filter_one, filter_two]), 0, 1), per_group, axis=0)
    got = lax.all_to_all(
        jnp.concatenate([proj_blk, dprod_blk, rows_sent], axis=1), "seq", 0, 0, tiled=True
    )
    proj = jnp.swapaxes(got[:, : 3 * per], 0, 1).reshape(3 * per, length)
    d_product = jnp.swapaxes(
        got[:, 3 * per : 4 * per].reshape(seq_n, per, block // LANES, LANES), 1, 2
    ).reshape(half, per, LANES)
    h_rows = jnp.swapaxes(got[:, 4 * per :], 0, 1).reshape(2, length)
    prev1 = jnp.pad(proj, ((0, 0), (1, 0)))[:, :length]
    prev2 = jnp.pad(proj, ((0, 0), (2, 0)))[:, :length]
    conv = taps_sel[0][:, None] * proj + taps_sel[1][:, None] * prev1 + taps_sel[2][:, None] * prev2
    conv_f = fold(conv)
    value = conv_f[:, :per]
    gate_one = conv_f[:, per : 2 * per]
    gate_two = conv_f[:, 2 * per :]


    both_spec = spectrum(jnp.concatenate([value, fold(h_rows)], axis=1), tab)
    v_spec = both_spec[:, :per]
    h_one = both_spec[:, per : per + 1]
    h_two = both_spec[:, per + 1 : per + 2]
    y_one = signal(cmul(v_spec, h_one), tab) + skip1 * value
    gated_mid = gate_one * y_one
    m_spec = spectrum(gated_mid, tab)
    y_two = signal(cmul(m_spec, h_two), tab) + skip2 * gated_mid
    product = (gate_two * y_two).astype(jnp.bfloat16)

    grad_two = d_product * gate_two
    d_gate_two = d_product * y_two
    g2_spec = spectrum(grad_two, tab)
    d_mid = signal(cmul(g2_spec, h_two, conj=True), tab) + skip2 * grad_two
    grad_one = d_mid * gate_one
    d_gate_one = d_mid * y_one
    g1_spec = spectrum(grad_one, tab)
    corr = jnp.concatenate(
        [
            jnp.sum(cmul(g1_spec, v_spec, conj=True), axis=1, keepdims=True),
            jnp.sum(cmul(g2_spec, m_spec, conj=True), axis=1, keepdims=True),
        ],
        axis=1,
    )
    last = signal(jnp.concatenate([cmul(g1_spec, h_one, conj=True), corr], axis=1), tab)
    d_value = last[:, :per] + skip1 * grad_one
    filt_grad = unfold(last[:, per:])

    d_conv = unfold(jnp.concatenate([d_value, d_gate_one, d_gate_two], axis=1))
    next1 = jnp.pad(d_conv, ((0, 0), (0, 1)))[:, 1:]
    next2 = jnp.pad(d_conv, ((0, 0), (0, 2)))[:, 2:]
    d_proj = (
        taps_sel[0][:, None] * d_conv + taps_sel[1][:, None] * next1 + taps_sel[2][:, None] * next2
    ).astype(jnp.bfloat16)

    local_taps = jnp.stack(
        [jnp.sum(d_conv * proj, axis=1), jnp.sum(d_conv * prev1, axis=1), jnp.sum(d_conv * prev2, axis=1)]
    )
    local_skip1 = jnp.sum(grad_one * value, axis=(0, 2))
    local_skip2 = jnp.sum(grad_two * gated_mid, axis=(0, 2))
    prod_sent = jnp.swapaxes(product.reshape(seq_n, half // seq_n, per, LANES), 1, 2)
    prod_sent = prod_sent.reshape(seq_n, per, block)
    dp_sent = jnp.swapaxes(d_proj.reshape(3 * per, seq_n, block), 0, 1)
    small = jnp.concatenate(
        [
            local_taps.reshape(3, 3, 1, per),
            jnp.stack([local_skip1, local_skip2, jnp.zeros_like(local_skip1)]).reshape(3, 1, 1, per),
        ],
        axis=1,
    )
    small_full = lax.dynamic_update_slice(
        jnp.zeros((3, 4, seq_n, per), jnp.float32), small, (0, 0, me, 0)
    )
    small_sent = jnp.transpose(grad_scale * small_full, (2, 0, 1, 3)).reshape(seq_n, -1)
    small_sent = jnp.pad(small_sent, ((0, 0), (0, 2 * block - small_sent.shape[1])))
    fg_sent = jnp.swapaxes(grad_scale * filt_grad.reshape(2, seq_n, block), 0, 1)
    side = jnp.concatenate([small_sent, fg_sent.reshape(seq_n, -1)], axis=1).reshape(seq_n, -1, LANES)
    back, full, fg = tail_rounds(
        jnp.concatenate([prod_sent, dp_sent], axis=1), series[0], cotangent[0], side,
        grad_scale, per_group, dp_n,
    )
    prod_rows = jnp.transpose(back[:, :per], (2, 0, 1)).reshape(block, width)
    dp_rows = jnp.transpose(back[:, per:].reshape(seq_n, 3, per, block), (3, 1, 0, 2))
    dp_rows = dp_rows.reshape(block, 3 * width)
    output = jnp.dot(prod_rows, w_out, preferred_element_type=jnp.float32).astype(jnp.bfloat16)
    output = output.reshape(1, block, width)
    d_series = jnp.einsum(
        "tc,dc->td", dp_rows, w_in, preferred_element_type=jnp.float32
    ).astype(jnp.bfloat16)
    d_series = d_series.reshape(1, block, width)

    fg_blocks = jnp.swapaxes(fg.reshape(filters, 2, block), 0, 1)
    grad_w_in = jnp.transpose(full[:, : 3 * per].reshape(seq_n, 3, per, width), (3, 1, 0, 2))
    grad_w_in = grad_w_in.reshape(width, 3 * width)
    grad_w_out = full[:, 3 * per : 4 * per].reshape(width, width)
    small_all = full[:, 4 * per :].reshape(seq_n, -1)[:, : 3 * 4 * per].reshape(seq_n, 3, 4, per)
    small_all = jnp.transpose(small_all, (1, 2, 0, 3)).reshape(3, 4, width)
    grad_taps = small_all[:, :3].reshape(3, 3 * width)
    grad_skip_one = small_all[0, 3]
    grad_skip_two = small_all[1, 3]

    return (
        output,
        d_series,
        grad_w_in,
        grad_w_out,
        grad_taps,
        grad_skip_one,
        grad_skip_two,
        fg_blocks[0],
        fg_blocks[1],
    )


def solution(mesh):
    in_specs = (
        P("dp", "seq", None),
        P("dp", "seq", None),
        P(),
        P(),
        P(),
        P(),
        P(),
        P(None, "seq"),
        P(None, "seq"),
    )
    out_specs = (
        P("dp", "seq", None),
        P("dp", "seq", None),
        P(),
        P(),
        P(),
        P(),
        P(),
        P(None, "seq"),
        P(None, "seq"),
    )
    return jax.shard_map(shards, mesh=mesh, in_specs=in_specs, out_specs=out_specs, check_vma=False)
```

```python
import math

import numpy as np

import jax
import jax.numpy as jnp
from jax import lax
from jax.experimental import pallas as pl
from jax.experimental.pallas import tpu as pltpu
from jax.sharding import PartitionSpec as P

PRECISION = lax.Precision.HIGH
LANES = 128


def dft_tables(length):
    size = 2 * length
    rows = size // LANES
    half = length // LANES
    k1 = np.arange(rows)
    f1 = np.exp(-2j * np.pi * (np.outer(k1, np.arange(half)) % rows) / rows)
    turn = np.exp(-2j * np.pi * np.outer(k1, np.arange(LANES)) / size)
    f2 = np.exp(-2j * np.pi * (np.outer(np.arange(LANES), np.arange(LANES)) % LANES) / LANES)
    fwd1 = np.concatenate([f1.real, f1.imag], axis=0)
    fwd2 = np.block([[f2.real, f2.imag], [-f2.imag, f2.real]])
    inv2 = np.block([[f2.real, -f2.imag], [f2.imag, f2.real]])
    inv1 = np.concatenate([f1.real.T, f1.imag.T], axis=1) / size
    as32 = lambda a: jnp.asarray(np.asarray(a, np.float32))
    return {
        "rows": rows,
        "fwd1": as32(fwd1),
        "fwd2": as32(fwd2),
        "inv1": as32(inv1),
        "inv2": as32(inv2),
        "turn_r": as32(turn.real)[:, None, :],
        "turn_i": as32(turn.imag)[:, None, :],
    }


def spectrum(x, tab):
    rows = tab["rows"]
    a = jnp.einsum("kn,ncm->kcm", tab["fwd1"], x, precision=PRECISION)
    ar, ai = a[:rows], a[rows:]
    tr, ti = tab["turn_r"], tab["turn_i"]
    cat = jnp.concatenate([ar * tr - ai * ti, ar * ti + ai * tr], axis=-1)
    return jnp.einsum("kcm,mj->kcj", cat, tab["fwd2"], precision=PRECISION)


def signal(s, tab):
    b = jnp.einsum("kcj,jm->kcm", s, tab["inv2"], precision=PRECISION)
    br, bi = b[..., :LANES], b[..., LANES:]
    tr, ti = tab["turn_r"], tab["turn_i"]
    stacked = jnp.concatenate([br * tr + bi * ti, bi * tr - br * ti], axis=0)
    return jnp.einsum("nk,kcm->ncm", tab["inv1"], stacked, precision=PRECISION)


def cmul(a, b, conj=False):
    ar, ai = a[..., :LANES], a[..., LANES:]
    br, bi = b[..., :LANES], b[..., LANES:]
    if conj:
        bi = -bi
    return jnp.concatenate([ar * br - ai * bi, ar * bi + ai * br], axis=-1)


def fold(x):
    c, length = x.shape
    return jnp.swapaxes(x.reshape(c, length // LANES, LANES), 0, 1)


def unfold(x):
    half, c, lanes = x.shape
    return jnp.swapaxes(x, 0, 1).reshape(c, half * lanes)


def tail_rounds(out_msg, series_blk, cot_blk, side, scale, pair, dp_n):
    seq_n, out_rows, block = out_msg.shape
    per = out_rows // 4
    width = series_blk.shape[1]
    side_rows = side.shape[1]
    filter_rows = side_rows // 2
    param_rows = 3 * per + per + filter_rows
    msg_rows = param_rows + filter_rows
    groups = seq_n // pair
    ag_rows = param_rows + groups * filter_rows
    mesh = pl.DeviceIdType.MESH

    def kernel(out_ref, ser_ref, cot_ref, side_ref, back_ref, full_ref, fg_ref,
               msg_buf, rs_buf, ag_buf, sems):
        ms = lax.axis_index("seq")
        md = lax.axis_index("dp")
        barrier = pltpu.get_barrier_semaphore()
        for k in range(1, seq_n):
            pl.semaphore_signal(barrier, inc=1, device_id=(md, lax.rem(ms + k, seq_n)), device_id_type=mesh)
        for k in range(1, dp_n):
            pl.semaphore_signal(barrier, inc=1, device_id=(lax.rem(md + k, dp_n), ms), device_id_type=mesh)
        pl.semaphore_wait(barrier, seq_n + dp_n - 2)

        def send_all(count, src, dst, stage, where):
            copies = []
            for k in range(1, count):
                copy = pltpu.make_async_remote_copy(
                    src_ref=src(k), dst_ref=dst, send_sem=sems.at[stage, 0, k],
                    recv_sem=sems.at[stage, 1, k], device_id=where(k), device_id_type=mesh,
                )
                copy.start()
                copies.append(copy)
            return copies

        seq_peer = lambda k: (md, lax.rem(ms + k, seq_n))
        dp_peer = lambda k: (lax.rem(md + k, dp_n), ms)

        copies = send_all(seq_n, lambda k: out_ref.at[lax.rem(ms + k, seq_n)], back_ref.at[ms], 3, seq_peer)
        back_ref[pl.ds(ms, 1)] = out_ref[pl.ds(ms, 1)]
        for copy in copies:
            copy.wait()
        ser = ser_ref[...].astype(jnp.float32)
        cot = cot_ref[...].astype(jnp.float32)
        for j in range(seq_n):
            rows = back_ref[j].astype(jnp.float32)
            msg_buf[j, : 3 * per] = scale * jnp.dot(rows[per:], ser, preferred_element_type=jnp.float32)
            msg_buf[j, 3 * per : 4 * per] = scale * jnp.dot(rows[:per], cot, preferred_element_type=jnp.float32)
        msg_buf[:, 4 * per :] = side_ref[...]

        copies = send_all(seq_n, lambda k: msg_buf.at[lax.rem(ms + k, seq_n)], rs_buf.at[ms], 0, seq_peer)
        rs_buf[pl.ds(ms, 1)] = msg_buf[pl.ds(ms, 1)]
        for copy in copies:
            copy.wait()
        got = rs_buf[...]
        p_sum = jnp.sum(got[:, :param_rows], axis=0)
        f_sum = jnp.sum(got[:, param_rows:].reshape(groups, pair, filter_rows, width), axis=1)
        mine = jnp.concatenate([p_sum, f_sum.reshape(groups * filter_rows, width)], axis=0)

        ag_buf[pl.ds(md, 1)] = mine[None]
        copies = send_all(dp_n, lambda k: ag_buf.at[md], ag_buf.at[md], 1, dp_peer)
        for copy in copies:
            copy.wait()
        total = jnp.sum(ag_buf[...], axis=0)
        fg_ref[...] = total[param_rows:].reshape(groups, filter_rows, width)

        full_ref[pl.ds(ms, 1)] = total[:param_rows][None]
        copies = send_all(seq_n, lambda k: full_ref.at[ms], full_ref.at[ms], 2, seq_peer)
        for copy in copies:
            copy.wait()

    vmem = pl.BlockSpec(memory_space=pltpu.VMEM)
    return pl.pallas_call(
        kernel,
        out_shape=(
            jax.ShapeDtypeStruct(out_msg.shape, out_msg.dtype),
            jax.ShapeDtypeStruct((seq_n, param_rows, width), jnp.float32),
            jax.ShapeDtypeStruct((groups, filter_rows, width), jnp.float32),
        ),
        in_specs=[vmem] * 4,
        out_specs=(vmem, vmem, vmem),
        scratch_shapes=[
            pltpu.VMEM((seq_n, msg_rows, width), jnp.float32),
            pltpu.VMEM((seq_n, msg_rows, width), jnp.float32),
            pltpu.VMEM((dp_n, ag_rows, width), jnp.float32),
            pltpu.SemaphoreType.DMA((4, 2, max(seq_n, dp_n))),
        ],
        compiler_params=pltpu.CompilerParams(collective_id=0, has_side_effects=True),
    )(out_msg, series_blk, cot_blk, side)


def shards(series, cotangent, w_in, w_out, taps, skip_one, skip_two, filter_one, filter_two):
    _, block, width = series.shape
    seq_n = lax.axis_size("seq")
    dp_n = lax.axis_size("dp")
    length = block * seq_n
    half = length // LANES
    me = lax.axis_index("seq")
    per = width // seq_n
    filters = filter_one.shape[0]
    group_width = width // filters
    per_group = group_width // per
    group = me // per_group
    grad_scale = 1.0 / math.sqrt(dp_n * series.shape[0] * length)
    tab = dft_tables(length)

    taps_sel = lax.dynamic_index_in_dim(
        taps.reshape(3, 3, seq_n, per), me, axis=2, keepdims=False
    ).reshape(3, 3 * per)
    skip1 = lax.dynamic_index_in_dim(skip_one.reshape(seq_n, per), me, axis=0, keepdims=False)
    skip2 = lax.dynamic_index_in_dim(skip_two.reshape(seq_n, per), me, axis=0, keepdims=False)
    skip1 = skip1[None, :, None]
    skip2 = skip2[None, :, None]

    proj_blk = jnp.einsum("td,dc->ct", series[0], w_in, preferred_element_type=jnp.float32)
    proj_blk = jnp.swapaxes(proj_blk.reshape(3, seq_n, per, block), 0, 1).reshape(seq_n, 3 * per, block)
    dprod_blk = jnp.einsum("td,cd->ct", cotangent[0], w_out, preferred_element_type=jnp.float32)
    dprod_blk = dprod_blk.reshape(seq_n, per, block)
    rows_sent = jnp.repeat(jnp.swapaxes(jnp.stack([filter_one, filter_two]), 0, 1), per_group, axis=0)
    got = lax.all_to_all(
        jnp.concatenate([proj_blk, dprod_blk, rows_sent], axis=1), "seq", 0, 0, tiled=True
    )
    proj = jnp.swapaxes(got[:, : 3 * per], 0, 1).reshape(3 * per, length)
    d_product = jnp.swapaxes(
        got[:, 3 * per : 4 * per].reshape(seq_n, per, block // LANES, LANES), 1, 2
    ).reshape(half, per, LANES)
    h_rows = jnp.swapaxes(got[:, 4 * per :], 0, 1).reshape(2, length)
    prev1 = jnp.pad(proj, ((0, 0), (1, 0)))[:, :length]
    prev2 = jnp.pad(proj, ((0, 0), (2, 0)))[:, :length]
    conv = taps_sel[0][:, None] * proj + taps_sel[1][:, None] * prev1 + taps_sel[2][:, None] * prev2
    conv_f = fold(conv)
    value = conv_f[:, :per]
    gate_one = conv_f[:, per : 2 * per]
    gate_two = conv_f[:, 2 * per :]


    grad_two = d_product * gate_two
    first = spectrum(jnp.concatenate([value, grad_two, fold(h_rows)], axis=1), tab)
    v_spec = first[:, :per]
    g2_spec = first[:, per : 2 * per]
    h_one = first[:, 2 * per : 2 * per + 1]
    h_two = first[:, 2 * per + 1 : 2 * per + 2]
    second = signal(
        jnp.concatenate([cmul(v_spec, h_one), cmul(g2_spec, h_two, conj=True)], axis=1), tab
    )
    y_one = second[:, :per] + skip1 * value
    d_mid = second[:, per:] + skip2 * grad_two
    gated_mid = gate_one * y_one
    grad_one = d_mid * gate_one
    d_gate_one = d_mid * y_one
    third = spectrum(jnp.concatenate([gated_mid, grad_one], axis=1), tab)
    m_spec = third[:, :per]
    g1_spec = third[:, per:]
    corr = jnp.concatenate(
        [
            jnp.sum(cmul(g1_spec, v_spec, conj=True), axis=1, keepdims=True),
            jnp.sum(cmul(g2_spec, m_spec, conj=True), axis=1, keepdims=True),
        ],
        axis=1,
    )
    last = signal(
        jnp.concatenate([cmul(m_spec, h_two), cmul(g1_spec, h_one, conj=True), corr], axis=1), tab
    )
    y_two = last[:, :per] + skip2 * gated_mid
    product = (gate_two * y_two).astype(jnp.bfloat16)
    d_gate_two = d_product * y_two
    d_value = last[:, per : 2 * per] + skip1 * grad_one
    filt_grad = unfold(last[:, 2 * per :])

    d_conv = unfold(jnp.concatenate([d_value, d_gate_one, d_gate_two], axis=1))
    next1 = jnp.pad(d_conv, ((0, 0), (0, 1)))[:, 1:]
    next2 = jnp.pad(d_conv, ((0, 0), (0, 2)))[:, 2:]
    d_proj = (
        taps_sel[0][:, None] * d_conv + taps_sel[1][:, None] * next1 + taps_sel[2][:, None] * next2
    ).astype(jnp.bfloat16)

    local_taps = jnp.stack(
        [jnp.sum(d_conv * proj, axis=1), jnp.sum(d_conv * prev1, axis=1), jnp.sum(d_conv * prev2, axis=1)]
    )
    local_skip1 = jnp.sum(grad_one * value, axis=(0, 2))
    local_skip2 = jnp.sum(grad_two * gated_mid, axis=(0, 2))
    prod_sent = jnp.swapaxes(product.reshape(seq_n, half // seq_n, per, LANES), 1, 2)
    prod_sent = prod_sent.reshape(seq_n, per, block)
    dp_sent = jnp.swapaxes(d_proj.reshape(3 * per, seq_n, block), 0, 1)
    small = jnp.concatenate(
        [
            local_taps.reshape(3, 3, 1, per),
            jnp.stack([local_skip1, local_skip2, jnp.zeros_like(local_skip1)]).reshape(3, 1, 1, per),
        ],
        axis=1,
    )
    small_full = lax.dynamic_update_slice(
        jnp.zeros((3, 4, seq_n, per), jnp.float32), small, (0, 0, me, 0)
    )
    small_sent = jnp.transpose(grad_scale * small_full, (2, 0, 1, 3)).reshape(seq_n, -1)
    small_sent = jnp.pad(small_sent, ((0, 0), (0, 2 * block - small_sent.shape[1])))
    fg_sent = jnp.swapaxes(grad_scale * filt_grad.reshape(2, seq_n, block), 0, 1)
    side = jnp.concatenate([small_sent, fg_sent.reshape(seq_n, -1)], axis=1).reshape(seq_n, -1, LANES)
    back, full, fg = tail_rounds(
        jnp.concatenate([prod_sent, dp_sent], axis=1), series[0], cotangent[0], side,
        grad_scale, per_group, dp_n,
    )
    prod_rows = jnp.transpose(back[:, :per], (2, 0, 1)).reshape(block, width)
    dp_rows = jnp.transpose(back[:, per:].reshape(seq_n, 3, per, block), (3, 1, 0, 2))
    dp_rows = dp_rows.reshape(block, 3 * width)
    output = jnp.dot(prod_rows, w_out, preferred_element_type=jnp.float32).astype(jnp.bfloat16)
    output = output.reshape(1, block, width)
    d_series = jnp.einsum(
        "tc,dc->td", dp_rows, w_in, preferred_element_type=jnp.float32
    ).astype(jnp.bfloat16)
    d_series = d_series.reshape(1, block, width)

    fg_blocks = jnp.swapaxes(fg.reshape(filters, 2, block), 0, 1)
    grad_w_in = jnp.transpose(full[:, : 3 * per].reshape(seq_n, 3, per, width), (3, 1, 0, 2))
    grad_w_in = grad_w_in.reshape(width, 3 * width)
    grad_w_out = full[:, 3 * per : 4 * per].reshape(width, width)
    small_all = full[:, 4 * per :].reshape(seq_n, -1)[:, : 3 * 4 * per].reshape(seq_n, 3, 4, per)
    small_all = jnp.transpose(small_all, (1, 2, 0, 3)).reshape(3, 4, width)
    grad_taps = small_all[:, :3].reshape(3, 3 * width)
    grad_skip_one = small_all[0, 3]
    grad_skip_two = small_all[1, 3]

    return (
        output,
        d_series,
        grad_w_in,
        grad_w_out,
        grad_taps,
        grad_skip_one,
        grad_skip_two,
        fg_blocks[0],
        fg_blocks[1],
    )


def solution(mesh):
    in_specs = (
        P("dp", "seq", None),
        P("dp", "seq", None),
        P(),
        P(),
        P(),
        P(),
        P(),
        P(None, "seq"),
        P(None, "seq"),
    )
    out_specs = (
        P("dp", "seq", None),
        P("dp", "seq", None),
        P(),
        P(),
        P(),
        P(),
        P(),
        P(None, "seq"),
        P(None, "seq"),
    )
    return jax.shard_map(shards, mesh=mesh, in_specs=in_specs, out_specs=out_specs, check_vma=False)
```

```python
import math

import numpy as np

import jax
import jax.numpy as jnp
from jax import lax
from jax.experimental import pallas as pl
from jax.experimental.pallas import tpu as pltpu
from jax.sharding import PartitionSpec as P

PRECISION = lax.Precision.HIGH
LANES = 128


def dft_tables(length):
    size = 2 * length
    rows = size // LANES
    half = length // LANES
    k1 = np.arange(rows)
    f1 = np.exp(-2j * np.pi * (np.outer(k1, np.arange(half)) % rows) / rows)
    turn = np.exp(-2j * np.pi * np.outer(k1, np.arange(LANES)) / size)
    f2 = np.exp(-2j * np.pi * (np.outer(np.arange(LANES), np.arange(LANES)) % LANES) / LANES)
    fwd1 = np.concatenate([f1.real, f1.imag], axis=0)
    fwd2 = np.block([[f2.real, f2.imag], [-f2.imag, f2.real]])
    inv2 = np.block([[f2.real, -f2.imag], [f2.imag, f2.real]])
    inv1 = np.concatenate([f1.real.T, f1.imag.T], axis=1) / size
    as32 = lambda a: jnp.asarray(np.asarray(a, np.float32))
    return {
        "rows": rows,
        "fwd1": as32(fwd1),
        "fwd2": as32(fwd2),
        "inv1": as32(inv1),
        "inv2": as32(inv2),
        "turn_r": as32(turn.real)[:, None, :],
        "turn_i": as32(turn.imag)[:, None, :],
    }


def spectrum(x, tab):
    rows = tab["rows"]
    a = jnp.einsum("kn,ncm->kcm", tab["fwd1"], x, precision=PRECISION)
    ar, ai = a[:rows], a[rows:]
    tr, ti = tab["turn_r"], tab["turn_i"]
    cat = jnp.concatenate([ar * tr - ai * ti, ar * ti + ai * tr], axis=-1)
    return jnp.einsum("kcm,mj->kcj", cat, tab["fwd2"], precision=PRECISION)


def signal(s, tab):
    b = jnp.einsum("kcj,jm->kcm", s, tab["inv2"], precision=PRECISION)
    br, bi = b[..., :LANES], b[..., LANES:]
    tr, ti = tab["turn_r"], tab["turn_i"]
    stacked = jnp.concatenate([br * tr + bi * ti, bi * tr - br * ti], axis=0)
    return jnp.einsum("nk,kcm->ncm", tab["inv1"], stacked, precision=PRECISION)


def cmul(a, b, conj=False):
    ar, ai = a[..., :LANES], a[..., LANES:]
    br, bi = b[..., :LANES], b[..., LANES:]
    if conj:
        bi = -bi
    return jnp.concatenate([ar * br - ai * bi, ar * bi + ai * br], axis=-1)


def fold(x):
    c, length = x.shape
    return jnp.swapaxes(x.reshape(c, length // LANES, LANES), 0, 1)


def unfold(x):
    half, c, lanes = x.shape
    return jnp.swapaxes(x, 0, 1).reshape(c, half * lanes)


def tail_rounds(out_msg, series_blk, cot_blk, side, scale, pair, dp_n):
    seq_n, out_rows, block = out_msg.shape
    per = out_rows // 4
    width = series_blk.shape[1]
    side_rows = side.shape[1]
    filter_rows = side_rows // 2
    param_rows = 3 * per + per + filter_rows
    msg_rows = param_rows + filter_rows
    groups = seq_n // pair
    ag_rows = param_rows + groups * filter_rows
    mesh = pl.DeviceIdType.MESH

    def kernel(out_ref, ser_ref, cot_ref, side_ref, back_ref, full_ref, fg_ref,
               msg_buf, rs_buf, ag_buf, sems):
        ms = lax.axis_index("seq")
        md = lax.axis_index("dp")
        barrier = pltpu.get_barrier_semaphore()
        for k in range(1, seq_n):
            pl.semaphore_signal(barrier, inc=1, device_id=(md, lax.rem(ms + k, seq_n)), device_id_type=mesh)
        for k in range(1, dp_n):
            pl.semaphore_signal(barrier, inc=1, device_id=(lax.rem(md + k, dp_n), ms), device_id_type=mesh)
        pl.semaphore_wait(barrier, seq_n + dp_n - 2)

        def send_all(count, src, dst, stage, where):
            copies = []
            for k in range(1, count):
                copy = pltpu.make_async_remote_copy(
                    src_ref=src(k), dst_ref=dst, send_sem=sems.at[stage, 0, k],
                    recv_sem=sems.at[stage, 1, k], device_id=where(k), device_id_type=mesh,
                )
                copy.start()
                copies.append(copy)
            return copies

        seq_peer = lambda k: (md, lax.rem(ms + k, seq_n))
        dp_peer = lambda k: (lax.rem(md + k, dp_n), ms)

        copies = send_all(seq_n, lambda k: out_ref.at[lax.rem(ms + k, seq_n)], back_ref.at[ms], 3, seq_peer)
        back_ref[pl.ds(ms, 1)] = out_ref[pl.ds(ms, 1)]
        for copy in copies:
            copy.wait()
        ser = ser_ref[...].astype(jnp.float32)
        cot = cot_ref[...].astype(jnp.float32)
        for j in range(seq_n):
            rows = back_ref[j].astype(jnp.float32)
            msg_buf[j, : 3 * per] = scale * jnp.dot(rows[per:], ser, preferred_element_type=jnp.float32)
            msg_buf[j, 3 * per : 4 * per] = scale * jnp.dot(rows[:per], cot, preferred_element_type=jnp.float32)
        msg_buf[:, 4 * per :] = side_ref[...]

        copies = send_all(seq_n, lambda k: msg_buf.at[lax.rem(ms + k, seq_n)], rs_buf.at[ms], 0, seq_peer)
        rs_buf[pl.ds(ms, 1)] = msg_buf[pl.ds(ms, 1)]
        for copy in copies:
            copy.wait()
        got = rs_buf[...]
        p_sum = jnp.sum(got[:, :param_rows], axis=0)
        f_sum = jnp.sum(got[:, param_rows:].reshape(groups, pair, filter_rows, width), axis=1)
        mine = jnp.concatenate([p_sum, f_sum.reshape(groups * filter_rows, width)], axis=0)

        ag_buf[pl.ds(md, 1)] = mine[None]
        copies = send_all(dp_n, lambda k: ag_buf.at[md], ag_buf.at[md], 1, dp_peer)
        for copy in copies:
            copy.wait()
        total = jnp.sum(ag_buf[...], axis=0)
        fg_ref[...] = total[param_rows:].reshape(groups, filter_rows, width)

        full_ref[pl.ds(ms, 1)] = total[:param_rows][None]
        copies = send_all(seq_n, lambda k: full_ref.at[ms], full_ref.at[ms], 2, seq_peer)
        for copy in copies:
            copy.wait()

    vmem = pl.BlockSpec(memory_space=pltpu.VMEM)
    return pl.pallas_call(
        kernel,
        out_shape=(
            jax.ShapeDtypeStruct(out_msg.shape, out_msg.dtype),
            jax.ShapeDtypeStruct((seq_n, param_rows, width), jnp.float32),
            jax.ShapeDtypeStruct((groups, filter_rows, width), jnp.float32),
        ),
        in_specs=[vmem] * 4,
        out_specs=(vmem, vmem, vmem),
        scratch_shapes=[
            pltpu.VMEM((seq_n, msg_rows, width), jnp.float32),
            pltpu.VMEM((seq_n, msg_rows, width), jnp.float32),
            pltpu.VMEM((dp_n, ag_rows, width), jnp.float32),
            pltpu.SemaphoreType.DMA((4, 2, max(seq_n, dp_n))),
        ],
        compiler_params=pltpu.CompilerParams(collective_id=0, has_side_effects=True),
    )(out_msg, series_blk, cot_blk, side)


def shards(series, cotangent, w_in, w_out, taps, skip_one, skip_two, filter_one, filter_two):
    _, block, width = series.shape
    seq_n = lax.axis_size("seq")
    dp_n = lax.axis_size("dp")
    length = block * seq_n
    half = length // LANES
    me = lax.axis_index("seq")
    per = width // seq_n
    filters = filter_one.shape[0]
    group_width = width // filters
    per_group = group_width // per
    group = me // per_group
    grad_scale = 1.0 / math.sqrt(dp_n * series.shape[0] * length)
    tab = dft_tables(length)

    taps_sel = lax.dynamic_index_in_dim(
        taps.reshape(3, 3, seq_n, per), me, axis=2, keepdims=False
    ).reshape(3, 3 * per)
    skip1 = lax.dynamic_index_in_dim(skip_one.reshape(seq_n, per), me, axis=0, keepdims=False)
    skip2 = lax.dynamic_index_in_dim(skip_two.reshape(seq_n, per), me, axis=0, keepdims=False)
    skip1 = skip1[None, :, None]
    skip2 = skip2[None, :, None]

    proj_blk = jnp.einsum("td,dc->ct", series[0], w_in, preferred_element_type=jnp.float32)
    proj_blk = jnp.swapaxes(proj_blk.reshape(3, seq_n, per, block), 0, 1).reshape(seq_n, 3 * per, block)
    dprod_blk = jnp.einsum("td,cd->ct", cotangent[0], w_out, preferred_element_type=jnp.float32)
    dprod_blk = dprod_blk.reshape(seq_n, per, block)
    rows_sent = jnp.repeat(jnp.swapaxes(jnp.stack([filter_one, filter_two]), 0, 1), per_group, axis=0)
    got = lax.all_to_all(
        jnp.concatenate([proj_blk, dprod_blk, rows_sent], axis=1), "seq", 0, 0, tiled=True
    )
    proj = jnp.swapaxes(got[:, : 3 * per], 0, 1).reshape(3 * per, length)
    d_product = jnp.swapaxes(
        got[:, 3 * per : 4 * per].reshape(seq_n, per, block // LANES, LANES), 1, 2
    ).reshape(half, per, LANES)
    h_rows = jnp.swapaxes(got[:, 4 * per :], 0, 1).reshape(2, length)
    prev1 = jnp.pad(proj, ((0, 0), (1, 0)))[:, :length]
    prev2 = jnp.pad(proj, ((0, 0), (2, 0)))[:, :length]
    conv = taps_sel[0][:, None] * proj + taps_sel[1][:, None] * prev1 + taps_sel[2][:, None] * prev2
    conv_f = fold(conv)
    value = conv_f[:, :per]
    gate_one = conv_f[:, per : 2 * per]
    gate_two = conv_f[:, 2 * per :]


    grad_two = d_product * gate_two
    h_spec = spectrum(fold(h_rows), tab)
    h_one = h_spec[:, 0:1]
    h_two = h_spec[:, 1:2]
    first = spectrum(jnp.concatenate([value, grad_two], axis=1), tab)
    v_spec = first[:, :per]
    g2_spec = first[:, per:]
    second = signal(
        jnp.concatenate([cmul(v_spec, h_one), cmul(g2_spec, h_two, conj=True)], axis=1), tab
    )
    y_one = second[:, :per] + skip1 * value
    d_mid = second[:, per:] + skip2 * grad_two
    gated_mid = gate_one * y_one
    grad_one = d_mid * gate_one
    d_gate_one = d_mid * y_one
    third = spectrum(jnp.concatenate([gated_mid, grad_one], axis=1), tab)
    m_spec = third[:, :per]
    g1_spec = third[:, per:]
    corr = jnp.concatenate(
        [
            jnp.sum(cmul(g1_spec, v_spec, conj=True), axis=1, keepdims=True),
            jnp.sum(cmul(g2_spec, m_spec, conj=True), axis=1, keepdims=True),
        ],
        axis=1,
    )
    last = signal(jnp.concatenate([cmul(m_spec, h_two), cmul(g1_spec, h_one, conj=True)], axis=1), tab)
    y_two = last[:, :per] + skip2 * gated_mid
    product = (gate_two * y_two).astype(jnp.bfloat16)
    d_gate_two = d_product * y_two
    d_value = last[:, per : 2 * per] + skip1 * grad_one
    filt_grad = unfold(signal(corr, tab))

    d_conv = unfold(jnp.concatenate([d_value, d_gate_one, d_gate_two], axis=1))
    next1 = jnp.pad(d_conv, ((0, 0), (0, 1)))[:, 1:]
    next2 = jnp.pad(d_conv, ((0, 0), (0, 2)))[:, 2:]
    d_proj = (
        taps_sel[0][:, None] * d_conv + taps_sel[1][:, None] * next1 + taps_sel[2][:, None] * next2
    ).astype(jnp.bfloat16)

    local_taps = jnp.stack(
        [jnp.sum(d_conv * proj, axis=1), jnp.sum(d_conv * prev1, axis=1), jnp.sum(d_conv * prev2, axis=1)]
    )
    local_skip1 = jnp.sum(grad_one * value, axis=(0, 2))
    local_skip2 = jnp.sum(grad_two * gated_mid, axis=(0, 2))
    prod_sent = jnp.swapaxes(product.reshape(seq_n, half // seq_n, per, LANES), 1, 2)
    prod_sent = prod_sent.reshape(seq_n, per, block)
    dp_sent = jnp.swapaxes(d_proj.reshape(3 * per, seq_n, block), 0, 1)
    small = jnp.concatenate(
        [
            local_taps.reshape(3, 3, 1, per),
            jnp.stack([local_skip1, local_skip2, jnp.zeros_like(local_skip1)]).reshape(3, 1, 1, per),
        ],
        axis=1,
    )
    small_full = lax.dynamic_update_slice(
        jnp.zeros((3, 4, seq_n, per), jnp.float32), small, (0, 0, me, 0)
    )
    small_sent = jnp.transpose(grad_scale * small_full, (2, 0, 1, 3)).reshape(seq_n, -1)
    small_sent = jnp.pad(small_sent, ((0, 0), (0, 2 * block - small_sent.shape[1])))
    fg_sent = jnp.swapaxes(grad_scale * filt_grad.reshape(2, seq_n, block), 0, 1)
    side = jnp.concatenate([small_sent, fg_sent.reshape(seq_n, -1)], axis=1).reshape(seq_n, -1, LANES)
    back, full, fg = tail_rounds(
        jnp.concatenate([prod_sent, dp_sent], axis=1), series[0], cotangent[0], side,
        grad_scale, per_group, dp_n,
    )
    prod_rows = jnp.transpose(back[:, :per], (2, 0, 1)).reshape(block, width)
    dp_rows = jnp.transpose(back[:, per:].reshape(seq_n, 3, per, block), (3, 1, 0, 2))
    dp_rows = dp_rows.reshape(block, 3 * width)
    output = jnp.dot(prod_rows, w_out, preferred_element_type=jnp.float32).astype(jnp.bfloat16)
    output = output.reshape(1, block, width)
    d_series = jnp.einsum(
        "tc,dc->td", dp_rows, w_in, preferred_element_type=jnp.float32
    ).astype(jnp.bfloat16)
    d_series = d_series.reshape(1, block, width)

    fg_blocks = jnp.swapaxes(fg.reshape(filters, 2, block), 0, 1)
    grad_w_in = jnp.transpose(full[:, : 3 * per].reshape(seq_n, 3, per, width), (3, 1, 0, 2))
    grad_w_in = grad_w_in.reshape(width, 3 * width)
    grad_w_out = full[:, 3 * per : 4 * per].reshape(width, width)
    small_all = full[:, 4 * per :].reshape(seq_n, -1)[:, : 3 * 4 * per].reshape(seq_n, 3, 4, per)
    small_all = jnp.transpose(small_all, (1, 2, 0, 3)).reshape(3, 4, width)
    grad_taps = small_all[:, :3].reshape(3, 3 * width)
    grad_skip_one = small_all[0, 3]
    grad_skip_two = small_all[1, 3]

    return (
        output,
        d_series,
        grad_w_in,
        grad_w_out,
        grad_taps,
        grad_skip_one,
        grad_skip_two,
        fg_blocks[0],
        fg_blocks[1],
    )


def solution(mesh):
    in_specs = (
        P("dp", "seq", None),
        P("dp", "seq", None),
        P(),
        P(),
        P(),
        P(),
        P(),
        P(None, "seq"),
        P(None, "seq"),
    )
    out_specs = (
        P("dp", "seq", None),
        P("dp", "seq", None),
        P(),
        P(),
        P(),
        P(),
        P(),
        P(None, "seq"),
        P(None, "seq"),
    )
    return jax.shard_map(shards, mesh=mesh, in_specs=in_specs, out_specs=out_specs, check_vma=False)
```

```python
import math

import numpy as np

import jax
import jax.numpy as jnp
from jax import lax
from jax.experimental import pallas as pl
from jax.experimental.pallas import tpu as pltpu
from jax.sharding import PartitionSpec as P

PRECISION = lax.Precision.HIGH
LANES = 128


def dft_tables(length):
    size = 2 * length
    rows = size // LANES
    half = length // LANES
    k1 = np.arange(rows)
    f1 = np.exp(-2j * np.pi * (np.outer(k1, np.arange(half)) % rows) / rows)
    turn = np.exp(-2j * np.pi * np.outer(k1, np.arange(LANES)) / size)
    f2 = np.exp(-2j * np.pi * (np.outer(np.arange(LANES), np.arange(LANES)) % LANES) / LANES)
    fwd1 = np.concatenate([f1.real, f1.imag], axis=0)
    fwd2 = np.block([[f2.real, f2.imag], [-f2.imag, f2.real]])
    inv2 = np.block([[f2.real, -f2.imag], [f2.imag, f2.real]])
    inv1 = np.concatenate([f1.real.T, f1.imag.T], axis=1) / size
    as32 = lambda a: jnp.asarray(np.asarray(a, np.float32))
    return {
        "rows": rows,
        "fwd1": as32(fwd1),
        "fwd2": as32(fwd2),
        "inv1": as32(inv1),
        "inv2": as32(inv2),
        "turn_r": as32(turn.real)[:, None, :],
        "turn_i": as32(turn.imag)[:, None, :],
    }


def spectrum(x, tab):
    rows = tab["rows"]
    a = jnp.einsum("kn,ncm->kcm", tab["fwd1"], x, precision=PRECISION)
    ar, ai = a[:rows], a[rows:]
    tr, ti = tab["turn_r"], tab["turn_i"]
    cat = jnp.concatenate([ar * tr - ai * ti, ar * ti + ai * tr], axis=-1)
    return jnp.einsum("kcm,mj->kcj", cat, tab["fwd2"], precision=PRECISION)


def signal(s, tab):
    b = jnp.einsum("kcj,jm->kcm", s, tab["inv2"], precision=PRECISION)
    br, bi = b[..., :LANES], b[..., LANES:]
    tr, ti = tab["turn_r"], tab["turn_i"]
    stacked = jnp.concatenate([br * tr + bi * ti, bi * tr - br * ti], axis=0)
    return jnp.einsum("nk,kcm->ncm", tab["inv1"], stacked, precision=PRECISION)


def cmul(a, b, conj=False):
    ar, ai = a[..., :LANES], a[..., LANES:]
    br, bi = b[..., :LANES], b[..., LANES:]
    if conj:
        bi = -bi
    return jnp.concatenate([ar * br - ai * bi, ar * bi + ai * br], axis=-1)


def fold(x):
    c, length = x.shape
    return jnp.swapaxes(x.reshape(c, length // LANES, LANES), 0, 1)


def unfold(x):
    half, c, lanes = x.shape
    return jnp.swapaxes(x, 0, 1).reshape(c, half * lanes)


def tail_rounds(out_msg, series_blk, cot_blk, side, scale, pair, dp_n):
    seq_n, out_rows, block = out_msg.shape
    per = out_rows // 4
    width = series_blk.shape[1]
    side_rows = side.shape[1]
    filter_rows = side_rows // 2
    param_rows = 3 * per + per + filter_rows
    msg_rows = param_rows + filter_rows
    groups = seq_n // pair
    ag_rows = param_rows + groups * filter_rows
    mesh = pl.DeviceIdType.MESH

    def kernel(out_ref, ser_ref, cot_ref, side_ref, back_ref, full_ref, fg_ref,
               msg_buf, rs_buf, ag_buf, sems):
        ms = lax.axis_index("seq")
        md = lax.axis_index("dp")
        barrier = pltpu.get_barrier_semaphore()
        for k in range(1, seq_n):
            pl.semaphore_signal(barrier, inc=1, device_id=(md, lax.rem(ms + k, seq_n)), device_id_type=mesh)
        for k in range(1, dp_n):
            pl.semaphore_signal(barrier, inc=1, device_id=(lax.rem(md + k, dp_n), ms), device_id_type=mesh)
        pl.semaphore_wait(barrier, seq_n + dp_n - 2)

        def send_all(count, src, dst, stage, where):
            copies = []
            for k in range(1, count):
                copy = pltpu.make_async_remote_copy(
                    src_ref=src(k), dst_ref=dst, send_sem=sems.at[stage, 0, k],
                    recv_sem=sems.at[stage, 1, k], device_id=where(k), device_id_type=mesh,
                )
                copy.start()
                copies.append(copy)
            return copies

        seq_peer = lambda k: (md, lax.rem(ms + k, seq_n))
        dp_peer = lambda k: (lax.rem(md + k, dp_n), ms)

        copies = send_all(seq_n, lambda k: out_ref.at[lax.rem(ms + k, seq_n)], back_ref.at[ms], 3, seq_peer)
        back_ref[pl.ds(ms, 1)] = out_ref[pl.ds(ms, 1)]
        for copy in copies:
            copy.wait()
        ser = ser_ref[...].astype(jnp.float32)
        cot = cot_ref[...].astype(jnp.float32)
        for j in range(seq_n):
            rows = back_ref[j].astype(jnp.float32)
            msg_buf[j, : 3 * per] = scale * jnp.dot(rows[per:], ser, preferred_element_type=jnp.float32)
            msg_buf[j, 3 * per : 4 * per] = scale * jnp.dot(rows[:per], cot, preferred_element_type=jnp.float32)
        msg_buf[:, 4 * per :] = side_ref[...]

        copies = send_all(seq_n, lambda k: msg_buf.at[lax.rem(ms + k, seq_n)], rs_buf.at[ms], 0, seq_peer)
        rs_buf[pl.ds(ms, 1)] = msg_buf[pl.ds(ms, 1)]
        for copy in copies:
            copy.wait()
        got = rs_buf[...]
        p_sum = jnp.sum(got[:, :param_rows], axis=0)
        f_sum = jnp.sum(got[:, param_rows:].reshape(groups, pair, filter_rows, width), axis=1)
        mine = jnp.concatenate([p_sum, f_sum.reshape(groups * filter_rows, width)], axis=0)

        ag_buf[pl.ds(md, 1)] = mine[None]
        copies = send_all(dp_n, lambda k: ag_buf.at[md], ag_buf.at[md], 1, dp_peer)
        for copy in copies:
            copy.wait()
        total = jnp.sum(ag_buf[...], axis=0)
        fg_ref[...] = total[param_rows:].reshape(groups, filter_rows, width)

        full_ref[pl.ds(ms, 1)] = total[:param_rows][None]
        copies = send_all(seq_n, lambda k: full_ref.at[ms], full_ref.at[ms], 2, seq_peer)
        for copy in copies:
            copy.wait()

    vmem = pl.BlockSpec(memory_space=pltpu.VMEM)
    return pl.pallas_call(
        kernel,
        out_shape=(
            jax.ShapeDtypeStruct(out_msg.shape, out_msg.dtype),
            jax.ShapeDtypeStruct((seq_n, param_rows, width), jnp.float32),
            jax.ShapeDtypeStruct((groups, filter_rows, width), jnp.float32),
        ),
        in_specs=[vmem] * 4,
        out_specs=(vmem, vmem, vmem),
        scratch_shapes=[
            pltpu.VMEM((seq_n, msg_rows, width), jnp.float32),
            pltpu.VMEM((seq_n, msg_rows, width), jnp.float32),
            pltpu.VMEM((dp_n, ag_rows, width), jnp.float32),
            pltpu.SemaphoreType.DMA((4, 2, max(seq_n, dp_n))),
        ],
        compiler_params=pltpu.CompilerParams(collective_id=0, has_side_effects=True),
    )(out_msg, series_blk, cot_blk, side)


def shards(series, cotangent, w_in, w_out, taps, skip_one, skip_two, filter_one, filter_two):
    _, block, width = series.shape
    seq_n = lax.axis_size("seq")
    dp_n = lax.axis_size("dp")
    length = block * seq_n
    half = length // LANES
    me = lax.axis_index("seq")
    per = width // seq_n
    filters = filter_one.shape[0]
    group_width = width // filters
    per_group = group_width // per
    group = me // per_group
    grad_scale = 1.0 / math.sqrt(dp_n * series.shape[0] * length)
    tab = dft_tables(length)

    taps_sel = lax.dynamic_index_in_dim(
        taps.reshape(3, 3, seq_n, per), me, axis=2, keepdims=False
    ).reshape(3, 3 * per)
    skip1 = lax.dynamic_index_in_dim(skip_one.reshape(seq_n, per), me, axis=0, keepdims=False)
    skip2 = lax.dynamic_index_in_dim(skip_two.reshape(seq_n, per), me, axis=0, keepdims=False)
    skip1 = skip1[None, :, None]
    skip2 = skip2[None, :, None]

    proj_blk = jnp.einsum("td,dc->ct", series[0], w_in, preferred_element_type=jnp.float32)
    proj_blk = jnp.swapaxes(proj_blk.reshape(3, seq_n, per, block), 0, 1).reshape(seq_n, 3 * per, block)
    dprod_blk = jnp.einsum("td,cd->ct", cotangent[0], w_out, preferred_element_type=jnp.float32)
    dprod_blk = dprod_blk.reshape(seq_n, per, block)
    rows_sent = jnp.repeat(jnp.swapaxes(jnp.stack([filter_one, filter_two]), 0, 1), per_group, axis=0)
    got = lax.all_to_all(
        jnp.concatenate([proj_blk, dprod_blk, rows_sent], axis=1), "seq", 0, 0, tiled=True
    )
    proj = jnp.swapaxes(got[:, : 3 * per], 0, 1).reshape(3 * per, length)
    d_product = jnp.swapaxes(
        got[:, 3 * per : 4 * per].reshape(seq_n, per, block // LANES, LANES), 1, 2
    ).reshape(half, per, LANES)
    h_rows = jnp.swapaxes(got[:, 4 * per :], 0, 1).reshape(2, length)
    prev1 = jnp.pad(proj, ((0, 0), (1, 0)))[:, :length]
    prev2 = jnp.pad(proj, ((0, 0), (2, 0)))[:, :length]
    conv = taps_sel[0][:, None] * proj + taps_sel[1][:, None] * prev1 + taps_sel[2][:, None] * prev2
    conv_f = fold(conv)
    value = conv_f[:, :per]
    gate_one = conv_f[:, per : 2 * per]
    gate_two = conv_f[:, 2 * per :]


    both_spec = spectrum(jnp.concatenate([value, fold(h_rows)], axis=1), tab)
    v_spec = both_spec[:, :per]
    h_one = both_spec[:, per : per + 1]
    h_two = both_spec[:, per + 1 : per + 2]
    y_one = signal(cmul(v_spec, h_one), tab) + skip1 * value
    gated_mid = gate_one * y_one
    grad_two = d_product * gate_two
    pair_spec = spectrum(jnp.concatenate([gated_mid, grad_two], axis=1), tab)
    m_spec = pair_spec[:, :per]
    g2_spec = pair_spec[:, per:]
    pair_sig = signal(
        jnp.concatenate([cmul(m_spec, h_two), cmul(g2_spec, h_two, conj=True)], axis=1), tab
    )
    y_two = pair_sig[:, :per] + skip2 * gated_mid
    product = (gate_two * y_two).astype(jnp.bfloat16)
    d_gate_two = d_product * y_two
    d_mid = pair_sig[:, per:] + skip2 * grad_two
    grad_one = d_mid * gate_one
    d_gate_one = d_mid * y_one
    g1_spec = spectrum(grad_one, tab)
    corr = jnp.concatenate(
        [
            jnp.sum(cmul(g1_spec, v_spec, conj=True), axis=1, keepdims=True),
            jnp.sum(cmul(g2_spec, m_spec, conj=True), axis=1, keepdims=True),
        ],
        axis=1,
    )
    last = signal(jnp.concatenate([cmul(g1_spec, h_one, conj=True), corr], axis=1), tab)
    d_value = last[:, :per] + skip1 * grad_one
    filt_grad = unfold(last[:, per:])

    d_conv = unfold(jnp.concatenate([d_value, d_gate_one, d_gate_two], axis=1))
    next1 = jnp.pad(d_conv, ((0, 0), (0, 1)))[:, 1:]
    next2 = jnp.pad(d_conv, ((0, 0), (0, 2)))[:, 2:]
    d_proj = (
        taps_sel[0][:, None] * d_conv + taps_sel[1][:, None] * next1 + taps_sel[2][:, None] * next2
    ).astype(jnp.bfloat16)

    local_taps = jnp.stack(
        [jnp.sum(d_conv * proj, axis=1), jnp.sum(d_conv * prev1, axis=1), jnp.sum(d_conv * prev2, axis=1)]
    )
    local_skip1 = jnp.sum(grad_one * value, axis=(0, 2))
    local_skip2 = jnp.sum(grad_two * gated_mid, axis=(0, 2))
    prod_sent = jnp.swapaxes(product.reshape(seq_n, half // seq_n, per, LANES), 1, 2)
    prod_sent = prod_sent.reshape(seq_n, per, block)
    dp_sent = jnp.swapaxes(d_proj.reshape(3 * per, seq_n, block), 0, 1)
    small = jnp.concatenate(
        [
            local_taps.reshape(3, 3, 1, per),
            jnp.stack([local_skip1, local_skip2, jnp.zeros_like(local_skip1)]).reshape(3, 1, 1, per),
        ],
        axis=1,
    )
    small_full = lax.dynamic_update_slice(
        jnp.zeros((3, 4, seq_n, per), jnp.float32), small, (0, 0, me, 0)
    )
    small_sent = jnp.transpose(grad_scale * small_full, (2, 0, 1, 3)).reshape(seq_n, -1)
    small_sent = jnp.pad(small_sent, ((0, 0), (0, 2 * block - small_sent.shape[1])))
    fg_sent = jnp.swapaxes(grad_scale * filt_grad.reshape(2, seq_n, block), 0, 1)
    side = jnp.concatenate([small_sent, fg_sent.reshape(seq_n, -1)], axis=1).reshape(seq_n, -1, LANES)
    back, full, fg = tail_rounds(
        jnp.concatenate([prod_sent, dp_sent], axis=1), series[0], cotangent[0], side,
        grad_scale, per_group, dp_n,
    )
    prod_rows = jnp.transpose(back[:, :per], (2, 0, 1)).reshape(block, width)
    dp_rows = jnp.transpose(back[:, per:].reshape(seq_n, 3, per, block), (3, 1, 0, 2))
    dp_rows = dp_rows.reshape(block, 3 * width)
    output = jnp.dot(prod_rows, w_out, preferred_element_type=jnp.float32).astype(jnp.bfloat16)
    output = output.reshape(1, block, width)
    d_series = jnp.einsum(
        "tc,dc->td", dp_rows, w_in, preferred_element_type=jnp.float32
    ).astype(jnp.bfloat16)
    d_series = d_series.reshape(1, block, width)

    fg_blocks = jnp.swapaxes(fg.reshape(filters, 2, block), 0, 1)
    grad_w_in = jnp.transpose(full[:, : 3 * per].reshape(seq_n, 3, per, width), (3, 1, 0, 2))
    grad_w_in = grad_w_in.reshape(width, 3 * width)
    grad_w_out = full[:, 3 * per : 4 * per].reshape(width, width)
    small_all = full[:, 4 * per :].reshape(seq_n, -1)[:, : 3 * 4 * per].reshape(seq_n, 3, 4, per)
    small_all = jnp.transpose(small_all, (1, 2, 0, 3)).reshape(3, 4, width)
    grad_taps = small_all[:, :3].reshape(3, 3 * width)
    grad_skip_one = small_all[0, 3]
    grad_skip_two = small_all[1, 3]

    return (
        output,
        d_series,
        grad_w_in,
        grad_w_out,
        grad_taps,
        grad_skip_one,
        grad_skip_two,
        fg_blocks[0],
        fg_blocks[1],
    )


def solution(mesh):
    in_specs = (
        P("dp", "seq", None),
        P("dp", "seq", None),
        P(),
        P(),
        P(),
        P(),
        P(),
        P(None, "seq"),
        P(None, "seq"),
    )
    out_specs = (
        P("dp", "seq", None),
        P("dp", "seq", None),
        P(),
        P(),
        P(),
        P(),
        P(),
        P(None, "seq"),
        P(None, "seq"),
    )
    return jax.shard_map(shards, mesh=mesh, in_specs=in_specs, out_specs=out_specs, check_vma=False)
```

```python
import math

import numpy as np

import jax
import jax.numpy as jnp
from jax import lax
from jax.experimental import pallas as pl
from jax.experimental.pallas import tpu as pltpu
from jax.sharding import PartitionSpec as P

PRECISION = lax.Precision.HIGH
LANES = 128


def dft_tables(length):
    size = 2 * length
    rows = size // LANES
    half = length // LANES
    k1 = np.arange(rows)
    f1 = np.exp(-2j * np.pi * (np.outer(k1, np.arange(half)) % rows) / rows)
    turn = np.exp(-2j * np.pi * np.outer(k1, np.arange(LANES)) / size)
    f2 = np.exp(-2j * np.pi * (np.outer(np.arange(LANES), np.arange(LANES)) % LANES) / LANES)
    fwd1 = np.concatenate([f1.real, f1.imag], axis=0)
    fwd2 = np.block([[f2.real, f2.imag], [-f2.imag, f2.real]])
    inv2 = np.block([[f2.real, -f2.imag], [f2.imag, f2.real]])
    inv1 = np.concatenate([f1.real.T, f1.imag.T], axis=1) / size
    as32 = lambda a: jnp.asarray(np.asarray(a, np.float32))
    return {
        "rows": rows,
        "fwd1": as32(fwd1),
        "fwd2": as32(fwd2),
        "inv1": as32(inv1),
        "inv2": as32(inv2),
        "turn_r": as32(turn.real)[:, None, :],
        "turn_i": as32(turn.imag)[:, None, :],
    }


def spectrum(x, tab):
    rows = tab["rows"]
    a = jnp.einsum("kn,ncm->kcm", tab["fwd1"], x, precision=PRECISION)
    ar, ai = a[:rows], a[rows:]
    tr, ti = tab["turn_r"], tab["turn_i"]
    cat = jnp.concatenate([ar * tr - ai * ti, ar * ti + ai * tr], axis=-1)
    return jnp.einsum("kcm,mj->kcj", cat, tab["fwd2"], precision=PRECISION)


def signal(s, tab):
    b = jnp.einsum("kcj,jm->kcm", s, tab["inv2"], precision=PRECISION)
    br, bi = b[..., :LANES], b[..., LANES:]
    tr, ti = tab["turn_r"], tab["turn_i"]
    stacked = jnp.concatenate([br * tr + bi * ti, bi * tr - br * ti], axis=0)
    return jnp.einsum("nk,kcm->ncm", tab["inv1"], stacked, precision=PRECISION)


def cmul(a, b, conj=False):
    ar, ai = a[..., :LANES], a[..., LANES:]
    br, bi = b[..., :LANES], b[..., LANES:]
    if conj:
        bi = -bi
    return jnp.concatenate([ar * br - ai * bi, ar * bi + ai * br], axis=-1)


def fold(x):
    c, length = x.shape
    return jnp.swapaxes(x.reshape(c, length // LANES, LANES), 0, 1)


def unfold(x):
    half, c, lanes = x.shape
    return jnp.swapaxes(x, 0, 1).reshape(c, half * lanes)


def tail_rounds(out_msg, series_blk, cot_blk, side, scale, pair, dp_n):
    seq_n, out_rows, block = out_msg.shape
    per = out_rows // 4
    width = series_blk.shape[1]
    side_rows = side.shape[1]
    filter_rows = side_rows // 2
    param_rows = 3 * per + per + filter_rows
    msg_rows = param_rows + filter_rows
    groups = seq_n // pair
    ag_rows = param_rows + groups * filter_rows
    mesh = pl.DeviceIdType.MESH

    def kernel(out_ref, ser_ref, cot_ref, side_ref, back_ref, full_ref, fg_ref,
               msg_buf, rs_buf, ag_buf, sems):
        ms = lax.axis_index("seq")
        md = lax.axis_index("dp")
        barrier = pltpu.get_barrier_semaphore()
        for k in range(1, seq_n):
            pl.semaphore_signal(barrier, inc=1, device_id=(md, lax.rem(ms + k, seq_n)), device_id_type=mesh)
        for k in range(1, dp_n):
            pl.semaphore_signal(barrier, inc=1, device_id=(lax.rem(md + k, dp_n), ms), device_id_type=mesh)
        pl.semaphore_wait(barrier, seq_n + dp_n - 2)

        def send_all(count, src, dst, stage, where):
            copies = []
            for k in range(1, count):
                copy = pltpu.make_async_remote_copy(
                    src_ref=src(k), dst_ref=dst, send_sem=sems.at[stage, 0, k],
                    recv_sem=sems.at[stage, 1, k], device_id=where(k), device_id_type=mesh,
                )
                copy.start()
                copies.append(copy)
            return copies

        seq_peer = lambda k: (md, lax.rem(ms + k, seq_n))
        dp_peer = lambda k: (lax.rem(md + k, dp_n), ms)

        copies = send_all(seq_n, lambda k: out_ref.at[lax.rem(ms + k, seq_n)], back_ref.at[ms], 3, seq_peer)
        back_ref[pl.ds(ms, 1)] = out_ref[pl.ds(ms, 1)]
        for copy in copies:
            copy.wait()
        ser = ser_ref[...]
        cot = cot_ref[...]
        for j in range(seq_n):
            rows = back_ref[j].astype(jnp.float32)
            dp_rows = rows[per:].astype(ser.dtype)
            pr_rows = rows[:per].astype(cot.dtype)
            msg_buf[j, : 3 * per] = scale * jnp.dot(dp_rows, ser, preferred_element_type=jnp.float32)
            msg_buf[j, 3 * per : 4 * per] = scale * jnp.dot(pr_rows, cot, preferred_element_type=jnp.float32)
        msg_buf[:, 4 * per :] = side_ref[...]

        copies = send_all(seq_n, lambda k: msg_buf.at[lax.rem(ms + k, seq_n)], rs_buf.at[ms], 0, seq_peer)
        rs_buf[pl.ds(ms, 1)] = msg_buf[pl.ds(ms, 1)]
        for copy in copies:
            copy.wait()
        got = rs_buf[...]
        p_sum = jnp.sum(got[:, :param_rows], axis=0)
        f_sum = jnp.sum(got[:, param_rows:].reshape(groups, pair, filter_rows, width), axis=1)
        mine = jnp.concatenate([p_sum, f_sum.reshape(groups * filter_rows, width)], axis=0)

        ag_buf[pl.ds(md, 1)] = mine[None]
        copies = send_all(dp_n, lambda k: ag_buf.at[md], ag_buf.at[md], 1, dp_peer)
        for copy in copies:
            copy.wait()
        total = jnp.sum(ag_buf[...], axis=0)
        fg_ref[...] = total[param_rows:].reshape(groups, filter_rows, width)

        full_ref[pl.ds(ms, 1)] = total[:param_rows][None]
        copies = send_all(seq_n, lambda k: full_ref.at[ms], full_ref.at[ms], 2, seq_peer)
        for copy in copies:
            copy.wait()

    vmem = pl.BlockSpec(memory_space=pltpu.VMEM)
    return pl.pallas_call(
        kernel,
        out_shape=(
            jax.ShapeDtypeStruct(out_msg.shape, out_msg.dtype),
            jax.ShapeDtypeStruct((seq_n, param_rows, width), jnp.float32),
            jax.ShapeDtypeStruct((groups, filter_rows, width), jnp.float32),
        ),
        in_specs=[vmem] * 4,
        out_specs=(vmem, vmem, vmem),
        scratch_shapes=[
            pltpu.VMEM((seq_n, msg_rows, width), jnp.float32),
            pltpu.VMEM((seq_n, msg_rows, width), jnp.float32),
            pltpu.VMEM((dp_n, ag_rows, width), jnp.float32),
            pltpu.SemaphoreType.DMA((4, 2, max(seq_n, dp_n))),
        ],
        compiler_params=pltpu.CompilerParams(collective_id=0, has_side_effects=True),
    )(out_msg, series_blk, cot_blk, side)


def shards(series, cotangent, w_in, w_out, taps, skip_one, skip_two, filter_one, filter_two):
    _, block, width = series.shape
    seq_n = lax.axis_size("seq")
    dp_n = lax.axis_size("dp")
    length = block * seq_n
    half = length // LANES
    me = lax.axis_index("seq")
    per = width // seq_n
    filters = filter_one.shape[0]
    group_width = width // filters
    per_group = group_width // per
    group = me // per_group
    grad_scale = 1.0 / math.sqrt(dp_n * series.shape[0] * length)
    tab = dft_tables(length)

    taps_sel = lax.dynamic_index_in_dim(
        taps.reshape(3, 3, seq_n, per), me, axis=2, keepdims=False
    ).reshape(3, 3 * per)
    skip1 = lax.dynamic_index_in_dim(skip_one.reshape(seq_n, per), me, axis=0, keepdims=False)
    skip2 = lax.dynamic_index_in_dim(skip_two.reshape(seq_n, per), me, axis=0, keepdims=False)
    skip1 = skip1[None, :, None]
    skip2 = skip2[None, :, None]

    proj_blk = jnp.einsum("td,dc->ct", series[0], w_in, preferred_element_type=jnp.float32)
    proj_blk = jnp.swapaxes(proj_blk.reshape(3, seq_n, per, block), 0, 1).reshape(seq_n, 3 * per, block)
    dprod_blk = jnp.einsum("td,cd->ct", cotangent[0], w_out, preferred_element_type=jnp.float32)
    dprod_blk = dprod_blk.reshape(seq_n, per, block)
    rows_sent = jnp.repeat(jnp.swapaxes(jnp.stack([filter_one, filter_two]), 0, 1), per_group, axis=0)
    got = lax.all_to_all(
        jnp.concatenate([proj_blk, dprod_blk, rows_sent], axis=1), "seq", 0, 0, tiled=True
    )
    proj = jnp.swapaxes(got[:, : 3 * per], 0, 1).reshape(3 * per, length)
    d_product = jnp.swapaxes(
        got[:, 3 * per : 4 * per].reshape(seq_n, per, block // LANES, LANES), 1, 2
    ).reshape(half, per, LANES)
    h_rows = jnp.swapaxes(got[:, 4 * per :], 0, 1).reshape(2, length)
    prev1 = jnp.pad(proj, ((0, 0), (1, 0)))[:, :length]
    prev2 = jnp.pad(proj, ((0, 0), (2, 0)))[:, :length]
    conv = taps_sel[0][:, None] * proj + taps_sel[1][:, None] * prev1 + taps_sel[2][:, None] * prev2
    conv_f = fold(conv)
    value = conv_f[:, :per]
    gate_one = conv_f[:, per : 2 * per]
    gate_two = conv_f[:, 2 * per :]


    both_spec = spectrum(jnp.concatenate([value, fold(h_rows)], axis=1), tab)
    v_spec = both_spec[:, :per]
    h_one = both_spec[:, per : per + 1]
    h_two = both_spec[:, per + 1 : per + 2]
    y_one = signal(cmul(v_spec, h_one), tab) + skip1 * value
    gated_mid = gate_one * y_one
    m_spec = spectrum(gated_mid, tab)
    y_two = signal(cmul(m_spec, h_two), tab) + skip2 * gated_mid
    product = (gate_two * y_two).astype(jnp.bfloat16)

    grad_two = d_product * gate_two
    d_gate_two = d_product * y_two
    g2_spec = spectrum(grad_two, tab)
    d_mid = signal(cmul(g2_spec, h_two, conj=True), tab) + skip2 * grad_two
    grad_one = d_mid * gate_one
    d_gate_one = d_mid * y_one
    g1_spec = spectrum(grad_one, tab)
    corr = jnp.concatenate(
        [
            jnp.sum(cmul(g1_spec, v_spec, conj=True), axis=1, keepdims=True),
            jnp.sum(cmul(g2_spec, m_spec, conj=True), axis=1, keepdims=True),
        ],
        axis=1,
    )
    last = signal(jnp.concatenate([cmul(g1_spec, h_one, conj=True), corr], axis=1), tab)
    d_value = last[:, :per] + skip1 * grad_one
    filt_grad = unfold(last[:, per:])

    d_conv = unfold(jnp.concatenate([d_value, d_gate_one, d_gate_two], axis=1))
    next1 = jnp.pad(d_conv, ((0, 0), (0, 1)))[:, 1:]
    next2 = jnp.pad(d_conv, ((0, 0), (0, 2)))[:, 2:]
    d_proj = (
        taps_sel[0][:, None] * d_conv + taps_sel[1][:, None] * next1 + taps_sel[2][:, None] * next2
    ).astype(jnp.bfloat16)

    local_taps = jnp.stack(
        [jnp.sum(d_conv * proj, axis=1), jnp.sum(d_conv * prev1, axis=1), jnp.sum(d_conv * prev2, axis=1)]
    )
    local_skip1 = jnp.sum(grad_one * value, axis=(0, 2))
    local_skip2 = jnp.sum(grad_two * gated_mid, axis=(0, 2))
    prod_sent = jnp.swapaxes(product.reshape(seq_n, half // seq_n, per, LANES), 1, 2)
    prod_sent = prod_sent.reshape(seq_n, per, block)
    dp_sent = jnp.swapaxes(d_proj.reshape(3 * per, seq_n, block), 0, 1)
    small = jnp.concatenate(
        [
            local_taps.reshape(3, 3, 1, per),
            jnp.stack([local_skip1, local_skip2, jnp.zeros_like(local_skip1)]).reshape(3, 1, 1, per),
        ],
        axis=1,
    )
    small_full = lax.dynamic_update_slice(
        jnp.zeros((3, 4, seq_n, per), jnp.float32), small, (0, 0, me, 0)
    )
    small_sent = jnp.transpose(grad_scale * small_full, (2, 0, 1, 3)).reshape(seq_n, -1)
    small_sent = jnp.pad(small_sent, ((0, 0), (0, 2 * block - small_sent.shape[1])))
    fg_sent = jnp.swapaxes(grad_scale * filt_grad.reshape(2, seq_n, block), 0, 1)
    side = jnp.concatenate([small_sent, fg_sent.reshape(seq_n, -1)], axis=1).reshape(seq_n, -1, LANES)
    back, full, fg = tail_rounds(
        jnp.concatenate([prod_sent, dp_sent], axis=1), series[0], cotangent[0], side,
        grad_scale, per_group, dp_n,
    )
    prod_rows = jnp.transpose(back[:, :per], (2, 0, 1)).reshape(block, width)
    dp_rows = jnp.transpose(back[:, per:].reshape(seq_n, 3, per, block), (3, 1, 0, 2))
    dp_rows = dp_rows.reshape(block, 3 * width)
    output = jnp.dot(prod_rows, w_out, preferred_element_type=jnp.float32).astype(jnp.bfloat16)
    output = output.reshape(1, block, width)
    d_series = jnp.einsum(
        "tc,dc->td", dp_rows, w_in, preferred_element_type=jnp.float32
    ).astype(jnp.bfloat16)
    d_series = d_series.reshape(1, block, width)

    fg_blocks = jnp.swapaxes(fg.reshape(filters, 2, block), 0, 1)
    grad_w_in = jnp.transpose(full[:, : 3 * per].reshape(seq_n, 3, per, width), (3, 1, 0, 2))
    grad_w_in = grad_w_in.reshape(width, 3 * width)
    grad_w_out = full[:, 3 * per : 4 * per].reshape(width, width)
    small_all = full[:, 4 * per :].reshape(seq_n, -1)[:, : 3 * 4 * per].reshape(seq_n, 3, 4, per)
    small_all = jnp.transpose(small_all, (1, 2, 0, 3)).reshape(3, 4, width)
    grad_taps = small_all[:, :3].reshape(3, 3 * width)
    grad_skip_one = small_all[0, 3]
    grad_skip_two = small_all[1, 3]

    return (
        output,
        d_series,
        grad_w_in,
        grad_w_out,
        grad_taps,
        grad_skip_one,
        grad_skip_two,
        fg_blocks[0],
        fg_blocks[1],
    )


def solution(mesh):
    in_specs = (
        P("dp", "seq", None),
        P("dp", "seq", None),
        P(),
        P(),
        P(),
        P(),
        P(),
        P(None, "seq"),
        P(None, "seq"),
    )
    out_specs = (
        P("dp", "seq", None),
        P("dp", "seq", None),
        P(),
        P(),
        P(),
        P(),
        P(),
        P(None, "seq"),
        P(None, "seq"),
    )
    return jax.shard_map(shards, mesh=mesh, in_specs=in_specs, out_specs=out_specs, check_vma=False)
```
